256 devices in a mesh: gx: 4 (over z_lo), gy: 16 (over z_hi, x, core), gz: 4 (over y).
Axes of the slice: x: 4, y: 4, z: 8 (z_hi: 2, z_lo: 4; z = z_hi * 4 + z_lo), core: 2. Of those that a mesh axis runs over, the one named last changes fastest.
Arguments:
- elevation: int32 [512, 512], P('gy', ('gx', 'gz')), may hold values from 0 to 499
- layer_base: float32 [64], P('gz'), may hold values from 0.6 to 1.6
- stretch: float32 [64], P('gz'), may hold values from -0.5 to 0.5
- material: int32 [64, 512, 512], P('gz', 'gy', 'gx'), may hold values from 0 to 15
- buoyancy: float32 [16], replicated, may hold values from 0.5 to 2
- lame_lambda: float32 [16], replicated, may hold values from 0.5 to 2
- shear_modulus: float32 [16], replicated, may hold values from 0.3 to 1.5
- relax_time: float32 [16], replicated, may hold values from 0.2 to 30
- anelastic_weight: float32 [16], replicated, may hold values from 0.05 to 0.5
- velocity: float32 [3, 64, 512, 512], P(None, 'gz', 'gy', 'gx'), may hold values from -6 to 6
- stress: float32 [6, 64, 512, 512], P(None, 'gz', 'gy', 'gx'), may hold values from -6 to 6
- memory: float32 [6, 64, 512, 512], P(None, 'gz', 'gy', 'gx'), may hold values from -4 to 4
Outputs:
- velocity_next: float32 [3, 64, 512, 512], P(None, 'gz', 'gy', 'gx')
- stress_next: float32 [6, 64, 512, 512], P(None, 'gz', 'gy', 'gx')
- memory_next: float32 [6, 64, 512, 512], P(None, 'gz', 'gy', 'gx')
The draws below stay inside these ranges and needn't reach their ends.
All inputs are finite; a program needn't handle non-finite values.
Results may differ from the reference program's by a relative error of at most 0.00002.
Values sent between devices are 32-bit elements; how exact they have to be, the bound alone decides.
A program may use at most 64 MiB of HBM per device.

```python
import math
import jax
import jax.numpy as jnp
from jax import lax

NMAT = 16
NX = 512
NY = 512
NZ = 64


def place_ends(array, stream_key, least, high):
    spot = [jax.random.randint(jax.random.fold_in(stream_key, axis), (), 0, length) for axis, length in enumerate(array.shape)]
    main_axis = array.shape.index(max(array.shape))
    neighbour = spot[:main_axis] + [(spot[main_axis] + 1) % array.shape[main_axis]] + spot[main_axis + 1:]
    return array.at[tuple(spot)].set(least).at[tuple(neighbour)].set(high)


def level_of(rng, extent, cuts, low, largest):
    def one(dim, shards_of):
        steps = jax.random.uniform(jax.random.fold_in(jax.random.fold_in(rng, 6), dim), (shards_of,), jnp.float32, low / len(cuts), largest / len(cuts))
        return jnp.repeat(jnp.exp(steps), extent[dim] // shards_of).reshape((-1,) + (1,) * (len(extent) - dim - 1))

    level = one(*cuts[0])
    for cut in cuts[1:]:
        level = level * one(*cut)
    return level


def scatter_about(stream_key, dims, width, most, cuts=(), held_as=jnp.bfloat16):
    array = jax.random.normal(stream_key, dims, jnp.float32) * width
    if len(cuts) > 0:
        array = level_of(stream_key, dims, cuts, -0.22, 0.18) * array
    return jnp.clip(array, min=-most, max=most).astype(held_as)


def setup_inputs(seed: int = 0) -> dict:
    streams_of = jax.random.split(jax.random.key(seed), 13)
    elevation = place_ends(jax.random.randint(streams_of[0], (NY, NX), 0, 500), jax.random.fold_in(streams_of[0], 1), 0, 499).astype(jnp.int32)
    layer_base = jnp.clip(jnp.exp(math.log(1.6) - 0.98082923 * jax.random.uniform(streams_of[1], (NZ,), jnp.float32) ** level_of(streams_of[1], (NZ,), ((0, 4),), -0.2, 0.2)), 0.6, 1.6)
    stretch = jnp.clip(jax.random.uniform(streams_of[2], (NZ,), jnp.float32, -0.5, 0.5) * level_of(streams_of[2], (NZ,), ((0, 4),), -0.4, 0.0), -0.5, 0.5)
    material = place_ends(jax.random.randint(streams_of[3], (NZ, NY, NX), 0, NMAT), jax.random.fold_in(streams_of[3], 1), 0, NMAT - 1).astype(jnp.int32)
    buoyancy = jnp.clip(jnp.exp(jax.random.uniform(streams_of[4], (NMAT,), jnp.float32, math.log(0.5), math.log(2.0))), 0.5, 2.0)
    lame_lambda = jnp.clip(jnp.exp(jax.random.uniform(streams_of[5], (NMAT,), jnp.float32, math.log(0.5), math.log(2.0))), 0.5, 2.0)
    shear_modulus = jnp.clip(jnp.exp(jax.random.uniform(streams_of[6], (NMAT,), jnp.float32, math.log(0.3), math.log(1.5))), 0.3, 1.5)
    relax_time = jnp.clip(jnp.exp(jax.random.uniform(streams_of[7], (NMAT,), jnp.float32, math.log(0.2), math.log(30.0))), 0.2, 30.0)
    anelastic_weight = jnp.clip(jax.random.uniform(streams_of[8], (NMAT,), jnp.float32, 0.05, 0.5), 0.05, 0.5)
    velocity = scatter_about(streams_of[9], (3, NZ, NY, NX), 1.0, 6.0, ((1, 4), (2, 16), (3, 4)), jnp.float32)
    stress = scatter_about(streams_of[10], (6, NZ, NY, NX), 1.0, 6.0, ((1, 4), (2, 16), (3, 4)), jnp.float32)
    memory = scatter_about(streams_of[11], (6, NZ, NY, NX), 0.5, 4.0, ((1, 4), (2, 16), (3, 4)), jnp.float32)
    return dict(elevation=elevation, layer_base=layer_base, stretch=stretch, material=material, buoyancy=buoyancy, lame_lambda=lame_lambda, shear_modulus=shear_modulus, relax_time=relax_time, anelastic_weight=anelastic_weight, velocity=velocity, stress=stress, memory=memory)


step_size = 0.3
binomial = (1.0, 4.0, 6.0, 4.0, 1.0)


def smooth_axis(values_in, dimension):
    length_out = values_in.shape[dimension] - 4
    summed = jnp.zeros_like(lax.slice_in_dim(values_in, 0, length_out, axis=dimension))
    for offset, weight in enumerate(binomial):
        summed = summed + weight * lax.slice_in_dim(values_in, offset, offset + length_out, axis=dimension)
    return summed / 16.0


def centred(values_in, dimension):
    length_out = values_in.shape[dimension] - 4
    closer = lax.slice_in_dim(values_in, 3, 3 + length_out, axis=dimension) - lax.slice_in_dim(values_in, 1, 1 + length_out, axis=dimension)
    farther = lax.slice_in_dim(values_in, 4, 4 + length_out, axis=dimension) - lax.slice_in_dim(values_in, 0, length_out, axis=dimension)
    return (8.0 * closer - farther) / 12.0


def new_velocity(velocity, grad_x, grad_y, grad_k, metric_x, metric_y, metric_z, buoy_cell):
    accel_x = (grad_x[0] - metric_x * grad_k[0]) + (grad_y[0] - metric_y * grad_k[3]) + metric_z * grad_k[4]
    accel_y = (grad_x[1] - metric_x * grad_k[3]) + (grad_y[1] - metric_y * grad_k[1]) + metric_z * grad_k[5]
    accel_z = (grad_x[2] - metric_x * grad_k[4]) + (grad_y[2] - metric_y * grad_k[5]) + metric_z * grad_k[2]
    return velocity + step_size * buoy_cell[None] * jnp.stack([accel_x, accel_y, accel_z])


def new_stress(stress, memory, vel_x, vel_y, vel_k, metric_x, metric_y, metric_z, properties):
    along_x = vel_x - metric_x[None] * vel_k
    along_y = vel_y - metric_y[None] * vel_k
    along_z = metric_z[None] * vel_k
    lame_cell = properties[1]
    shear_cell = properties[2]
    volume_rate = along_x[0] + along_y[1] + along_z[2]
    elastic_rate = jnp.stack([
        lame_cell * volume_rate + 2.0 * shear_cell * along_x[0],
        lame_cell * volume_rate + 2.0 * shear_cell * along_y[1],
        lame_cell * volume_rate + 2.0 * shear_cell * along_z[2],
        shear_cell * (along_y[0] + along_x[1]),
        shear_cell * (along_z[0] + along_x[2]),
        shear_cell * (along_z[1] + along_y[2]),
    ])
    keep_factor = properties[3][None]
    memory_next = keep_factor * memory + (1.0 - keep_factor) * properties[4][None] * elastic_rate
    stress_next = stress + step_size * (elastic_rate - memory_next)
    return stress_next, memory_next


def reference(elevation, layer_base, stretch, material, buoyancy, lame_lambda, shear_modulus, relax_time, anelastic_weight, velocity, stress, memory):
    height = elevation.astype(jnp.float32) / 200.0
    rimmed = jnp.pad(height, 4)
    surface = smooth_axis(smooth_axis(rimmed, 0), 1)
    slope_x = centred(surface[2:-2, :], 1)
    slope_y = centred(surface[:, 2:-2], 0)
    surface_own = surface[2:-2, 2:-2]
    thickness = layer_base[:, None, None] * jnp.exp(stretch[:, None, None] * surface_own[None])
    weighted = stretch[:, None, None] * thickness
    lift = jnp.cumsum(weighted, axis=0) - 0.5 * weighted
    factor = (lift - 1.0) / thickness
    metric_x = slope_x[None] * factor
    metric_y = slope_y[None] * factor
    metric_z = 1.0 / thickness
    tables = jnp.stack([buoyancy, lame_lambda, shear_modulus, jnp.exp(-step_size / relax_time), anelastic_weight])
    properties = tables[:, material]
    padded = jnp.pad(stress, ((0, 0), (2, 2), (2, 2), (2, 2)))
    stress_x = jnp.concatenate([padded[0:1], padded[3:5]])[:, 2:-2, 2:-2, :]
    stress_y = jnp.concatenate([padded[3:4], padded[1:2], padded[5:6]])[:, 2:-2, :, 2:-2]
    stress_z = padded[:, :, 2:-2, 2:-2]
    velocity_next = new_velocity(velocity, centred(stress_x, 3), centred(stress_y, 2), centred(stress_z, 1), metric_x, metric_y, metric_z, properties[0])
    vel_pad = jnp.pad(velocity_next, ((0, 0), (2, 2), (2, 2), (2, 2)))
    vel_x = centred(vel_pad[:, 2:-2, 2:-2, :], 3)
    vel_y = centred(vel_pad[:, 2:-2, :, 2:-2], 2)
    vel_k = centred(vel_pad[:, :, 2:-2, 2:-2], 1)
    stress_next, memory_next = new_stress(stress, memory, vel_x, vel_y, vel_k, metric_x, metric_y, metric_z, properties)
    return velocity_next, stress_next, memory_next
```

```python
import functools

import jax
import jax.numpy as jnp
from jax import lax
from jax.experimental import pallas as pl
from jax.experimental.pallas import tpu as pltpu
from jax.sharding import PartitionSpec as P

MESH = pl.DeviceIdType.MESH
STEP = 0.3
GX, GY, GZ = 4, 16, 4
NZ, NY, NX = 16, 32, 128
X_PARTS = (0, 3, 4)
Y_PARTS = (3, 1, 5)
Y_SENT = (1, 3, 5)
BLOCK = 16


def when(condition, action):
    if condition is None:
        action()
    else:
        pl.when(condition)(lambda: action())


def centred_12(before_2, before_1, after_1, after_2):
    return 8.0 * (after_1 - before_1) - (after_2 - before_2)


def kernel(
    elevation, layer_base, stretch, material, buoyancy, lame, shear, relax, weight, velocity, stress, memory,
    v_out, s_out, m_out,
    sigma, vel, terrain, wide, surf, slopes, layers, mat, tables, metric, packs, halo_s, halo_v,
    small, local_sem, s_send, s_recv, v_send, v_recv, y_send, y_recv, layer_send, layer_recv, t_send, t_recv,
):
    x, y, z = lax.axis_index("gx"), lax.axis_index("gy"), lax.axis_index("gz")
    x_low, x_high = x > 0, x < GX - 1
    y_low, y_high = y > 0, y < GY - 1
    z_low, z_high = z > 0, z < GZ - 1
    lane = lax.broadcasted_iota(jnp.int32, (8, NX), 1)

    own_slot = 1 + z
    tables_in = (buoyancy, lame, shear, relax, weight, layer_base, stretch)
    scalars = [pltpu.make_async_copy(ref, small.at[i], local_sem.at[i]) for i, ref in enumerate(tables_in)]
    for copy in scalars:
        copy.start()
    stress_in = {
        c: pltpu.make_async_copy(stress.at[c], sigma.at[c, 2:18, 8:40, :], local_sem.at[7 + c])
        for c in (0, 3, 4, 1, 2, 5)
    }
    for c in (0, 3, 4, 1, 2, 5):
        stress_in[c].start()
    elevation_in = pltpu.make_async_copy(elevation, terrain.at[own_slot, 8:40, :], local_sem.at[13])
    velocity_in = pltpu.make_async_copy(velocity, v_out, local_sem.at[14])
    material_in = pltpu.make_async_copy(material, mat, local_sem.at[15])
    memory_in = pltpu.make_async_copy(memory, m_out, local_sem.at[16])
    for copy in (elevation_in, material_in, velocity_in, memory_in):
        copy.start()

    barrier = pltpu.get_barrier_semaphore()
    partners = [(None, {"gz": (z + d) % GZ}) for d in range(1, GZ)]
    partners += [(y_low, {"gy": y - 1}), (y_high, {"gy": y + 1})]
    for g in range(GZ):
        partners.append((x_high & ((z == g) | (z == GZ - 1) | (g == 0)), {"gx": x + 1, "gz": g}))
        partners.append((x_low & ((z == g) | (z == 0) | (g == GZ - 1)), {"gx": x - 1, "gz": g}))
    for condition, target in partners:
        when(condition, lambda target=target: pl.semaphore_signal(barrier, inc=1, device_id=target, device_id_type=MESH))

    for copy in scalars:
        copy.wait()
    for k in range(NZ):
        for row in range(2):
            layers[row, pl.ds(NZ * z + k, 1), :] = jnp.full((1, NX), small[5 + row, k], jnp.float32)
    columns = []
    for i in range(5):
        column = jnp.zeros((8, NX), jnp.float32)
        for block_id in range(16):
            column = jnp.where(lane == block_id, small[i, block_id], column)
        columns.append(column)
    keep = jnp.exp(-STEP / jnp.where(lane < 16, columns[3], 1.0))
    tables[0] = columns[0] * (STEP / 12.0)
    tables[1] = columns[1] * (1.0 / 12.0)
    tables[2] = columns[2] * (1.0 / 12.0)
    tables[3] = keep
    tables[4] = (1.0 - keep) * columns[4]

    def zero_stress_z(first):
        sigma[:, pl.ds(first, 2), 8:40, :] = jnp.zeros((6, 2, NY, NX), jnp.float32)
        vel[:, pl.ds(first, 2), 8:40, :] = jnp.zeros((3, 2, NY, NX), jnp.float32)

    def zero_y(first):
        def layer(k, carry):
            for c in Y_SENT:
                sigma[c, 2 + k, first : first + 8, :] = jnp.zeros((8, NX), jnp.float32)
            for c in range(3):
                vel[c, 2 + k, first : first + 8, :] = jnp.zeros((8, NX), jnp.float32)
            return carry

        lax.fori_loop(0, NZ, layer, 0)
        for m in range(6):
            terrain[m, first : first + 8, :] = jnp.zeros((8, 32), jnp.int32)

    def zero_x(side, slot):
        halo_s[side] = jnp.zeros((2, NY, NX), jnp.float32)
        halo_v[side] = jnp.zeros((2, NY, NX), jnp.float32)
        terrain[slot] = jnp.zeros((48, 32), jnp.int32)

    when(z == 0, lambda: zero_stress_z(0))
    when(z == GZ - 1, lambda: zero_stress_z(18))
    when(y == 0, lambda: zero_y(0))
    when(y == GY - 1, lambda: zero_y(40))
    when(x == 0, lambda: zero_x(0, 0))
    when(x == GX - 1, lambda: zero_x(1, 5))

    def pack(parts, field, phase):
        def layer(k, held):
            held = list(held)
            for i, c in enumerate(parts):
                at = 4 * (k + (NZ if i == 1 else 0))
                spot = (lane >= at) & (lane < at + 4)
                for r in range(4):
                    rolled = pltpu.roll(field[c, 2 + k, 8 + 8 * r : 16 + 8 * r, :], at + 2, 1)
                    j = 4 * (i // 2) + r
                    held[j] = jnp.where(spot, rolled, held[j])
            return tuple(held)

        held = lax.fori_loop(0, NZ, layer, tuple(jnp.zeros((8, NX), jnp.float32) for _ in range(8)))
        for j in range(8):
            packs[phase, j // 4, 8 * (j % 4) : 8 * (j % 4) + 8, :] = held[j]

    for c in X_PARTS:
        stress_in[c].wait()
    pack(X_PARTS, sigma, 0)

    pl.semaphore_wait(barrier, sum(1 if c is None else c.astype(jnp.int32) for c, _ in partners))

    def remote(source, to, send, recv, target):
        return pltpu.make_async_remote_copy(
            src_ref=source, dst_ref=to, send_sem=send, recv_sem=recv, device_id=target, device_id_type=MESH
        )

    sends = []

    def send(condition, copy):
        sends.append((condition, copy))
        when(condition, copy.start)

    up_y, down_y = {"gy": y + 1}, {"gy": y - 1}
    low_rows, high_rows = terrain.at[own_slot, 0:8, :], terrain.at[own_slot, 40:48, :]
    send(y_high, remote(elevation.at[24:32, :], low_rows, t_send.at[1, 7], t_recv.at[own_slot, 1], up_y))
    send(y_low, remote(elevation.at[0:8, :], high_rows, t_send.at[2, 7], t_recv.at[own_slot, 2], down_y))
    for i, c in enumerate(Y_SENT):
        send(y_high, remote(stress.at[c, :, 30:32, :], sigma.at[c, 2:18, 6:8, :], y_send.at[0, i], y_recv.at[0, i], up_y))
        send(y_low, remote(stress.at[c, :, 0:2, :], sigma.at[c, 2:18, 40:42, :], y_send.at[1, i], y_recv.at[1, i], down_y))

    def spread(part, source, rows, condition):
        def both(other):
            return other if condition is None else (condition if other is None else condition & other)

        for d in range(1, GZ):
            g = (z + d) % GZ
            send(both(None), remote(source, terrain.at[own_slot, rows, :], t_send.at[part, d - 1], t_recv.at[own_slot, part], {"gz": g}))
        for g in range(GZ):
            send(both(x_high & (z == GZ - 1)), remote(source, terrain.at[0, rows, :], t_send.at[part, 3 + g], t_recv.at[0, part], {"gx": x + 1, "gz": g}))
            send(both(x_low & (z == 0)), remote(source, terrain.at[5, rows, :], t_send.at[part, 3 + g], t_recv.at[5, part], {"gx": x - 1, "gz": g}))

    spread(0, elevation, slice(8, 40), None)
    mine = pl.ds(NZ * z, NZ)
    for d in range(1, GZ):
        send(None, remote(layers.at[:, mine, :], layers.at[:, mine, :], layer_send.at[d - 1], layer_recv.at[z], {"gz": (z + d) % GZ}))
    send(x_high, remote(packs.at[0], halo_s.at[0], s_send.at[0], s_recv.at[0], {"gx": x + 1}))
    send(x_low, remote(packs.at[0], halo_s.at[1], s_send.at[1], s_recv.at[1], {"gx": x - 1}))
    send(z_high, remote(stress.at[:, 14:16], sigma.at[:, 0:2, 8:40, :], s_send.at[2], s_recv.at[2], {"gz": z + 1}))
    send(z_low, remote(stress.at[:, 0:2], sigma.at[:, 18:20, 8:40, :], s_send.at[3], s_recv.at[3], {"gz": z - 1}))

    def arrived(ref, recv):
        remote(ref, ref, s_send.at[0], recv, {"gz": z}).wait_recv()

    when(y_low, lambda: arrived(low_rows, t_recv.at[own_slot, 1]))
    when(y_high, lambda: arrived(high_rows, t_recv.at[own_slot, 2]))
    spread(1, low_rows, slice(0, 8), y_low)
    spread(2, high_rows, slice(40, 48), y_high)

    elevation_in.wait()

    def slot_arrived(slot, condition):
        def both(other):
            return other if condition is None else (condition if other is None else condition & other)

        when(both(None), lambda: arrived(terrain.at[slot, 8:40, :], t_recv.at[slot, 0]))
        when(both(y_low), lambda: arrived(terrain.at[slot, 0:8, :], t_recv.at[slot, 1]))
        when(both(y_high), lambda: arrived(terrain.at[slot, 40:48, :], t_recv.at[slot, 2]))

    for d in range(1, GZ):
        g = (z + d) % GZ
        slot_arrived(1 + g, None)
        arrived(layers.at[:, pl.ds(NZ * g, NZ), :], layer_recv.at[g])
    slot_arrived(0, x_low)
    slot_arrived(5, x_high)

    for r in range(6):
        rows = slice(8 * r, 8 * r + 8)
        held = [terrain[m, rows, :].astype(jnp.float32) / 200.0 for m in range(6)]
        blank = jnp.zeros((8, 96), jnp.float32)
        wide[0, rows, :] = jnp.concatenate([blank, held[0]], axis=1)
        wide[1, rows, :] = jnp.concatenate(held[1:5], axis=1)
        wide[2, rows, :] = jnp.concatenate([held[5], blank], axis=1)
    binomial = (1.0, 4.0, 6.0, 4.0, 1.0)
    along_y = []
    for part in range(3):
        total = jnp.zeros((40, NX), jnp.float32)
        for d, factor in enumerate(binomial):
            total = total + factor * wide[part, 2 + d : 42 + d, :]
        along_y.append(total / 16.0)
    row = jnp.concatenate(along_y, axis=1)
    total = jnp.zeros_like(row)
    for d, factor in enumerate(binomial):
        total = total + factor * (row if d == 2 else pltpu.roll(row, (2 - d) % 384, 1))
    total = total / 16.0
    for part in range(3):
        surf[part] = total[:, 128 * part : 128 * part + 128]
    own = jnp.concatenate([surf[part, 4:36, :] for part in range(3)], axis=1)
    shifted = [pltpu.roll(own, d % 384, 1)[:, 128:256] for d in (2, 1, -1, -2)]
    slopes[0] = centred_12(*shifted) / 12.0
    slopes[1] = centred_12(*[surf[1, 4 + d : 36 + d, :] for d in (-2, -1, 1, 2)]) / 12.0

    def metrics(first, rows):
        at = slice(first, first + rows)
        height = surf[1, 4 + first : 4 + first + rows, :]
        slope_x, slope_y = slopes[0, at, :], slopes[1, at, :]

        def above(layer, total):
            base, follow = layers[0, pl.ds(layer, 1), :], layers[1, pl.ds(layer, 1), :]
            return total + follow * (base * jnp.exp(follow * height))

        upper = lax.fori_loop(0, NZ * z, above, jnp.zeros((rows, NX), jnp.float32))

        def layer(k, total):
            base, follow = layers[0, pl.ds(NZ * z + k, 1), :], layers[1, pl.ds(NZ * z + k, 1), :]
            thickness = base * jnp.exp(follow * height)
            weighted = follow * thickness
            inverse = 1.0 / thickness
            factor = (total + 0.5 * weighted - 1.0) * inverse
            metric[0, k, at, :] = slope_x * factor
            metric[1, k, at, :] = slope_y * factor
            metric[2, k, at, :] = inverse
            return total + weighted

        lax.fori_loop(0, NZ, layer, upper)

    for first in range(0, NY, BLOCK):
        metrics(first, BLOCK)

    side = lax.broadcasted_iota(jnp.int32, (BLOCK, NX), 1)

    def d_k(field, c, k, first):
        at = slice(8 + first, 8 + first + BLOCK)
        return centred_12(*[field[c, k + 2 + d, at, :] for d in (-2, -1, 1, 2)])

    def d_y(field, c, k, first):
        return centred_12(*[field[c, k + 2, 8 + first + d : 8 + first + d + BLOCK, :] for d in (-2, -1, 1, 2)])

    def d_x(field, c, k, first, halo, i):
        here = field[c, k + 2, 8 + first : 8 + first + BLOCK, :]
        at = 4 * (k + (NZ if i == 1 else 0))
        beside = pltpu.roll(halo[0, i // 2, first : first + BLOCK, :], 126 - at, 1)
        return centred_12(
            pltpu.roll(jnp.where(side >= 126, beside, here), 2, 1), pltpu.roll(jnp.where(side >= 127, beside, here), 1, 1),
            pltpu.roll(jnp.where(side < 1, beside, here), 127, 1), pltpu.roll(jnp.where(side < 2, beside, here), 126, 1),
        )

    def join(halo):
        for i in range(2):
            for r in range(4):
                rows = slice(8 * r, 8 * r + 8)
                halo[0, i, rows, :] = jnp.where(lane % 4 < 2, halo[0, i, rows, :], halo[1, i, rows, :])

    def look_up(i, block_id):
        table = jnp.concatenate([tables[i]] * (BLOCK // 8), axis=0)
        return jnp.take_along_axis(table, block_id, axis=1)

    for copy in (stress_in[1], stress_in[2], stress_in[5], velocity_in, material_in):
        copy.wait()
    when(x_low, lambda: arrived(halo_s.at[0], s_recv.at[0]))
    when(x_high, lambda: arrived(halo_s.at[1], s_recv.at[1]))
    join(halo_s)
    when(z_low, lambda: arrived(sigma.at[:, 0:2, 8:40, :], s_recv.at[2]))
    when(z_high, lambda: arrived(sigma.at[:, 18:20, 8:40, :], s_recv.at[3]))
    for i, c in enumerate(Y_SENT):
        when(y_low, lambda: arrived(sigma.at[c, 2:18, 6:8, :], y_recv.at[0, i]))
        when(y_high, lambda: arrived(sigma.at[c, 2:18, 40:42, :], y_recv.at[1, i]))

    def velocity_layer(k, carry):
        for first in range(0, NY, BLOCK):
            at = slice(first, first + BLOCK)
            m_x, m_y, m_z = (metric[i, k, at, :] for i in range(3))
            grad_k = [d_k(sigma, c, k, first) for c in range(6)]
            grad_x = [d_x(sigma, c, k, first, halo_s, i) for i, c in enumerate(X_PARTS)]
            grad_y = [d_y(sigma, c, k, first) for c in Y_PARTS]
            scale = look_up(0, mat[k, at, :])
            for c, (a, b, d) in enumerate(((0, 3, 4), (3, 1, 5), (4, 5, 2))):
                accel = (grad_x[c] - m_x * grad_k[a]) + (grad_y[c] - m_y * grad_k[b]) + m_z * grad_k[d]
                new = v_out[c, k, at, :] + scale * accel
                v_out[c, k, at, :] = new
                vel[c, 2 + k, 8 + first : 8 + first + BLOCK, :] = new
        return carry

    lax.fori_loop(0, NZ, velocity_layer, 0)
    send(y_high, remote(vel.at[:, 2:18, 38:40, :], vel.at[:, 2:18, 6:8, :], v_send.at[4], v_recv.at[4], up_y))
    send(y_low, remote(vel.at[:, 2:18, 8:10, :], vel.at[:, 2:18, 40:42, :], v_send.at[5], v_recv.at[5], down_y))
    send(z_high, remote(vel.at[:, 16:18, 8:40, :], vel.at[:, 0:2, 8:40, :], v_send.at[2], v_recv.at[2], {"gz": z + 1}))
    send(z_low, remote(vel.at[:, 2:4, 8:40, :], vel.at[:, 18:20, 8:40, :], v_send.at[3], v_recv.at[3], {"gz": z - 1}))
    pack((0, 1, 2), vel, 1)
    send(x_high, remote(packs.at[1], halo_v.at[0], v_send.at[0], v_recv.at[0], {"gx": x + 1}))
    send(x_low, remote(packs.at[1], halo_v.at[1], v_send.at[1], v_recv.at[1], {"gx": x - 1}))

    memory_in.wait()
    when(x_low, lambda: arrived(halo_v.at[0], v_recv.at[0]))
    when(x_high, lambda: arrived(halo_v.at[1], v_recv.at[1]))
    join(halo_v)
    when(z_low, lambda: arrived(vel.at[:, 0:2, 8:40, :], v_recv.at[2]))
    when(z_high, lambda: arrived(vel.at[:, 18:20, 8:40, :], v_recv.at[3]))
    when(y_low, lambda: arrived(vel.at[:, 2:18, 6:8, :], v_recv.at[4]))
    when(y_high, lambda: arrived(vel.at[:, 2:18, 40:42, :], v_recv.at[5]))

    def stress_layer(k, carry):
        for first in range(0, NY, BLOCK):
            at = slice(first, first + BLOCK)
            m_x, m_y, m_z = (metric[i, k, at, :] for i in range(3))
            along_k = [d_k(vel, c, k, first) for c in range(3)]
            along_x = [d_x(vel, c, k, first, halo_v, c) - m_x * along_k[c] for c in range(3)]
            along_y = [d_y(vel, c, k, first) - m_y * along_k[c] for c in range(3)]
            along_z = [m_z * along_k[c] for c in range(3)]
            block_id = mat[k, at, :]
            lam, mu, kept, gain = (look_up(i, block_id) for i in range(1, 5))
            volume = lam * (along_x[0] + along_y[1] + along_z[2])
            twice = mu + mu
            rates = (
                volume + twice * along_x[0],
                volume + twice * along_y[1],
                volume + twice * along_z[2],
                mu * (along_y[0] + along_x[1]),
                mu * (along_z[0] + along_x[2]),
                mu * (along_z[1] + along_y[2]),
            )
            for c, rate in enumerate(rates):
                new = kept * m_out[c, k, at, :] + gain * rate
                m_out[c, k, at, :] = new
                s_out[c, k, at, :] = sigma[c, 2 + k, 8 + first : 8 + first + BLOCK, :] + STEP * (rate - new)
        return carry

    lax.fori_loop(0, NZ, stress_layer, 0)
    for condition, copy in sends:
        when(condition, copy.wait_send)


def local(*arrays):
    held = [pltpu.with_memory_space_constraint(array, pltpu.HBM) for array in arrays]
    f32, vmem, dma = jnp.float32, pltpu.VMEM, pltpu.SemaphoreType.DMA
    outputs = [(n, NZ, NY, NX) for n in (3, 6, 6)]
    return pl.pallas_call(
        kernel,
        out_shape=tuple(vmem(shape, f32) for shape in outputs),
        in_specs=[pl.BlockSpec(memory_space=pltpu.HBM)] * len(held),
        out_specs=tuple(pl.BlockSpec(memory_space=vmem) for _ in outputs),
        scratch_shapes=[
            vmem((6, 20, 48, NX), f32),
            vmem((3, 20, 48, NX), f32),
            vmem((6, 48, 32), jnp.int32),
            vmem((3, 48, NX), f32),
            vmem((3, 40, NX), f32),
            vmem((2, NY, NX), f32),
            vmem((2, GZ * NZ, NX), f32),
            vmem((NZ, NY, NX), jnp.int32),
            vmem((5, 8, NX), f32),
            vmem((3, NZ, NY, NX), f32),
            vmem((2, 2, NY, NX), f32),
            vmem((2, 2, NY, NX), f32),
            vmem((2, 2, NY, NX), f32),
            pltpu.SMEM((7, 16), f32),
            dma((17,)), dma((4,)), dma((4,)), dma((6,)), dma((6,)), dma((2, 3)), dma((2, 3)),
            dma((3,)), dma((4,)), dma((3, 8)), dma((6, 3)),
        ],
        compiler_params=pltpu.CompilerParams(
            collective_id=0, has_side_effects=True, vmem_limit_bytes=24 << 20
        ),
    )(*held)


def solution(mesh):
    field = P(None, "gz", "gy", "gx")
    return jax.shard_map(
        local,
        mesh=mesh,
        in_specs=(
            P("gy", ("gx", "gz")), P("gz"), P("gz"), P("gz", "gy", "gx"),
            P(), P(), P(), P(), P(), field, field, field,
        ),
        out_specs=(field, field, field),
        check_vma=False,
    )
```

```python
import functools

import jax
import jax.numpy as jnp
from jax import lax
from jax.experimental import pallas as pl
from jax.experimental.pallas import tpu as pltpu
from jax.sharding import PartitionSpec as P

MESH = pl.DeviceIdType.MESH
STEP = 0.3
GX, GY, GZ = 4, 16, 4
NZ, NY, NX = 16, 32, 128
X_PARTS = (0, 3, 4)
Y_PARTS = (3, 1, 5)
Y_SENT = (1, 3, 5)


def when(condition, action):
    if condition is None:
        action()
    else:
        pl.when(condition)(lambda: action())


def centred_12(before_2, before_1, after_1, after_2):
    return 8.0 * (after_1 - before_1) - (after_2 - before_2)


def kernel(
    elevation, layer_base, stretch, material, buoyancy, lame, shear, relax, weight, velocity, stress, memory,
    v_out, s_out, m_out,
    sigma, vel, terrain, wide, surf, layers, mat, tables, metric, packs, halo_s, halo_v,
    small, local_sem, s_send, s_recv, y_send, y_recv, layer_send, layer_recv, t_send, t_recv, edge_send, edge_recv,
    z_send, z_recv, x_send, x_recv, vy_send, vy_recv, far_sem,
):
    x, y, z = lax.axis_index("gx"), lax.axis_index("gy"), lax.axis_index("gz")
    x_low, x_high = x > 0, x < GX - 1
    y_low, y_high = y > 0, y < GY - 1
    z_low, z_high = z > 0, z < GZ - 1
    before_gap, after_gap = y == GY // 2 - 1, y == GY // 2
    lane = lax.broadcasted_iota(jnp.int32, (8, NX), 1)

    own_slot = 1 + z
    tables_in = (buoyancy, lame, shear, relax, weight, layer_base, stretch)
    scalars = [pltpu.make_async_copy(ref, small.at[i], local_sem.at[i]) for i, ref in enumerate(tables_in)]
    for copy in scalars:
        copy.start()
    stress_in = {
        c: pltpu.make_async_copy(stress.at[c], sigma.at[c, 2:18, 8:40, :], local_sem.at[7 + c])
        for c in (0, 3, 4, 1, 2, 5)
    }
    for c in (0, 3, 4, 1, 2, 5):
        stress_in[c].start()
    elevation_in = pltpu.make_async_copy(elevation, terrain.at[own_slot, 8:40, :], local_sem.at[13])
    velocity_in = pltpu.make_async_copy(velocity, v_out, local_sem.at[14])
    material_in = pltpu.make_async_copy(material, mat, local_sem.at[15])
    memory_in = pltpu.make_async_copy(memory, m_out, local_sem.at[16])
    for copy in (elevation_in, material_in, velocity_in, memory_in):
        copy.start()

    barrier = pltpu.get_barrier_semaphore()
    beside = [(None, {"gz": (z + d) % GZ}) for d in range(1, GZ)]
    for g in range(GZ):
        beside.append((x_high & ((z == g) | (z == GZ - 1) | (g == 0)), {"gx": x + 1, "gz": g}))
        beside.append((x_low & ((z == g) | (z == 0) | (g == GZ - 1)), {"gx": x - 1, "gz": g}))
    up_y, down_y = {"gy": y + 1}, {"gy": y - 1}
    for condition, target in [(y_high, up_y), (y_low & ~after_gap, down_y)] + beside:
        when(condition, lambda target=target: pl.semaphore_signal(barrier, inc=1, device_id=target, device_id_type=MESH))
    expected = [y_low, y_high & ~before_gap] + [condition for condition, _ in beside]

    for copy in scalars:
        copy.wait()
    for k in range(NZ):
        for row in range(2):
            layers[row, pl.ds(NZ * z + k, 1), :] = jnp.full((1, NX), small[5 + row, k], jnp.float32)

    def pack_spot(k, i):
        at = 4 * (k + (NZ if i == 1 else 0))
        return at, (lane >= at) & (lane < at + 4)

    def pack_layer(held, blocks, i, k, at, spot):
        for r, block in enumerate(blocks):
            j = len(blocks) * (i // 2) + r
            held[j] = jnp.where(spot, pltpu.roll(block, at + 2, 1), held[j])

    def pack_stress(step, held):
        held = list(held)
        for k in (2 * step, 2 * step + 1):
            for i, c in enumerate(X_PARTS):
                at, spot = pack_spot(k, i)
                pack_layer(held, [sigma[c, 2 + k, 8 + 8 * r : 16 + 8 * r, :] for r in range(4)], i, k, at, spot)
        return tuple(held)

    for c in X_PARTS:
        stress_in[c].wait()
    zero = jnp.zeros((8, NX), jnp.float32)
    held = lax.fori_loop(0, NZ // 2, pack_stress, (zero,) * 8)
    for j in range(8):
        packs[0, j // 4, 8 * (j % 4) : 8 * (j % 4) + 8, :] = held[j]

    pl.semaphore_wait(barrier, sum(1 if c is None else c.astype(jnp.int32) for c in expected))
    when(after_gap, lambda: pl.semaphore_signal(far_sem, inc=1, device_id=down_y, device_id_type=MESH))

    def remote(source, to, send, recv, target):
        return pltpu.make_async_remote_copy(
            src_ref=source, dst_ref=to, send_sem=send, recv_sem=recv, device_id=target, device_id_type=MESH
        )

    sends = []

    def send(condition, copy, now=True):
        sends.append((condition, copy))
        if now:
            when(condition, copy.start)
        return copy

    up_copies = [
        send(y_high, remote(stress.at[c, :, 30:32, :], sigma.at[c, 2:18, 6:8, :], y_send.at[0, i], y_recv.at[0, i], up_y), now=False)
        for i, c in enumerate(Y_SENT)
    ]

    def start_up():
        for copy in up_copies:
            copy.start()

    when(y_high & ~before_gap, start_up)
    for d in range(1, GZ):
        send(None, remote(elevation, terrain.at[own_slot, 8:40, :], t_send.at[d - 1], t_recv.at[own_slot], {"gz": (z + d) % GZ}))
    for g in range(GZ):
        send(x_high & (z == GZ - 1), remote(elevation, terrain.at[0, 8:40, :], t_send.at[3 + g], t_recv.at[0], {"gx": x + 1, "gz": g}))
        send(x_low & (z == 0), remote(elevation, terrain.at[5, 8:40, :], t_send.at[3 + g], t_recv.at[5], {"gx": x - 1, "gz": g}))
    mine = pl.ds(NZ * z, NZ)
    for d in range(1, GZ):
        send(None, remote(layers.at[:, mine, :], layers.at[:, mine, :], layer_send.at[d - 1], layer_recv.at[z], {"gz": (z + d) % GZ}))
    for i, c in enumerate(Y_SENT):
        send(y_low, remote(stress.at[c, :, 0:2, :], sigma.at[c, 2:18, 40:42, :], y_send.at[1, i], y_recv.at[1, i], down_y))
    send(x_high, remote(packs.at[0], halo_s.at[0], s_send.at[0], s_recv.at[0], {"gx": x + 1}))
    send(x_low, remote(packs.at[0], halo_s.at[1], s_send.at[1], s_recv.at[1], {"gx": x - 1}))
    send(z_high, remote(stress.at[:, 14:16], sigma.at[:, 0:2, 8:40, :], s_send.at[2], s_recv.at[2], {"gz": z + 1}))
    send(z_low, remote(stress.at[:, 0:2], sigma.at[:, 18:20, 8:40, :], s_send.at[3], s_recv.at[3], {"gz": z - 1}))

    def arrived(ref, recv):
        remote(ref, ref, s_send.at[0], recv, {"gz": z}).wait_recv()

    columns = []
    for i in range(5):
        column = zero
        for block_id in range(16):
            column = jnp.where(lane == block_id, small[i, block_id], column)
        columns.append(column)
    keep = jnp.exp(-STEP / jnp.where(lane < 16, columns[3], 1.0))
    tables[0] = columns[0] * (STEP / 12.0)
    tables[1] = columns[1] * (1.0 / 12.0)
    tables[2] = columns[2] * (1.0 / 12.0)
    tables[3] = keep
    tables[4] = (1.0 - keep) * columns[4]

    def zero_z(first):
        sigma[:, pl.ds(first, 2), 8:40, :] = jnp.zeros((6, 2, NY, NX), jnp.float32)
        vel[:, pl.ds(first, 2), 8:40, :] = jnp.zeros((3, 2, NY, NX), jnp.float32)

    def zero_y(first):
        def layer(k, carry):
            for c in Y_SENT:
                sigma[c, 2 + k, first : first + 8, :] = zero
            for c in range(3):
                vel[c, 2 + k, first : first + 8, :] = zero
            return carry

        lax.fori_loop(0, NZ, layer, 0)
        for m in range(6):
            terrain[m, first : first + 8, :] = jnp.zeros((8, 32), jnp.int32)

    def zero_x(side, slot):
        halo_s[side] = jnp.zeros((2, NY, NX), jnp.float32)
        halo_v[side] = jnp.zeros((2, NY, NX), jnp.float32)
        terrain[slot, 8:40, :] = jnp.zeros((32, 32), jnp.int32)

    when(z == 0, lambda: zero_z(0))
    when(z == GZ - 1, lambda: zero_z(18))
    when(y == 0, lambda: zero_y(0))
    when(y == GY - 1, lambda: zero_y(40))
    when(x == 0, lambda: zero_x(0, 0))
    when(x == GX - 1, lambda: zero_x(1, 5))

    elevation_in.wait()
    for d in range(1, GZ):
        g = (z + d) % GZ
        arrived(terrain.at[1 + g, 8:40, :], t_recv.at[1 + g])
    when(x_low, lambda: arrived(terrain.at[0, 8:40, :], t_recv.at[0]))
    when(x_high, lambda: arrived(terrain.at[5, 8:40, :], t_recv.at[5]))
    edge_up = send(y_high, remote(terrain.at[:, 32:40, :], terrain.at[:, 0:8, :], edge_send.at[0], edge_recv.at[0], up_y), now=False)
    when(y_high & ~before_gap, edge_up.start)
    send(y_low, remote(terrain.at[:, 8:16, :], terrain.at[:, 40:48, :], edge_send.at[1], edge_recv.at[1], down_y))

    def heights(row):
        rows = pl.ds(row, 8)
        held = [terrain[m, rows, :].astype(jnp.float32) / 200.0 for m in range(6)]
        blank = jnp.zeros((8, 96), jnp.float32)
        wide[0, rows, :] = jnp.concatenate([blank, held[0]], axis=1)
        wide[1, rows, :] = jnp.concatenate(held[1:5], axis=1)
        wide[2, rows, :] = jnp.concatenate([held[5], blank], axis=1)

    binomial = (1.0, 4.0, 6.0, 4.0, 1.0)

    def metrics(first, rows):
        along_y = []
        for part in range(3):
            total = jnp.zeros((rows + 8, NX), jnp.float32)
            for d, factor in enumerate(binomial):
                total = total + factor * wide[part, pl.ds(first + 2 + d, rows + 8), :]
            along_y.append(total / 16.0)
        row = jnp.concatenate(along_y, axis=1)
        total = jnp.zeros_like(row)
        for d, factor in enumerate(binomial):
            total = total + factor * (row if d == 2 else pltpu.roll(row, (2 - d) % 384, 1))
        total = total / 16.0
        for part in range(3):
            surf[part, 0 : rows + 8, :] = total[:, 128 * part : 128 * part + 128]
        own = jnp.concatenate([surf[part, 4 : 4 + rows, :] for part in range(3)], axis=1)
        height = own[:, 128:256]
        shifted = [pltpu.roll(own, d % 384, 1)[:, 128:256] for d in (2, 1, -1, -2)]
        slope_x = centred_12(*shifted) / 12.0
        slope_y = centred_12(*[surf[1, 4 + d : 4 + d + rows, :] for d in (-2, -1, 1, 2)]) / 12.0

        def above(step, total):
            for layer in [4 * step + i for i in range(4)]:
                base, follow = layers[0, pl.ds(layer, 1), :], layers[1, pl.ds(layer, 1), :]
                total = total + follow * (base * jnp.exp(follow * height))
            return total

        upper = lax.fori_loop(0, (NZ // 4) * z, above, jnp.zeros((rows, NX), jnp.float32))

        def layer(step, total):
            for k in [4 * step + i for i in range(4)]:
                base, follow = layers[0, pl.ds(NZ * z + k, 1), :], layers[1, pl.ds(NZ * z + k, 1), :]
                thickness = base * jnp.exp(follow * height)
                weighted = follow * thickness
                inverse = 1.0 / thickness
                factor = (total + 0.5 * weighted - 1.0) * inverse
                at = pl.ds(first, rows)
                metric[0, k, at, :] = slope_x * factor
                metric[1, k, at, :] = slope_y * factor
                metric[2, k, at, :] = inverse
                total = total + weighted
            return total

        lax.fori_loop(0, NZ // 4, layer, upper)

    def d_k(field, c, k, first, rows):
        return centred_12(*[field[c, k + 2 + d, pl.ds(8 + first, rows), :] for d in (-2, -1, 1, 2)])

    def d_y(field, c, k, first, rows):
        return centred_12(*[field[c, k + 2, pl.ds(8 + first + d, rows), :] for d in (-2, -1, 1, 2)])

    def d_x(field, c, k, first, rows, halo, i):
        side = lax.broadcasted_iota(jnp.int32, (rows, NX), 1)
        here = field[c, k + 2, pl.ds(8 + first, rows), :]
        at = 4 * (k + (NZ if i == 1 else 0))
        beyond = pltpu.roll(halo[0, i // 2, pl.ds(first, rows), :], 126 - at, 1)
        return centred_12(
            pltpu.roll(jnp.where(side >= 126, beyond, here), 2, 1), pltpu.roll(jnp.where(side >= 127, beyond, here), 1, 1),
            pltpu.roll(jnp.where(side < 1, beyond, here), 127, 1), pltpu.roll(jnp.where(side < 2, beyond, here), 126, 1),
        )

    def join(halo, first, rows):
        side = lax.broadcasted_iota(jnp.int32, (rows, NX), 1)
        for i in range(2):
            at = pl.ds(first, rows)
            halo[0, i, at, :] = jnp.where(side % 4 < 2, halo[0, i, at, :], halo[1, i, at, :])

    def look_up(i, block_id):
        table = jnp.concatenate([tables[i]] * (block_id.shape[0] // 8), axis=0)
        return jnp.take_along_axis(table, block_id, axis=1)

    def velocity_rows(first, rows, unroll):
        blocks = rows // 8

        def velocity_layer(step, held):
            held = list(held)
            at = pl.ds(first, rows)
            for k in [unroll * step + i for i in range(unroll)]:
                m_x, m_y, m_z = (metric[i, k, at, :] for i in range(3))
                grad_k = [d_k(sigma, c, k, first, rows) for c in range(6)]
                grad_x = [d_x(sigma, c, k, first, rows, halo_s, i) for i, c in enumerate(X_PARTS)]
                grad_y = [d_y(sigma, c, k, first, rows) for c in Y_PARTS]
                scale = look_up(0, mat[k, at, :])
                for c, (a, b, d) in enumerate(((0, 3, 4), (3, 1, 5), (4, 5, 2))):
                    accel = (grad_x[c] - m_x * grad_k[a]) + (grad_y[c] - m_y * grad_k[b]) + m_z * grad_k[d]
                    new = v_out[c, k, at, :] + scale * accel
                    v_out[c, k, at, :] = new
                    vel[c, 2 + k, pl.ds(8 + first, rows), :] = new
                    spot_at, spot = pack_spot(k, c)
                    pack_layer(held, [new[8 * r : 8 * r + 8] for r in range(blocks)], c, k, spot_at, spot)
            return tuple(held)

        held = lax.fori_loop(0, NZ // unroll, velocity_layer, (zero,) * (2 * blocks))
        for j in range(2 * blocks):
            packs[1, j // blocks, pl.ds(first + 8 * (j % blocks), 8), :] = held[j]

    def send_rows(part, first, rows):
        at = pl.ds(first, rows)
        send(x_high, remote(packs.at[1, :, at, :], halo_v.at[0, :, at, :], x_send.at[0, part], x_recv.at[0, part], {"gx": x + 1}))
        send(x_low, remote(packs.at[1, :, at, :], halo_v.at[1, :, at, :], x_send.at[1, part], x_recv.at[1, part], {"gx": x - 1}))
        at = pl.ds(8 + first, rows)
        send(z_high, remote(vel.at[:, 16:18, at, :], vel.at[:, 0:2, at, :], z_send.at[0, part], z_recv.at[0, part], {"gz": z + 1}))
        send(z_low, remote(vel.at[:, 2:4, at, :], vel.at[:, 18:20, at, :], z_send.at[1, part], z_recv.at[1, part], {"gz": z - 1}))

    def wait_x(part, first, rows):
        at = pl.ds(first, rows)
        when(x_low, lambda: arrived(halo_v.at[0, :, at, :], x_recv.at[0, part]))
        when(x_high, lambda: arrived(halo_v.at[1, :, at, :], x_recv.at[1, part]))
        join(halo_v, first, rows)

    def wait_z(part, first, rows):
        at = pl.ds(8 + first, rows)
        when(z_low, lambda: arrived(vel.at[:, 0:2, at, :], z_recv.at[0, part]))
        when(z_high, lambda: arrived(vel.at[:, 18:20, at, :], z_recv.at[1, part]))

    for row in range(8, 40, 8):
        heights(row)
    for d in range(1, GZ):
        g = (z + d) % GZ
        arrived(layers.at[:, pl.ds(NZ * g, NZ), :], layer_recv.at[g])
    metrics(8, 16)

    def start_far():
        pl.semaphore_wait(far_sem, 1)
        edge_up.start()
        start_up()

    when(before_gap, start_far)
    for copy in (stress_in[1], stress_in[2], stress_in[5], velocity_in, material_in):
        copy.wait()
    when(x_low, lambda: arrived(halo_s.at[0], s_recv.at[0]))
    when(x_high, lambda: arrived(halo_s.at[1], s_recv.at[1]))
    join(halo_s, 0, NY)
    when(z_low, lambda: arrived(sigma.at[:, 0:2, 8:40, :], s_recv.at[2]))
    when(z_high, lambda: arrived(sigma.at[:, 18:20, 8:40, :], s_recv.at[3]))
    velocity_rows(8, 16, 2)
    send_rows(0, 8, 16)

    odd = y % 2
    strips = []
    for part in (1, 2):
        low = (odd == 1) if part == 1 else (odd == 0)
        side = odd if part == 1 else 1 - odd
        strips.append((part, low, pl.multiple_of(24 - 24 * side, 8), pl.multiple_of(40 - 40 * side, 8)))
    low_copy = remote(vel.at[:, 2:18, 8:10, :], vel.at[:, 2:18, 40:42, :], vy_send.at[1], vy_recv.at[1], down_y)
    high_copy = remote(vel.at[:, 2:18, 38:40, :], vel.at[:, 2:18, 6:8, :], vy_send.at[0], vy_recv.at[0], up_y)
    sends.append((y_low, low_copy))
    sends.append((y_high, high_copy))
    for part, low, first, outer in strips:
        when(low & y_low, lambda: arrived(terrain.at[:, 0:8, :], edge_recv.at[0]))
        when(~low & y_high, lambda: arrived(terrain.at[:, 40:48, :], edge_recv.at[1]))
        heights(outer)
        metrics(first, 8)
        for i, c in enumerate(Y_SENT):
            when(low & y_low, lambda: arrived(sigma.at[c, 2:18, 6:8, :], y_recv.at[0, i]))
            when(~low & y_high, lambda: arrived(sigma.at[c, 2:18, 40:42, :], y_recv.at[1, i]))
        velocity_rows(first, 8, 4)
        when(low & y_low, low_copy.start)
        when(~low & y_high, high_copy.start)
        send_rows(part, first, 8)

    memory_in.wait()

    def stress_rows(first, rows, ks):
        at = pl.ds(first, rows)
        for k in ks:
            m_x, m_y, m_z = (metric[i, k, at, :] for i in range(3))
            along_k = [d_k(vel, c, k, first, rows) for c in range(3)]
            along_x = [d_x(vel, c, k, first, rows, halo_v, c) - m_x * along_k[c] for c in range(3)]
            along_y = [d_y(vel, c, k, first, rows) - m_y * along_k[c] for c in range(3)]
            along_z = [m_z * along_k[c] for c in range(3)]
            block_id = mat[k, at, :]
            lam, mu, kept, gain = (look_up(i, block_id) for i in range(1, 5))
            volume = lam * (along_x[0] + along_y[1] + along_z[2])
            twice = mu + mu
            rates = (
                volume + twice * along_x[0],
                volume + twice * along_y[1],
                volume + twice * along_z[2],
                mu * (along_y[0] + along_x[1]),
                mu * (along_z[0] + along_x[2]),
                mu * (along_z[1] + along_y[2]),
            )
            for c, rate in enumerate(rates):
                new = kept * m_out[c, k, at, :] + gain * rate
                m_out[c, k, at, :] = new
                s_out[c, k, at, :] = sigma[c, 2 + k, pl.ds(8 + first, rows), :] + STEP * (rate - new)

    def inner(step, carry):
        stress_rows(8, 16, (2 * step, 2 * step + 1))
        return carry

    wait_x(0, 8, 16)
    lax.fori_loop(1, NZ // 2 - 1, inner, 0)
    wait_z(0, 8, 16)
    lax.fori_loop(0, 2, lambda step, carry: inner(step * (NZ // 2 - 1), carry), 0)
    for part, low, first, outer in strips:
        wait_x(part, first, 8)
        wait_z(part, first, 8)
        when(low & y_low, lambda: arrived(vel.at[:, 2:18, 6:8, :], vy_recv.at[0]))
        when(~low & y_high, lambda: arrived(vel.at[:, 2:18, 40:42, :], vy_recv.at[1]))

        def strip(step, carry):
            stress_rows(first, 8, [4 * step + i for i in range(4)])
            return carry

        lax.fori_loop(0, NZ // 4, strip, 0)
    for condition, copy in sends:
        when(condition, copy.wait_send)


def write_out(v_in, s_in, m_in, v_ref, s_ref, m_ref, sems):
    copies = [pltpu.make_async_copy(v_in, v_ref, sems.at[0])]
    for half in range(2):
        rows = slice(3 * half, 3 * half + 3)
        copies.append(pltpu.make_async_copy(s_in.at[rows], s_ref.at[rows], sems.at[1 + half]))
        copies.append(pltpu.make_async_copy(m_in.at[rows], m_ref.at[rows], sems.at[3 + half]))
    for copy in copies:
        copy.start()
    for copy in copies:
        copy.wait()


def local(*arrays):
    held = [pltpu.with_memory_space_constraint(array, pltpu.HBM) for array in arrays]
    f32, vmem, dma = jnp.float32, pltpu.VMEM, pltpu.SemaphoreType.DMA
    outputs = [(n, NZ, NY, NX) for n in (3, 6, 6)]
    results = pl.pallas_call(
        kernel,
        out_shape=tuple(vmem(shape, f32) for shape in outputs),
        in_specs=[pl.BlockSpec(memory_space=pltpu.HBM)] * len(held),
        out_specs=tuple(pl.BlockSpec(memory_space=vmem) for _ in outputs),
        scratch_shapes=[
            vmem((6, 20, 48, NX), f32),
            vmem((3, 20, 48, NX), f32),
            vmem((6, 48, 32), jnp.int32),
            vmem((3, 48, NX), f32),
            vmem((3, 24, NX), f32),
            vmem((2, GZ * NZ, NX), f32),
            vmem((NZ, NY, NX), jnp.int32),
            vmem((5, 8, NX), f32),
            vmem((3, NZ, NY, NX), f32),
            vmem((2, 2, NY, NX), f32),
            vmem((2, 2, NY, NX), f32),
            vmem((2, 2, NY, NX), f32),
            pltpu.SMEM((7, 16), f32),
            dma((17,)), dma((4,)), dma((4,)), dma((2, 3)), dma((2, 3)), dma((3,)), dma((4,)), dma((7,)), dma((6,)), dma((2,)), dma((2,)),
            dma((2, 3)), dma((2, 3)), dma((2, 3)), dma((2, 3)), dma((2,)), dma((2,)),
            pltpu.SemaphoreType.REGULAR,
        ],
        compiler_params=pltpu.CompilerParams(
            collective_id=0, has_side_effects=True, vmem_limit_bytes=24 << 20
        ),
    )(*held)
    return pl.pallas_call(
        write_out,
        out_shape=tuple(jax.ShapeDtypeStruct(shape, f32) for shape in outputs),
        in_specs=[pl.BlockSpec(memory_space=vmem)] * 3,
        out_specs=tuple(pl.BlockSpec(memory_space=pltpu.HBM) for _ in outputs),
        scratch_shapes=[dma((5,))],
        compiler_params=pltpu.CompilerParams(vmem_limit_bytes=8 << 20),
    )(*results)


def solution(mesh):
    field = P(None, "gz", "gy", "gx")
    return jax.shard_map(
        local,
        mesh=mesh,
        in_specs=(
            P("gy", ("gx", "gz")), P("gz"), P("gz"), P("gz", "gy", "gx"),
            P(), P(), P(), P(), P(), field, field, field,
        ),
        out_specs=(field, field, field),
        check_vma=False,
    )
```

```python
import functools

import jax
import jax.numpy as jnp
from jax import lax
from jax.experimental import pallas as pl
from jax.experimental.pallas import tpu as pltpu
from jax.sharding import PartitionSpec as P

MESH = pl.DeviceIdType.MESH
STEP = 0.3
GX, GY, GZ = 4, 16, 4
NZ, NY, NX = 16, 32, 128
X_PARTS = (0, 3, 4)
Y_PARTS = (3, 1, 5)
Y_SENT = (1, 3, 5)


def when(condition, action):
    if condition is None:
        action()
    else:
        pl.when(condition)(lambda: action())


def centred_12(before_2, before_1, after_1, after_2):
    return 8.0 * (after_1 - before_1) - (after_2 - before_2)


def kernel(
    elevation, layer_base, stretch, material, buoyancy, lame, shear, relax, weight, velocity, stress, memory,
    v_out, s_out, m_out,
    sigma, vel, terrain, wide, surf, layers, mat, tables, props, stencil, along, metric, packs, halo_s, halo_v,
    small, local_sem, s_send, s_recv, y_send, y_recv, layer_send, layer_recv, t_send, t_recv, edge_send, edge_recv,
    z_send, z_recv, x_send, x_recv, vy_send, vy_recv, far_sem,
):
    x, y, z = lax.axis_index("gx"), lax.axis_index("gy"), lax.axis_index("gz")
    x_low, x_high = x > 0, x < GX - 1
    y_low, y_high = y > 0, y < GY - 1
    z_low, z_high = z > 0, z < GZ - 1
    before_gap, after_gap = y == GY // 2 - 1, y == GY // 2
    lane = lax.broadcasted_iota(jnp.int32, (8, NX), 1)

    own_slot = 1 + z
    tables_in = (buoyancy, lame, shear, relax, weight, layer_base, stretch)
    scalars = [pltpu.make_async_copy(ref, small.at[i], local_sem.at[i]) for i, ref in enumerate(tables_in)]
    for copy in scalars:
        copy.start()
    stress_in = {
        c: pltpu.make_async_copy(stress.at[c], sigma.at[c, 2:18, 8:40, :], local_sem.at[7 + c])
        for c in (0, 3, 4, 1, 2, 5)
    }
    for c in (0, 3, 4):
        stress_in[c].start()
    material_in = pltpu.make_async_copy(material, mat, local_sem.at[15])
    material_in.start()
    for c in (1, 2, 5):
        stress_in[c].start()
    elevation_in = pltpu.make_async_copy(elevation, terrain.at[own_slot, 8:40, :], local_sem.at[13])
    velocity_in = pltpu.make_async_copy(velocity, v_out, local_sem.at[14])
    memory_in = pltpu.make_async_copy(memory, m_out, local_sem.at[16])
    for copy in (elevation_in, velocity_in, memory_in):
        copy.start()

    barrier = pltpu.get_barrier_semaphore()
    beside = [(None, {"gz": (z + d) % GZ}) for d in range(1, GZ)]
    for g in range(GZ):
        beside.append((x_high & ((z == g) | (z == GZ - 1) | (g == 0)), {"gx": x + 1, "gz": g}))
        beside.append((x_low & ((z == g) | (z == 0) | (g == GZ - 1)), {"gx": x - 1, "gz": g}))
    up_y, down_y = {"gy": y + 1}, {"gy": y - 1}
    for condition, target in [(y_high, up_y), (y_low & ~after_gap, down_y)] + beside:
        when(condition, lambda target=target: pl.semaphore_signal(barrier, inc=1, device_id=target, device_id_type=MESH))
    expected = [y_low, y_high & ~before_gap] + [condition for condition, _ in beside]

    pl.semaphore_wait(barrier, sum(1 if c is None else c.astype(jnp.int32) for c in expected))
    when(after_gap, lambda: pl.semaphore_signal(far_sem, inc=1, device_id=down_y, device_id_type=MESH))

    def remote(source, to, send, recv, target):
        return pltpu.make_async_remote_copy(
            src_ref=source, dst_ref=to, send_sem=send, recv_sem=recv, device_id=target, device_id_type=MESH
        )

    sends = []

    def send(condition, copy, now=True):
        sends.append((condition, copy))
        if now:
            when(condition, copy.start)
        return copy

    up_copies = [
        send(y_high, remote(stress.at[c, :, 30:32, :], sigma.at[c, 2:18, 6:8, :], y_send.at[0, i], y_recv.at[0, i], up_y), now=False)
        for i, c in enumerate(Y_SENT)
    ]

    def start_up():
        for copy in up_copies:
            copy.start()

    when(y_high & ~before_gap, start_up)
    for d in range(1, GZ):
        send(None, remote(elevation, terrain.at[own_slot, 8:40, :], t_send.at[d - 1], t_recv.at[own_slot], {"gz": (z + d) % GZ}))
    for g in range(GZ):
        send(x_high & (z == GZ - 1), remote(elevation, terrain.at[0, 8:40, :], t_send.at[3 + g], t_recv.at[0], {"gx": x + 1, "gz": g}))
        send(x_low & (z == 0), remote(elevation, terrain.at[5, 8:40, :], t_send.at[3 + g], t_recv.at[5], {"gx": x - 1, "gz": g}))
    for i, c in enumerate(Y_SENT):
        send(y_low, remote(stress.at[c, :, 0:2, :], sigma.at[c, 2:18, 40:42, :], y_send.at[1, i], y_recv.at[1, i], down_y))
    send(z_high, remote(stress.at[:, 14:16], sigma.at[:, 0:2, 8:40, :], s_send.at[2], s_recv.at[2], {"gz": z + 1}))
    send(z_low, remote(stress.at[:, 0:2], sigma.at[:, 18:20, 8:40, :], s_send.at[3], s_recv.at[3], {"gz": z - 1}))

    zero = jnp.zeros((8, NX), jnp.float32)

    def pack_spot(k, i):
        at = 4 * (k + (NZ if i == 1 else 0))
        return at, (lane >= at) & (lane < at + 4)

    def pack_layer(held, blocks, i, k, at, spot):
        for r, block in enumerate(blocks):
            j = len(blocks) * (i // 2) + r
            held[j] = jnp.where(spot, pltpu.roll(block, at + 2, 1), held[j])

    def pack_stress(step, held):
        held = list(held)
        for k in (2 * step, 2 * step + 1):
            for i, c in enumerate(X_PARTS):
                at, spot = pack_spot(k, i)
                pack_layer(held, [sigma[c, 2 + k, 8 + 8 * r : 16 + 8 * r, :] for r in range(4)], i, k, at, spot)
        return tuple(held)

    for copy in scalars:
        copy.wait()
    for k in range(NZ):
        for row in range(2):
            layers[row, pl.ds(NZ * z + k, 1), :] = jnp.full((1, NX), small[5 + row, k], jnp.float32)

    for c in X_PARTS:
        stress_in[c].wait()
    held = lax.fori_loop(0, NZ // 2, pack_stress, (zero,) * 8)
    for j in range(8):
        packs[0, j // 4, 8 * (j % 4) : 8 * (j % 4) + 8, :] = held[j]

    mine = pl.ds(NZ * z, NZ)
    for d in range(1, GZ):
        send(None, remote(layers.at[:, mine, :], layers.at[:, mine, :], layer_send.at[d - 1], layer_recv.at[z], {"gz": (z + d) % GZ}))
    columns = []
    for i in range(5):
        column = zero
        for block_id in range(16):
            column = jnp.where(lane == block_id, small[i, block_id], column)
        columns.append(column)
    keep = jnp.exp(-STEP / jnp.where(lane < 16, columns[3], 1.0))
    tables[0] = columns[0] * (STEP / 12.0)
    tables[1] = columns[1] * (1.0 / 12.0)
    tables[2] = columns[2] * (1.0 / 12.0)
    tables[3] = keep
    tables[4] = (1.0 - keep) * columns[4]

    send(x_high, remote(packs.at[0], halo_s.at[0], s_send.at[0], s_recv.at[0], {"gx": x + 1}))
    send(x_low, remote(packs.at[0], halo_s.at[1], s_send.at[1], s_recv.at[1], {"gx": x - 1}))
    material_in.wait()

    def property_layer(k, carry):
        for r in range(4):
            rows = slice(8 * r, 8 * r + 8)
            block_id = mat[k, rows, :]
            for i in range(5):
                props[i, k, rows, :] = jnp.take_along_axis(tables[i], block_id, axis=1)
        return carry

    lax.fori_loop(0, NZ, property_layer, 0)

    offset = lax.broadcasted_iota(jnp.int32, (NX, NX), 0) - lax.broadcasted_iota(jnp.int32, (NX, NX), 1)
    weights = jnp.zeros((NX, NX), jnp.float32)
    for distance, factor in ((-2, 1.0), (-1, -8.0), (1, 8.0), (2, -1.0)):
        weights = jnp.where(offset == distance, factor, weights)
    stencil[...] = weights.astype(jnp.bfloat16)

    def differentiate_x(parts, field, first, rows, unroll):
        def layers_of(step, carry):
            spots = [(i, c, unroll * step + n) for i, c in enumerate(parts) for n in range(unroll)]
            rest = jnp.concatenate([field[c, k + 2, pl.ds(8 + first, rows), :] for _, c, k in spots], axis=0)
            total = None
            for _ in range(3):
                piece = rest.astype(jnp.bfloat16)
                rest = rest - piece.astype(jnp.float32)
                product = jnp.dot(piece, stencil[...], preferred_element_type=jnp.float32)
                total = product if total is None else total + product
            for n, (i, _, k) in enumerate(spots):
                along[i, k, pl.ds(first, rows), :] = total[n * rows : (n + 1) * rows]
            return carry

        lax.fori_loop(0, NZ // unroll, layers_of, 0)

    differentiate_x(X_PARTS, sigma, 0, NY, 4)

    def arrived(ref, recv):
        remote(ref, ref, s_send.at[0], recv, {"gz": z}).wait_recv()

    def zero_z(first):
        sigma[:, pl.ds(first, 2), 8:40, :] = jnp.zeros((6, 2, NY, NX), jnp.float32)
        vel[:, pl.ds(first, 2), 8:40, :] = jnp.zeros((3, 2, NY, NX), jnp.float32)

    def zero_y(first):
        def layer(k, carry):
            for c in Y_SENT:
                sigma[c, 2 + k, first : first + 8, :] = zero
            for c in range(3):
                vel[c, 2 + k, first : first + 8, :] = zero
            return carry

        lax.fori_loop(0, NZ, layer, 0)
        for m in range(6):
            terrain[m, first : first + 8, :] = jnp.zeros((8, 32), jnp.int32)

    def zero_x(side, slot):
        halo_s[side] = jnp.zeros((2, NY, NX), jnp.float32)
        halo_v[side] = jnp.zeros((2, NY, NX), jnp.float32)
        terrain[slot, 8:40, :] = jnp.zeros((32, 32), jnp.int32)

    when(z == 0, lambda: zero_z(0))
    when(z == GZ - 1, lambda: zero_z(18))
    when(y == 0, lambda: zero_y(0))
    when(y == GY - 1, lambda: zero_y(40))
    when(x == 0, lambda: zero_x(0, 0))
    when(x == GX - 1, lambda: zero_x(1, 5))

    elevation_in.wait()
    for d in range(1, GZ):
        g = (z + d) % GZ
        arrived(terrain.at[1 + g, 8:40, :], t_recv.at[1 + g])
    when(x_low, lambda: arrived(terrain.at[0, 8:40, :], t_recv.at[0]))
    when(x_high, lambda: arrived(terrain.at[5, 8:40, :], t_recv.at[5]))
    edge_up = send(y_high, remote(terrain.at[:, 32:40, :], terrain.at[:, 0:8, :], edge_send.at[0], edge_recv.at[0], up_y), now=False)
    when(y_high & ~before_gap, edge_up.start)
    send(y_low, remote(terrain.at[:, 8:16, :], terrain.at[:, 40:48, :], edge_send.at[1], edge_recv.at[1], down_y))

    def heights(row):
        rows = pl.ds(row, 8)
        held = [terrain[m, rows, :].astype(jnp.float32) / 200.0 for m in range(6)]
        blank = jnp.zeros((8, 96), jnp.float32)
        wide[0, rows, :] = jnp.concatenate([blank, held[0]], axis=1)
        wide[1, rows, :] = jnp.concatenate(held[1:5], axis=1)
        wide[2, rows, :] = jnp.concatenate([held[5], blank], axis=1)

    binomial = (1.0, 4.0, 6.0, 4.0, 1.0)

    def metrics(first, rows):
        along_y = []
        for part in range(3):
            total = jnp.zeros((rows + 8, NX), jnp.float32)
            for d, factor in enumerate(binomial):
                total = total + factor * wide[part, pl.ds(first + 2 + d, rows + 8), :]
            along_y.append(total / 16.0)
        row = jnp.concatenate(along_y, axis=1)
        total = jnp.zeros_like(row)
        for d, factor in enumerate(binomial):
            total = total + factor * (row if d == 2 else pltpu.roll(row, (2 - d) % 384, 1))
        total = total / 16.0
        for part in range(3):
            surf[part, 0 : rows + 8, :] = total[:, 128 * part : 128 * part + 128]
        own = jnp.concatenate([surf[part, 4 : 4 + rows, :] for part in range(3)], axis=1)
        height = own[:, 128:256]
        shifted = [pltpu.roll(own, d % 384, 1)[:, 128:256] for d in (2, 1, -1, -2)]
        slope_x = centred_12(*shifted) / 12.0
        slope_y = centred_12(*[surf[1, 4 + d : 4 + d + rows, :] for d in (-2, -1, 1, 2)]) / 12.0

        def above(step, total):
            for layer in [4 * step + i for i in range(4)]:
                base, follow = layers[0, pl.ds(layer, 1), :], layers[1, pl.ds(layer, 1), :]
                total = total + follow * (base * jnp.exp(follow * height))
            return total

        upper = lax.fori_loop(0, (NZ // 4) * z, above, jnp.zeros((rows, NX), jnp.float32))

        def layer(step, total):
            for k in [4 * step + i for i in range(4)]:
                base, follow = layers[0, pl.ds(NZ * z + k, 1), :], layers[1, pl.ds(NZ * z + k, 1), :]
                thickness = base * jnp.exp(follow * height)
                weighted = follow * thickness
                inverse = 1.0 / thickness
                factor = (total + 0.5 * weighted - 1.0) * inverse
                at = pl.ds(first, rows)
                metric[0, k, at, :] = slope_x * factor
                metric[1, k, at, :] = slope_y * factor
                metric[2, k, at, :] = inverse
                total = total + weighted
            return total

        lax.fori_loop(0, NZ // 4, layer, upper)

    def d_k(field, c, k, first, rows):
        return centred_12(*[field[c, k + 2 + d, pl.ds(8 + first, rows), :] for d in (-2, -1, 1, 2)])

    def d_y(field, c, k, first, rows):
        return centred_12(*[field[c, k + 2, pl.ds(8 + first + d, rows), :] for d in (-2, -1, 1, 2)])

    def d_x(c, k, first, rows, halo, i):
        side = lax.broadcasted_iota(jnp.int32, (rows, NX), 1)
        at = 4 * (k + (NZ if i == 1 else 0))
        fix = pltpu.roll(halo[0, i // 2, pl.ds(first, rows), :], 126 - at, 1)
        return along[i, k, pl.ds(first, rows), :] + jnp.where((side < 2) | (side >= 126), fix, 0.0)

    def join(halo, first, rows):
        spot = lax.broadcasted_iota(jnp.int32, (rows, NX), 1) % 4
        at = pl.ds(first, rows)
        for i in range(2):
            change = jnp.where(spot < 2, halo[0, i, at, :], halo[1, i, at, :])
            low = 8.0 * jnp.where(spot == 1, pltpu.roll(change, 127, 1), 0.0) - pltpu.roll(change, 126, 1)
            high = pltpu.roll(change, 2, 1) - 8.0 * jnp.where(spot == 2, pltpu.roll(change, 1, 1), 0.0)
            halo[0, i, at, :] = jnp.where(spot < 2, low, high)

    def velocity_rows(first, rows, unroll):
        blocks = rows // 8

        def velocity_layer(step, carried):
            held, last = list(carried[0]), carried[1]
            at = pl.ds(first, rows)
            ks = [unroll * step + i for i in range(unroll)]
            pack_rows(held, [k - unroll for k in ks], last)
            made = []
            for k in ks:
                m_x, m_y, m_z = (metric[i, k, at, :] for i in range(3))
                grad_k = [d_k(sigma, c, k, first, rows) for c in range(6)]
                grad_x = [d_x(c, k, first, rows, halo_s, i) for i, c in enumerate(X_PARTS)]
                grad_y = [d_y(sigma, c, k, first, rows) for c in Y_PARTS]
                scale = props[0, k, at, :]
                row = []
                for c, (a, b, d) in enumerate(((0, 3, 4), (3, 1, 5), (4, 5, 2))):
                    accel = (grad_x[c] - m_x * grad_k[a]) + (grad_y[c] - m_y * grad_k[b]) + m_z * grad_k[d]
                    new = v_out[c, k, at, :] + scale * accel
                    v_out[c, k, at, :] = new
                    vel[c, 2 + k, pl.ds(8 + first, rows), :] = new
                    row.append(new)
                made.append(row)
            return tuple(held), made

        def pack_rows(held, ks, made):
            for k, row in zip(ks, made):
                for c in range(3):
                    spot_at, spot = pack_spot(k, c)
                    pack_layer(held, [row[c][8 * r : 8 * r + 8] for r in range(blocks)], c, k, spot_at, spot)

        nothing = jnp.zeros((rows, NX), jnp.float32)
        start = ((zero,) * (2 * blocks), [[nothing] * 3 for _ in range(unroll)])
        held, last = lax.fori_loop(0, NZ // unroll, velocity_layer, start)
        held = list(held)
        pack_rows(held, range(NZ - unroll, NZ), last)
        for j in range(2 * blocks):
            packs[1, j // blocks, pl.ds(first + 8 * (j % blocks), 8), :] = held[j]

    def send_rows(part, first, rows):
        at = pl.ds(first, rows)
        send(x_high, remote(packs.at[1, :, at, :], halo_v.at[0, :, at, :], x_send.at[0, part], x_recv.at[0, part], {"gx": x + 1}))
        send(x_low, remote(packs.at[1, :, at, :], halo_v.at[1, :, at, :], x_send.at[1, part], x_recv.at[1, part], {"gx": x - 1}))
        at = pl.ds(8 + first, rows)
        send(z_high, remote(vel.at[:, 16:18, at, :], vel.at[:, 0:2, at, :], z_send.at[0, part], z_recv.at[0, part], {"gz": z + 1}))
        send(z_low, remote(vel.at[:, 2:4, at, :], vel.at[:, 18:20, at, :], z_send.at[1, part], z_recv.at[1, part], {"gz": z - 1}))

    def wait_x(part, first, rows):
        at = pl.ds(first, rows)
        when(x_low, lambda: arrived(halo_v.at[0, :, at, :], x_recv.at[0, part]))
        when(x_high, lambda: arrived(halo_v.at[1, :, at, :], x_recv.at[1, part]))
        join(halo_v, first, rows)

    def wait_z(part, first, rows):
        at = pl.ds(8 + first, rows)
        when(z_low, lambda: arrived(vel.at[:, 0:2, at, :], z_recv.at[0, part]))
        when(z_high, lambda: arrived(vel.at[:, 18:20, at, :], z_recv.at[1, part]))

    for row in range(8, 40, 8):
        heights(row)
    for d in range(1, GZ):
        g = (z + d) % GZ
        arrived(layers.at[:, pl.ds(NZ * g, NZ), :], layer_recv.at[g])
    metrics(8, 16)

    def start_far():
        pl.semaphore_wait(far_sem, 1)
        edge_up.start()
        start_up()

    when(before_gap, start_far)
    for copy in (stress_in[1], stress_in[2], stress_in[5], velocity_in):
        copy.wait()
    when(x_low, lambda: arrived(halo_s.at[0], s_recv.at[0]))
    when(x_high, lambda: arrived(halo_s.at[1], s_recv.at[1]))
    join(halo_s, 0, NY)
    when(z_low, lambda: arrived(sigma.at[:, 0:2, 8:40, :], s_recv.at[2]))
    when(z_high, lambda: arrived(sigma.at[:, 18:20, 8:40, :], s_recv.at[3]))
    velocity_rows(8, 16, 2)
    send_rows(0, 8, 16)

    odd = y % 2
    strips = []
    for part in (1, 2):
        low = (odd == 1) if part == 1 else (odd == 0)
        side = odd if part == 1 else 1 - odd
        strips.append((part, low, pl.multiple_of(24 - 24 * side, 8), pl.multiple_of(40 - 40 * side, 8)))
    low_copy = remote(vel.at[:, 2:18, 8:10, :], vel.at[:, 2:18, 40:42, :], vy_send.at[1], vy_recv.at[1], down_y)
    high_copy = remote(vel.at[:, 2:18, 38:40, :], vel.at[:, 2:18, 6:8, :], vy_send.at[0], vy_recv.at[0], up_y)
    sends.append((y_low, low_copy))
    sends.append((y_high, high_copy))
    for part, low, first, outer in strips:
        when(low & y_low, lambda: arrived(terrain.at[:, 0:8, :], edge_recv.at[0]))
        when(~low & y_high, lambda: arrived(terrain.at[:, 40:48, :], edge_recv.at[1]))
        heights(outer)
        metrics(first, 8)
        for i, c in enumerate(Y_SENT):
            when(low & y_low, lambda: arrived(sigma.at[c, 2:18, 6:8, :], y_recv.at[0, i]))
            when(~low & y_high, lambda: arrived(sigma.at[c, 2:18, 40:42, :], y_recv.at[1, i]))
        velocity_rows(first, 8, 4)
        when(low & y_low, low_copy.start)
        when(~low & y_high, high_copy.start)
        send_rows(part, first, 8)
        if part == 1:
            differentiate_x(range(3), vel, 8, 16, 4)
        differentiate_x(range(3), vel, first, 8, 8)

    memory_in.wait()

    def stress_rows(first, rows, unroll, steps, stride=1):
        at = pl.ds(first, rows)

        def stress_layer(step, carry):
            for k in [unroll * stride * step + i for i in range(unroll)]:
                grad_x = [d_x(c, k, first, rows, halo_v, c) for c in range(3)]
                m_x, m_y, m_z = (metric[i, k, at, :] for i in range(3))
                along_k = [d_k(vel, c, k, first, rows) for c in range(3)]
                along_x = [grad_x[c] - m_x * along_k[c] for c in range(3)]
                along_y = [d_y(vel, c, k, first, rows) - m_y * along_k[c] for c in range(3)]
                along_z = [m_z * along_k[c] for c in range(3)]
                lam, mu, kept, gain = (props[i, k, at, :] for i in range(1, 5))
                volume = lam * (along_x[0] + along_y[1] + along_z[2])
                twice = mu + mu
                rates = (
                    volume + twice * along_x[0],
                    volume + twice * along_y[1],
                    volume + twice * along_z[2],
                    mu * (along_y[0] + along_x[1]),
                    mu * (along_z[0] + along_x[2]),
                    mu * (along_z[1] + along_y[2]),
                )
                for c, rate in enumerate(rates):
                    new = kept * m_out[c, k, at, :] + gain * rate
                    m_out[c, k, at, :] = new
                    s_out[c, k, at, :] = sigma[c, 2 + k, pl.ds(8 + first, rows), :] + STEP * (rate - new)
            return carry

        lax.fori_loop(steps[0], steps[1], stress_layer, 0)

    wait_x(0, 8, 16)
    stress_rows(8, 16, 2, (1, NZ // 2 - 1))
    wait_z(0, 8, 16)
    stress_rows(8, 16, 2, (0, 2), NZ // 2 - 1)
    for part, low, first, outer in strips:
        wait_x(part, first, 8)
        wait_z(part, first, 8)
        when(low & y_low, lambda: arrived(vel.at[:, 2:18, 6:8, :], vy_recv.at[0]))
        when(~low & y_high, lambda: arrived(vel.at[:, 2:18, 40:42, :], vy_recv.at[1]))
        stress_rows(first, 8, 4, (0, NZ // 4))
    for condition, copy in sends:
        when(condition, copy.wait_send)


def write_out(v_in, s_in, m_in, v_ref, s_ref, m_ref, sems):
    pairs = [(v_in, v_ref, c) for c in range(3)] + [(a, b, c) for a, b in ((s_in, s_ref), (m_in, m_ref)) for c in range(6)]
    copies = [pltpu.make_async_copy(a.at[c], b.at[c], sems.at[i]) for i, (a, b, c) in enumerate(pairs)]
    for copy in copies:
        copy.start()
    for copy in copies:
        copy.wait()


def local(*arrays):
    held = [pltpu.with_memory_space_constraint(array, pltpu.HBM) for array in arrays]
    f32, vmem, dma = jnp.float32, pltpu.VMEM, pltpu.SemaphoreType.DMA
    outputs = [(n, NZ, NY, NX) for n in (3, 6, 6)]
    results = pl.pallas_call(
        kernel,
        out_shape=tuple(vmem(shape, f32) for shape in outputs),
        in_specs=[pl.BlockSpec(memory_space=pltpu.HBM)] * len(held),
        out_specs=tuple(pl.BlockSpec(memory_space=vmem) for _ in outputs),
        scratch_shapes=[
            vmem((6, 20, 48, NX), f32),
            vmem((3, 20, 48, NX), f32),
            vmem((6, 48, 32), jnp.int32),
            vmem((3, 48, NX), f32),
            vmem((3, 24, NX), f32),
            vmem((2, GZ * NZ, NX), f32),
            vmem((NZ, NY, NX), jnp.int32),
            vmem((5, 8, NX), f32),
            vmem((5, NZ, NY, NX), f32),
            vmem((NX, NX), jnp.bfloat16),
            vmem((3, NZ, NY, NX), f32),
            vmem((3, NZ, NY, NX), f32),
            vmem((2, 2, NY, NX), f32),
            vmem((2, 2, NY, NX), f32),
            vmem((2, 2, NY, NX), f32),
            pltpu.SMEM((7, 16), f32),
            dma((17,)), dma((4,)), dma((4,)), dma((2, 3)), dma((2, 3)), dma((3,)), dma((4,)), dma((7,)), dma((6,)), dma((2,)), dma((2,)),
            dma((2, 3)), dma((2, 3)), dma((2, 3)), dma((2, 3)), dma((2,)), dma((2,)),
            pltpu.SemaphoreType.REGULAR,
        ],
        compiler_params=pltpu.CompilerParams(
            collective_id=0, has_side_effects=True, vmem_limit_bytes=24 << 20
        ),
    )(*held)
    return pl.pallas_call(
        write_out,
        out_shape=tuple(jax.ShapeDtypeStruct(shape, f32) for shape in outputs),
        in_specs=[pl.BlockSpec(memory_space=vmem)] * 3,
        out_specs=tuple(pl.BlockSpec(memory_space=pltpu.HBM) for _ in outputs),
        scratch_shapes=[dma((15,))],
        compiler_params=pltpu.CompilerParams(vmem_limit_bytes=8 << 20),
    )(*results)


def solution(mesh):
    field = P(None, "gz", "gy", "gx")
    return jax.shard_map(
        local,
        mesh=mesh,
        in_specs=(
            P("gy", ("gx", "gz")), P("gz"), P("gz"), P("gz", "gy", "gx"),
            P(), P(), P(), P(), P(), field, field, field,
        ),
        out_specs=(field, field, field),
        check_vma=False,
    )
```

```python
import functools

import jax
import jax.numpy as jnp
from jax import lax
from jax.experimental import pallas as pl
from jax.experimental.pallas import tpu as pltpu
from jax.sharding import PartitionSpec as P

MESH = pl.DeviceIdType.MESH
STEP = 0.3
GX, GY, GZ = 4, 16, 4
NZ, NY, NX = 16, 32, 128
X_PARTS = (0, 3, 4)
Y_PARTS = (3, 1, 5)
Y_SENT = (1, 3, 5)


def when(condition, action):
    if condition is None:
        action()
    else:
        pl.when(condition)(lambda: action())


def centred_12(before_2, before_1, after_1, after_2):
    return 8.0 * (after_1 - before_1) - (after_2 - before_2)


def kernel(
    elevation, layer_base, stretch, material, buoyancy, lame, shear, relax, weight, velocity, stress, memory,
    v_out, s_out, m_out,
    sigma, vel, terrain, wide, surf, layers, mat, tables, props, stencil, along, metric, packs, halo_s, halo_v,
    small, local_sem, s_send, s_recv, y_send, y_recv, layer_send, layer_recv, t_send, t_recv, edge_send, edge_recv,
    z_send, z_recv, x_send, x_recv, vy_send, vy_recv, zs_send, zs_recv, gap_out, gap_in, gap_sem, far_sem,
):
    x, y, z = lax.axis_index("gx"), lax.axis_index("gy"), lax.axis_index("gz")
    x_low, x_high = x > 0, x < GX - 1
    y_low, y_high = y > 0, y < GY - 1
    z_low, z_high = z > 0, z < GZ - 1
    before_gap, after_gap = y == GY // 2 - 1, y == GY // 2
    lane = lax.broadcasted_iota(jnp.int32, (8, NX), 1)

    own_slot = 1 + z
    tables_in = (buoyancy, lame, shear, relax, weight, layer_base, stretch)
    scalars = [pltpu.make_async_copy(ref, small.at[i], local_sem.at[i]) for i, ref in enumerate(tables_in)]
    for copy in scalars:
        copy.start()
    stress_in = {
        c: pltpu.make_async_copy(stress.at[c], sigma.at[c, 2:18, 8:40, :], local_sem.at[7 + c])
        for c in (0, 3, 4, 1, 2, 5)
    }
    for c in (0, 3, 4):
        stress_in[c].start()
    material_in = pltpu.make_async_copy(material, mat, local_sem.at[15])
    material_in.start()
    for c in (1, 2, 5):
        stress_in[c].start()
    elevation_in = pltpu.make_async_copy(elevation, terrain.at[own_slot, 8:40, :], local_sem.at[13])
    velocity_in = pltpu.make_async_copy(velocity, v_out, local_sem.at[14])
    memory_in = pltpu.make_async_copy(memory, m_out, local_sem.at[16])
    for copy in (elevation_in, velocity_in, memory_in):
        copy.start()

    barrier = pltpu.get_barrier_semaphore()
    beside = [(None, {"gz": (z + d) % GZ}) for d in range(1, GZ)]
    for g in range(GZ):
        beside.append((x_high & ((z == g) | (z == GZ - 1) | (g == 0)), {"gx": x + 1, "gz": g}))
        beside.append((x_low & ((z == g) | (z == 0) | (g == GZ - 1)), {"gx": x - 1, "gz": g}))
    up_y, down_y = {"gy": y + 1}, {"gy": y - 1}
    for condition, target in [(y_high, up_y), (y_low & ~after_gap, down_y)] + beside:
        when(condition, lambda target=target: pl.semaphore_signal(barrier, inc=1, device_id=target, device_id_type=MESH))
    expected = [y_low, y_high & ~before_gap] + [condition for condition, _ in beside]

    pl.semaphore_wait(barrier, sum(1 if c is None else c.astype(jnp.int32) for c in expected))
    when(after_gap, lambda: pl.semaphore_signal(far_sem, inc=1, device_id=down_y, device_id_type=MESH))

    def remote(source, to, send, recv, target):
        return pltpu.make_async_remote_copy(
            src_ref=source, dst_ref=to, send_sem=send, recv_sem=recv, device_id=target, device_id_type=MESH
        )

    sends = []

    def send(condition, copy, now=True):
        sends.append((condition, copy))
        if now:
            when(condition, copy.start)
        return copy

    up_copies = [
        send(y_high, remote(stress.at[c, :, 30:32, :], sigma.at[c, 2:18, 6:8, :], y_send.at[0, i], y_recv.at[0, i], up_y), now=False)
        for i, c in enumerate(Y_SENT)
    ]

    def start_up():
        for copy in up_copies:
            copy.start()

    when(y_high & ~before_gap, start_up)
    for d in range(1, GZ):
        send(None, remote(elevation, terrain.at[own_slot, 8:40, :], t_send.at[d - 1], t_recv.at[own_slot], {"gz": (z + d) % GZ}))
    for g in range(GZ):
        send(x_high & (z == GZ - 1), remote(elevation, terrain.at[0, 8:40, :], t_send.at[3 + g], t_recv.at[0], {"gx": x + 1, "gz": g}))
        send(x_low & (z == 0), remote(elevation, terrain.at[5, 8:40, :], t_send.at[3 + g], t_recv.at[5], {"gx": x - 1, "gz": g}))
    for i, c in enumerate(Y_SENT):
        send(y_low, remote(stress.at[c, :, 0:2, :], sigma.at[c, 2:18, 40:42, :], y_send.at[1, i], y_recv.at[1, i], down_y))
    odd = y % 2
    strips = []
    for part in (1, 2):
        low = (odd == 1) if part == 1 else (odd == 0)
        side = odd if part == 1 else 1 - odd
        strips.append((part, low, pl.multiple_of(24 - 24 * side, 8), pl.multiple_of(40 - 40 * side, 8)))
    z_parts = [(0, 8, 16)] + [(part, first, 8) for part, _, first, _ in strips]
    z_copies = []
    for part, first, rows in z_parts:
        at, to = pl.ds(first, rows), pl.ds(8 + first, rows)
        z_copies.append((
            send(z_high, remote(stress.at[:, 14:16, at, :], sigma.at[:, 0:2, to, :], zs_send.at[0, part], zs_recv.at[0, part], {"gz": z + 1}), now=False),
            send(z_low, remote(stress.at[:, 0:2, at, :], sigma.at[:, 18:20, to, :], zs_send.at[1, part], zs_recv.at[1, part], {"gz": z - 1}), now=False),
        ))

    def start_z(part, condition):
        when(z_high if condition is None else condition & z_high, z_copies[part][0].start)
        when(z_low if condition is None else condition & z_low, z_copies[part][1].start)

    start_z(2, after_gap)
    start_z(0, None)
    start_z(1, None)
    start_z(2, ~after_gap)

    zero = jnp.zeros((8, NX), jnp.float32)

    def pack_spot(k, i):
        at = 4 * (k + (NZ if i == 1 else 0))
        return at, (lane >= at) & (lane < at + 4)

    def pack_layer(held, blocks, i, k, at, spot):
        for r, block in enumerate(blocks):
            j = len(blocks) * (i // 2) + r
            held[j] = jnp.where(spot, pltpu.roll(block, at + 2, 1), held[j])

    def pack_stress(step, held):
        held = list(held)
        for k in (2 * step, 2 * step + 1):
            for i, c in enumerate(X_PARTS):
                at, spot = pack_spot(k, i)
                pack_layer(held, [sigma[c, 2 + k, 8 + 8 * r : 16 + 8 * r, :] for r in range(4)], i, k, at, spot)
        return tuple(held)

    for copy in scalars:
        copy.wait()
    for k in range(NZ):
        for row in range(2):
            layers[row, pl.ds(NZ * z + k, 1), :] = jnp.full((1, NX), small[5 + row, k], jnp.float32)

    for c in X_PARTS:
        stress_in[c].wait()
    held = lax.fori_loop(0, NZ // 2, pack_stress, (zero,) * 8)
    for j in range(8):
        packs[0, j // 4, 8 * (j % 4) : 8 * (j % 4) + 8, :] = held[j]

    mine = pl.ds(NZ * z, NZ)
    for d in range(1, GZ):
        send(None, remote(layers.at[:, mine, :], layers.at[:, mine, :], layer_send.at[d - 1], layer_recv.at[z], {"gz": (z + d) % GZ}))
    columns = []
    for i in range(5):
        column = zero
        for block_id in range(16):
            column = jnp.where(lane == block_id, small[i, block_id], column)
        columns.append(column)
    keep = jnp.exp(-STEP / jnp.where(lane < 16, columns[3], 1.0))
    tables[0] = columns[0] * (STEP / 12.0)
    tables[1] = columns[1] * (1.0 / 12.0)
    tables[2] = columns[2] * (1.0 / 12.0)
    tables[3] = keep
    tables[4] = (1.0 - keep) * columns[4]

    send(x_high, remote(packs.at[0], halo_s.at[0], s_send.at[0], s_recv.at[0], {"gx": x + 1}))
    send(x_low, remote(packs.at[0], halo_s.at[1], s_send.at[1], s_recv.at[1], {"gx": x - 1}))
    material_in.wait()

    def property_layer(k, carry):
        for r in range(4):
            rows = slice(8 * r, 8 * r + 8)
            block_id = mat[k, rows, :]
            for i in range(5):
                props[i, k, rows, :] = jnp.take_along_axis(tables[i], block_id, axis=1)
        return carry

    lax.fori_loop(0, NZ, property_layer, 0)

    offset = lax.broadcasted_iota(jnp.int32, (NX, NX), 0) - lax.broadcasted_iota(jnp.int32, (NX, NX), 1)
    weights = jnp.zeros((NX, NX), jnp.float32)
    for distance, factor in ((-2, 1.0), (-1, -8.0), (1, 8.0), (2, -1.0)):
        weights = jnp.where(offset == distance, factor, weights)
    stencil[...] = weights.astype(jnp.bfloat16)

    def differentiate_x(parts, field, first, rows, unroll):
        def layers_of(step, carry):
            spots = [(i, c, unroll * step + n) for i, c in enumerate(parts) for n in range(unroll)]
            rest = jnp.concatenate([field[c, k + 2, pl.ds(8 + first, rows), :] for _, c, k in spots], axis=0)
            total = None
            for _ in range(3):
                piece = rest.astype(jnp.bfloat16)
                rest = rest - piece.astype(jnp.float32)
                product = jnp.dot(piece, stencil[...], preferred_element_type=jnp.float32)
                total = product if total is None else total + product
            for n, (i, _, k) in enumerate(spots):
                along[i, k, pl.ds(first, rows), :] = total[n * rows : (n + 1) * rows]
            return carry

        lax.fori_loop(0, NZ // unroll, layers_of, 0)

    differentiate_x(X_PARTS, sigma, 0, NY, 4)

    def arrived(ref, recv):
        remote(ref, ref, s_send.at[0], recv, {"gz": z}).wait_recv()

    def zero_z(first):
        sigma[:, pl.ds(first, 2), 8:40, :] = jnp.zeros((6, 2, NY, NX), jnp.float32)
        vel[:, pl.ds(first, 2), 8:40, :] = jnp.zeros((3, 2, NY, NX), jnp.float32)

    def zero_y(first):
        def layer(k, carry):
            for c in Y_SENT:
                sigma[c, 2 + k, first : first + 8, :] = zero
            for c in range(3):
                vel[c, 2 + k, first : first + 8, :] = zero
            return carry

        lax.fori_loop(0, NZ, layer, 0)
        for m in range(6):
            terrain[m, first : first + 8, :] = jnp.zeros((8, 32), jnp.int32)

    def zero_x(side, slot):
        halo_s[side] = jnp.zeros((2, NY, NX), jnp.float32)
        halo_v[side] = jnp.zeros((2, NY, NX), jnp.float32)
        terrain[slot, 8:40, :] = jnp.zeros((32, 32), jnp.int32)

    when(z == 0, lambda: zero_z(0))
    when(z == GZ - 1, lambda: zero_z(18))
    when(y == 0, lambda: zero_y(0))
    when(y == GY - 1, lambda: zero_y(40))
    when(x == 0, lambda: zero_x(0, 0))
    when(x == GX - 1, lambda: zero_x(1, 5))

    elevation_in.wait()
    for d in range(1, GZ):
        g = (z + d) % GZ
        arrived(terrain.at[1 + g, 8:40, :], t_recv.at[1 + g])
    when(x_low, lambda: arrived(terrain.at[0, 8:40, :], t_recv.at[0]))
    when(x_high, lambda: arrived(terrain.at[5, 8:40, :], t_recv.at[5]))
    edge_up = send(y_high, remote(terrain.at[:, 32:40, :], terrain.at[:, 0:8, :], edge_send.at[0], edge_recv.at[0], up_y), now=False)
    when(y_high & ~before_gap, edge_up.start)
    send(y_low, remote(terrain.at[:, 8:16, :], terrain.at[:, 40:48, :], edge_send.at[1], edge_recv.at[1], down_y))

    def heights(row):
        rows = pl.ds(row, 8)
        held = [terrain[m, rows, :].astype(jnp.float32) / 200.0 for m in range(6)]
        blank = jnp.zeros((8, 96), jnp.float32)
        wide[0, rows, :] = jnp.concatenate([blank, held[0]], axis=1)
        wide[1, rows, :] = jnp.concatenate(held[1:5], axis=1)
        wide[2, rows, :] = jnp.concatenate([held[5], blank], axis=1)

    binomial = (1.0, 4.0, 6.0, 4.0, 1.0)

    def metrics(first, rows):
        along_y = []
        for part in range(3):
            total = jnp.zeros((rows + 8, NX), jnp.float32)
            for d, factor in enumerate(binomial):
                total = total + factor * wide[part, pl.ds(first + 2 + d, rows + 8), :]
            along_y.append(total / 16.0)
        row = jnp.concatenate(along_y, axis=1)
        total = jnp.zeros_like(row)
        for d, factor in enumerate(binomial):
            total = total + factor * (row if d == 2 else pltpu.roll(row, (2 - d) % 384, 1))
        total = total / 16.0
        for part in range(3):
            surf[part, 0 : rows + 8, :] = total[:, 128 * part : 128 * part + 128]
        own = jnp.concatenate([surf[part, 4 : 4 + rows, :] for part in range(3)], axis=1)
        height = own[:, 128:256]
        shifted = [pltpu.roll(own, d % 384, 1)[:, 128:256] for d in (2, 1, -1, -2)]
        slope_x = centred_12(*shifted) / 12.0
        slope_y = centred_12(*[surf[1, 4 + d : 4 + d + rows, :] for d in (-2, -1, 1, 2)]) / 12.0

        def above(step, total):
            for layer in [4 * step + i for i in range(4)]:
                base, follow = layers[0, pl.ds(layer, 1), :], layers[1, pl.ds(layer, 1), :]
                total = total + follow * (base * jnp.exp(follow * height))
            return total

        upper = lax.fori_loop(0, (NZ // 4) * z, above, jnp.zeros((rows, NX), jnp.float32))

        def layer(step, total):
            for k in [4 * step + i for i in range(4)]:
                base, follow = layers[0, pl.ds(NZ * z + k, 1), :], layers[1, pl.ds(NZ * z + k, 1), :]
                thickness = base * jnp.exp(follow * height)
                weighted = follow * thickness
                inverse = 1.0 / thickness
                factor = (total + 0.5 * weighted - 1.0) * inverse
                at = pl.ds(first, rows)
                metric[0, k, at, :] = slope_x * factor
                metric[1, k, at, :] = slope_y * factor
                metric[2, k, at, :] = inverse
                total = total + weighted
            return total

        lax.fori_loop(0, NZ // 4, layer, upper)

    def d_k(field, c, k, first, rows):
        return centred_12(*[field[c, k + 2 + d, pl.ds(8 + first, rows), :] for d in (-2, -1, 1, 2)])

    def d_y(field, c, k, first, rows):
        return centred_12(*[field[c, k + 2, pl.ds(8 + first + d, rows), :] for d in (-2, -1, 1, 2)])

    def d_x(c, k, first, rows, halo, i):
        side = lax.broadcasted_iota(jnp.int32, (rows, NX), 1)
        at = 4 * (k + (NZ if i == 1 else 0))
        fix = pltpu.roll(halo[0, i // 2, pl.ds(first, rows), :], 126 - at, 1)
        return along[i, k, pl.ds(first, rows), :] + jnp.where((side < 2) | (side >= 126), fix, 0.0)

    def join(halo, first, rows):
        spot = lax.broadcasted_iota(jnp.int32, (rows, NX), 1) % 4
        at = pl.ds(first, rows)
        for i in range(2):
            change = jnp.where(spot < 2, halo[0, i, at, :], halo[1, i, at, :])
            low = 8.0 * jnp.where(spot == 1, pltpu.roll(change, 127, 1), 0.0) - pltpu.roll(change, 126, 1)
            high = pltpu.roll(change, 2, 1) - 8.0 * jnp.where(spot == 2, pltpu.roll(change, 1, 1), 0.0)
            halo[0, i, at, :] = jnp.where(spot < 2, low, high)

    def velocity_rows(first, rows, unroll):
        blocks = rows // 8

        def velocity_layer(step, carried):
            held, last = list(carried[0]), carried[1]
            at = pl.ds(first, rows)
            ks = [unroll * step + i for i in range(unroll)]
            pack_rows(held, [k - unroll for k in ks], last)
            made = []
            for k in ks:
                m_x, m_y, m_z = (metric[i, k, at, :] for i in range(3))
                grad_k = [d_k(sigma, c, k, first, rows) for c in range(6)]
                grad_x = [d_x(c, k, first, rows, halo_s, i) for i, c in enumerate(X_PARTS)]
                grad_y = [d_y(sigma, c, k, first, rows) for c in Y_PARTS]
                scale = props[0, k, at, :]
                row = []
                for c, (a, b, d) in enumerate(((0, 3, 4), (3, 1, 5), (4, 5, 2))):
                    accel = (grad_x[c] - m_x * grad_k[a]) + (grad_y[c] - m_y * grad_k[b]) + m_z * grad_k[d]
                    new = v_out[c, k, at, :] + scale * accel
                    v_out[c, k, at, :] = new
                    vel[c, 2 + k, pl.ds(8 + first, rows), :] = new
                    row.append(new)
                made.append(row)
            return tuple(held), made

        def pack_rows(held, ks, made):
            for k, row in zip(ks, made):
                for c in range(3):
                    spot_at, spot = pack_spot(k, c)
                    pack_layer(held, [row[c][8 * r : 8 * r + 8] for r in range(blocks)], c, k, spot_at, spot)

        nothing = jnp.zeros((rows, NX), jnp.float32)
        start = ((zero,) * (2 * blocks), [[nothing] * 3 for _ in range(unroll)])
        held, last = lax.fori_loop(0, NZ // unroll, velocity_layer, start)
        held = list(held)
        pack_rows(held, range(NZ - unroll, NZ), last)
        for j in range(2 * blocks):
            packs[1, j // blocks, pl.ds(first + 8 * (j % blocks), 8), :] = held[j]

    def send_rows(part, first, rows):
        at = pl.ds(first, rows)
        send(x_high, remote(packs.at[1, :, at, :], halo_v.at[0, :, at, :], x_send.at[0, part], x_recv.at[0, part], {"gx": x + 1}))
        send(x_low, remote(packs.at[1, :, at, :], halo_v.at[1, :, at, :], x_send.at[1, part], x_recv.at[1, part], {"gx": x - 1}))
        at = pl.ds(8 + first, rows)
        send(z_high, remote(vel.at[:, 16:18, at, :], vel.at[:, 0:2, at, :], z_send.at[0, part], z_recv.at[0, part], {"gz": z + 1}))
        send(z_low, remote(vel.at[:, 2:4, at, :], vel.at[:, 18:20, at, :], z_send.at[1, part], z_recv.at[1, part], {"gz": z - 1}))

    def wait_x(part, first, rows):
        at = pl.ds(first, rows)
        when(x_low, lambda: arrived(halo_v.at[0, :, at, :], x_recv.at[0, part]))
        when(x_high, lambda: arrived(halo_v.at[1, :, at, :], x_recv.at[1, part]))
        join(halo_v, first, rows)

    def wait_z(part, first, rows):
        at = pl.ds(8 + first, rows)
        when(z_low, lambda: arrived(vel.at[:, 0:2, at, :], z_recv.at[0, part]))
        when(z_high, lambda: arrived(vel.at[:, 18:20, at, :], z_recv.at[1, part]))

    for row in range(8, 40, 8):
        heights(row)
    for d in range(1, GZ):
        g = (z + d) % GZ
        arrived(layers.at[:, pl.ds(NZ * g, NZ), :], layer_recv.at[g])
    metrics(8, 16)

    def start_far():
        pl.semaphore_wait(far_sem, 1)
        edge_up.start()
        start_up()

    when(before_gap, start_far)
    for copy in (stress_in[1], stress_in[2], stress_in[5], velocity_in):
        copy.wait()
    when(x_low, lambda: arrived(halo_s.at[0], s_recv.at[0]))
    when(x_high, lambda: arrived(halo_s.at[1], s_recv.at[1]))
    join(halo_s, 0, NY)
    def wait_stress_z(part, condition):
        _, first, rows = z_parts[part]
        to = pl.ds(8 + first, rows)
        when(condition & z_low, lambda: arrived(sigma.at[:, 0:2, to, :], zs_recv.at[0, part]))
        when(condition & z_high, lambda: arrived(sigma.at[:, 18:20, to, :], zs_recv.at[1, part]))

    gap_copy = remote(gap_out, gap_in, gap_sem.at[0], gap_sem.at[1], down_y)
    sends.append((after_gap, gap_copy))

    def gap_package():
        top = lax.broadcasted_iota(jnp.int32, (8, NX), 0) == 0

        def layers_of(step, carry):
            for k in (2 * step, 2 * step + 1):
                scale = props[0, k, 0:8, :]
                for c in range(6):
                    gap_out[3 + c, k] = (scale * d_k(sigma, c, k, 0, 8))[0:2]
                gap_out[9, k] = scale[0:2]
                for i, (c_x, c_y) in enumerate(zip(X_PARTS, Y_PARTS)):
                    here, after_1, after_2 = (sigma[c_y, k + 2, 8 + d : 16 + d, :] for d in range(3))
                    before_1 = jnp.where(top, 0.0, pltpu.roll(here, 1, 0))
                    grad_y = 8.0 * (after_1 - before_1) - after_2
                    known = v_out[i, k, 0:8, :] + scale * (d_x(c_x, k, 0, 8, halo_s, i) + grad_y)
                    gap_out[i, k] = known[0:2]
            return carry

        lax.fori_loop(0, NZ // 2, layers_of, 0)
        gap_copy.start()

    def gap_velocity():
        arrived(gap_in, gap_sem.at[1])

        def layers_of(step, carry):
            for k in (2 * step, 2 * step + 1):
                m_x, m_y, m_z = (metric[i, k, NY : NY + 2, :] for i in range(3))
                for i, (a, b, d) in enumerate(((0, 3, 4), (3, 1, 5), (4, 5, 2))):
                    edge = sigma[Y_PARTS[i], k + 2, 38:40, :]
                    beyond = jnp.concatenate([edge[0:1] - 8.0 * edge[1:2], edge[1:2]], axis=0)
                    known = gap_in[i, k] + gap_in[9, k] * beyond
                    vel[i, 2 + k, 40:42, :] = known - m_x * gap_in[3 + a, k] - m_y * gap_in[3 + b, k] + m_z * gap_in[3 + d, k]
            return carry

        lax.fori_loop(0, NZ // 2, layers_of, 0)

    def gap_metrics():
        for part in range(3):
            wide[part, 48:64, :] = jnp.zeros((16, NX), jnp.float32)
        metrics(NY, 8)

    wait_stress_z(2, after_gap)
    when(after_gap, gap_package)
    wait_stress_z(0, z >= 0)
    velocity_rows(8, 16, 2)
    send_rows(0, 8, 16)

    low_copy = remote(vel.at[:, 2:18, 8:10, :], vel.at[:, 2:18, 40:42, :], vy_send.at[1], vy_recv.at[1], down_y)
    high_copy = remote(vel.at[:, 2:18, 38:40, :], vel.at[:, 2:18, 6:8, :], vy_send.at[0], vy_recv.at[0], up_y)
    sends.append((y_low & ~after_gap, low_copy))
    sends.append((y_high, high_copy))
    for part, low, first, outer in strips:
        when(low & y_low, lambda: arrived(terrain.at[:, 0:8, :], edge_recv.at[0]))
        when(~low & y_high, lambda: arrived(terrain.at[:, 40:48, :], edge_recv.at[1]))
        heights(outer)
        metrics(first, 8)
        for i, c in enumerate(Y_SENT):
            when(low & y_low, lambda: arrived(sigma.at[c, 2:18, 6:8, :], y_recv.at[0, i]))
            when(~low & y_high, lambda: arrived(sigma.at[c, 2:18, 40:42, :], y_recv.at[1, i]))
        wait_stress_z(part, (z >= 0) if part == 1 else ~after_gap)
        velocity_rows(first, 8, 4)
        when(low & y_low & ~after_gap, low_copy.start)
        when(~low & y_high, high_copy.start)
        send_rows(part, first, 8)
        if part == 1:
            differentiate_x(range(3), vel, 8, 16, 4)
        differentiate_x(range(3), vel, first, 8, 8)
    when(before_gap, gap_metrics)

    memory_in.wait()

    def stress_rows(first, rows, unroll, steps, stride=1):
        at = pl.ds(first, rows)

        def stress_layer(step, carry):
            for k in [unroll * stride * step + i for i in range(unroll)]:
                grad_x = [d_x(c, k, first, rows, halo_v, c) for c in range(3)]
                m_x, m_y, m_z = (metric[i, k, at, :] for i in range(3))
                along_k = [d_k(vel, c, k, first, rows) for c in range(3)]
                along_x = [grad_x[c] - m_x * along_k[c] for c in range(3)]
                along_y = [d_y(vel, c, k, first, rows) - m_y * along_k[c] for c in range(3)]
                along_z = [m_z * along_k[c] for c in range(3)]
                lam, mu, kept, gain = (props[i, k, at, :] for i in range(1, 5))
                volume = lam * (along_x[0] + along_y[1] + along_z[2])
                twice = mu + mu
                rates = (
                    volume + twice * along_x[0],
                    volume + twice * along_y[1],
                    volume + twice * along_z[2],
                    mu * (along_y[0] + along_x[1]),
                    mu * (along_z[0] + along_x[2]),
                    mu * (along_z[1] + along_y[2]),
                )
                for c, rate in enumerate(rates):
                    new = kept * m_out[c, k, at, :] + gain * rate
                    m_out[c, k, at, :] = new
                    s_out[c, k, at, :] = sigma[c, 2 + k, pl.ds(8 + first, rows), :] + STEP * (rate - new)
            return carry

        lax.fori_loop(steps[0], steps[1], stress_layer, 0)

    wait_x(0, 8, 16)
    stress_rows(8, 16, 2, (1, NZ // 2 - 1))
    wait_z(0, 8, 16)
    stress_rows(8, 16, 2, (0, 2), NZ // 2 - 1)
    for part, low, first, outer in strips:
        wait_x(part, first, 8)
        wait_z(part, first, 8)
        when(low & y_low, lambda: arrived(vel.at[:, 2:18, 6:8, :], vy_recv.at[0]))
        when(~low & y_high & ~before_gap, lambda: arrived(vel.at[:, 2:18, 40:42, :], vy_recv.at[1]))
        if part == 2:
            when(before_gap, gap_velocity)
        stress_rows(first, 8, 4, (0, NZ // 4))
    for condition, copy in sends:
        when(condition, copy.wait_send)


def write_out(v_in, s_in, m_in, v_ref, s_ref, m_ref, sems):
    pairs = [(v_in, v_ref, c) for c in range(3)] + [(a, b, c) for a, b in ((s_in, s_ref), (m_in, m_ref)) for c in range(6)]
    copies = [pltpu.make_async_copy(a.at[c], b.at[c], sems.at[i]) for i, (a, b, c) in enumerate(pairs)]
    for copy in copies:
        copy.start()
    for copy in copies:
        copy.wait()


def local(*arrays):
    held = [pltpu.with_memory_space_constraint(array, pltpu.HBM) for array in arrays]
    f32, vmem, dma = jnp.float32, pltpu.VMEM, pltpu.SemaphoreType.DMA
    outputs = [(n, NZ, NY, NX) for n in (3, 6, 6)]
    results = pl.pallas_call(
        kernel,
        out_shape=tuple(vmem(shape, f32) for shape in outputs),
        in_specs=[pl.BlockSpec(memory_space=pltpu.HBM)] * len(held),
        out_specs=tuple(pl.BlockSpec(memory_space=vmem) for _ in outputs),
        scratch_shapes=[
            vmem((6, 20, 48, NX), f32),
            vmem((3, 20, 48, NX), f32),
            vmem((6, 48, 32), jnp.int32),
            vmem((3, 64, NX), f32),
            vmem((3, 24, NX), f32),
            vmem((2, GZ * NZ, NX), f32),
            vmem((NZ, NY, NX), jnp.int32),
            vmem((5, 8, NX), f32),
            vmem((5, NZ, NY, NX), f32),
            vmem((NX, NX), jnp.bfloat16),
            vmem((3, NZ, NY, NX), f32),
            vmem((3, NZ, NY + 8, NX), f32),
            vmem((2, 2, NY, NX), f32),
            vmem((2, 2, NY, NX), f32),
            vmem((2, 2, NY, NX), f32),
            pltpu.SMEM((7, 16), f32),
            dma((17,)), dma((4,)), dma((4,)), dma((2, 3)), dma((2, 3)), dma((3,)), dma((4,)), dma((7,)), dma((6,)), dma((2,)), dma((2,)),
            dma((2, 3)), dma((2, 3)), dma((2, 3)), dma((2, 3)), dma((2,)), dma((2,)),
            dma((2, 3)), dma((2, 3)),
            vmem((10, NZ, 2, NX), f32),
            vmem((10, NZ, 2, NX), f32),
            dma((2,)),
            pltpu.SemaphoreType.REGULAR,
        ],
        compiler_params=pltpu.CompilerParams(
            collective_id=0, has_side_effects=True, vmem_limit_bytes=24 << 20
        ),
    )(*held)
    return pl.pallas_call(
        write_out,
        out_shape=tuple(jax.ShapeDtypeStruct(shape, f32) for shape in outputs),
        in_specs=[pl.BlockSpec(memory_space=vmem)] * 3,
        out_specs=tuple(pl.BlockSpec(memory_space=pltpu.HBM) for _ in outputs),
        scratch_shapes=[dma((15,))],
        compiler_params=pltpu.CompilerParams(vmem_limit_bytes=8 << 20),
    )(*results)


def solution(mesh):
    field = P(None, "gz", "gy", "gx")
    return jax.shard_map(
        local,
        mesh=mesh,
        in_specs=(
            P("gy", ("gx", "gz")), P("gz"), P("gz"), P("gz", "gy", "gx"),
            P(), P(), P(), P(), P(), field, field, field,
        ),
        out_specs=(field, field, field),
        check_vma=False,
    )
```

```python
import functools

import jax
import jax.numpy as jnp
from jax import lax
from jax.experimental import pallas as pl
from jax.experimental.pallas import tpu as pltpu
from jax.sharding import PartitionSpec as P

MESH = pl.DeviceIdType.MESH
STEP = 0.3
GX, GY, GZ = 4, 16, 4
NZ, NY, NX = 16, 32, 128
X_PARTS = (0, 3, 4)
Y_PARTS = (3, 1, 5)
Y_SENT = (1, 3, 5)


def when(condition, action):
    if condition is None:
        action()
    else:
        pl.when(condition)(lambda: action())


def centred_12(before_2, before_1, after_1, after_2):
    return 8.0 * (after_1 - before_1) - (after_2 - before_2)


def kernel(
    elevation, layer_base, stretch, material, buoyancy, lame, shear, relax, weight, velocity, stress, memory,
    v_out, s_out, m_out,
    sigma, vel, terrain, wide, surf, layers, mat, tables, props, stencil, along, metric, packs, halo_s, halo_v,
    small, local_sem, s_send, s_recv, y_send, y_recv, layer_send, layer_recv, t_send, t_recv, edge_send, edge_recv,
    z_send, z_recv, x_send, x_recv, vy_send, vy_recv, zs_send, zs_recv, gap_out, gap_in, gap_sem, far_sem,
):
    x, y, z = lax.axis_index("gx"), lax.axis_index("gy"), lax.axis_index("gz")
    x_low, x_high = x > 0, x < GX - 1
    y_low, y_high = y > 0, y < GY - 1
    z_low, z_high = z > 0, z < GZ - 1
    before_gap, after_gap = y == GY // 2 - 1, y == GY // 2
    lane = lax.broadcasted_iota(jnp.int32, (8, NX), 1)

    own_slot = 1 + z
    tables_in = (buoyancy, lame, shear, relax, weight, layer_base, stretch)
    scalars = [pltpu.make_async_copy(ref, small.at[i], local_sem.at[i]) for i, ref in enumerate(tables_in)]
    for copy in scalars:
        copy.start()
    stress_in = {
        c: pltpu.make_async_copy(stress.at[c], sigma.at[c, 2:18, 8:40, :], local_sem.at[7 + c])
        for c in (0, 3, 4, 1, 2, 5)
    }
    for c in (0, 3, 4):
        stress_in[c].start()
    material_in = pltpu.make_async_copy(material, mat, local_sem.at[15])
    material_in.start()
    for c in (1, 2, 5):
        stress_in[c].start()
    elevation_in = pltpu.make_async_copy(elevation, terrain.at[own_slot, 8:40, :], local_sem.at[13])
    velocity_in = pltpu.make_async_copy(velocity, v_out, local_sem.at[14])
    memory_in = pltpu.make_async_copy(memory, m_out, local_sem.at[16])
    for copy in (elevation_in, velocity_in, memory_in):
        copy.start()

    barrier = pltpu.get_barrier_semaphore()
    beside = [(None, {"gz": (z + d) % GZ}) for d in range(1, GZ)]
    for g in range(GZ):
        beside.append((x_high & ((z == g) | (z == GZ - 1) | (g == 0)), {"gx": x + 1, "gz": g}))
        beside.append((x_low & ((z == g) | (z == 0) | (g == GZ - 1)), {"gx": x - 1, "gz": g}))
    up_y, down_y = {"gy": y + 1}, {"gy": y - 1}
    for condition, target in [(y_high, up_y), (y_low & ~after_gap, down_y)] + beside:
        when(condition, lambda target=target: pl.semaphore_signal(barrier, inc=1, device_id=target, device_id_type=MESH))
    expected = [y_low, y_high & ~before_gap] + [condition for condition, _ in beside]

    pl.semaphore_wait(barrier, sum(1 if c is None else c.astype(jnp.int32) for c in expected))
    when(after_gap, lambda: pl.semaphore_signal(far_sem, inc=1, device_id=down_y, device_id_type=MESH))

    def remote(source, to, send, recv, target):
        return pltpu.make_async_remote_copy(
            src_ref=source, dst_ref=to, send_sem=send, recv_sem=recv, device_id=target, device_id_type=MESH
        )

    sends = []

    def send(condition, copy, now=True):
        sends.append((condition, copy))
        if now:
            when(condition, copy.start)
        return copy

    for d in range(1, GZ):
        send(None, remote(elevation, terrain.at[own_slot, 8:40, :], t_send.at[d - 1], t_recv.at[own_slot], {"gz": (z + d) % GZ}))
    for g in range(GZ):
        send(x_high & (z == GZ - 1), remote(elevation, terrain.at[0, 8:40, :], t_send.at[3 + g], t_recv.at[0], {"gx": x + 1, "gz": g}))
        send(x_low & (z == 0), remote(elevation, terrain.at[5, 8:40, :], t_send.at[3 + g], t_recv.at[5], {"gx": x - 1, "gz": g}))
    up_copies = [
        send(y_high, remote(stress.at[c, :, 30:32, :], sigma.at[c, 2:18, 6:8, :], y_send.at[0, i], y_recv.at[0, i], up_y), now=False)
        for i, c in enumerate(Y_SENT)
    ]

    def start_up():
        for copy in up_copies:
            copy.start()

    when(y_high & ~before_gap, start_up)
    for i, c in enumerate(Y_SENT):
        send(y_low, remote(stress.at[c, :, 0:2, :], sigma.at[c, 2:18, 40:42, :], y_send.at[1, i], y_recv.at[1, i], down_y))
    odd = y % 2
    strips = []
    for part in (1, 2):
        low = (odd == 1) if part == 1 else (odd == 0)
        side = odd if part == 1 else 1 - odd
        strips.append((part, low, pl.multiple_of(24 - 24 * side, 8), pl.multiple_of(40 - 40 * side, 8)))
    z_parts = [(0, 8, 16)] + [(part, first, 8) for part, _, first, _ in strips]
    z_copies = []
    for part, first, rows in z_parts:
        at, to = pl.ds(first, rows), pl.ds(8 + first, rows)
        z_copies.append((
            send(z_high, remote(stress.at[:, 14:16, at, :], sigma.at[:, 0:2, to, :], zs_send.at[0, part], zs_recv.at[0, part], {"gz": z + 1}), now=False),
            send(z_low, remote(stress.at[:, 0:2, at, :], sigma.at[:, 18:20, to, :], zs_send.at[1, part], zs_recv.at[1, part], {"gz": z - 1}), now=False),
        ))

    def start_z(part, condition):
        when(z_high if condition is None else condition & z_high, z_copies[part][0].start)
        when(z_low if condition is None else condition & z_low, z_copies[part][1].start)

    start_z(2, after_gap)
    start_z(0, None)
    start_z(1, None)
    start_z(2, ~after_gap)

    zero = jnp.zeros((8, NX), jnp.float32)

    def pack_spot(k, i):
        at = 4 * (k + (NZ if i == 1 else 0))
        return at, (lane >= at) & (lane < at + 4)

    def pack_layer(held, blocks, i, k, at, spot):
        for r, block in enumerate(blocks):
            j = len(blocks) * (i // 2) + r
            held[j] = jnp.where(spot, pltpu.roll(block, at + 2, 1), held[j])

    def pack_stress(step, held):
        held = list(held)
        for k in (2 * step, 2 * step + 1):
            for i, c in enumerate(X_PARTS):
                at, spot = pack_spot(k, i)
                pack_layer(held, [sigma[c, 2 + k, 8 + 8 * r : 16 + 8 * r, :] for r in range(4)], i, k, at, spot)
        return tuple(held)

    for copy in scalars:
        copy.wait()
    for k in range(NZ):
        for row in range(2):
            layers[row, pl.ds(NZ * z + k, 1), :] = jnp.full((1, NX), small[5 + row, k], jnp.float32)

    for c in X_PARTS:
        stress_in[c].wait()
    held = lax.fori_loop(0, NZ // 2, pack_stress, (zero,) * 8)
    for j in range(8):
        packs[0, j // 4, 8 * (j % 4) : 8 * (j % 4) + 8, :] = held[j]

    mine = pl.ds(NZ * z, NZ)
    for d in range(1, GZ):
        send(None, remote(layers.at[:, mine, :], layers.at[:, mine, :], layer_send.at[d - 1], layer_recv.at[z], {"gz": (z + d) % GZ}))
    columns = []
    for i in range(5):
        column = zero
        for block_id in range(16):
            column = jnp.where(lane == block_id, small[i, block_id], column)
        columns.append(column)
    keep = jnp.exp(-STEP / jnp.where(lane < 16, columns[3], 1.0))
    tables[0] = columns[0] * (STEP / 12.0)
    tables[1] = columns[1] * (1.0 / 12.0)
    tables[2] = columns[2] * (1.0 / 12.0)
    tables[3] = keep
    tables[4] = (1.0 - keep) * columns[4]

    send(x_high, remote(packs.at[0], halo_s.at[0], s_send.at[0], s_recv.at[0], {"gx": x + 1}))
    send(x_low, remote(packs.at[0], halo_s.at[1], s_send.at[1], s_recv.at[1], {"gx": x - 1}))
    material_in.wait()

    def property_layer(k, carry):
        for r in range(4):
            rows = slice(8 * r, 8 * r + 8)
            block_id = mat[k, rows, :]
            for i in range(5):
                props[i, k, rows, :] = jnp.take_along_axis(tables[i], block_id, axis=1)
        return carry

    lax.fori_loop(0, NZ, property_layer, 0)

    offset = lax.broadcasted_iota(jnp.int32, (NX, NX), 0) - lax.broadcasted_iota(jnp.int32, (NX, NX), 1)
    weights = jnp.zeros((NX, NX), jnp.float32)
    for distance, factor in ((-2, 1.0), (-1, -8.0), (1, 8.0), (2, -1.0)):
        weights = jnp.where(offset == distance, factor, weights)
    stencil[...] = weights.astype(jnp.bfloat16)

    def differentiate_x(parts, field, first, rows, unroll):
        def layers_of(step, carry):
            spots = [(i, c, unroll * step + n) for i, c in enumerate(parts) for n in range(unroll)]
            rest = jnp.concatenate([field[c, k + 2, pl.ds(8 + first, rows), :] for _, c, k in spots], axis=0)
            total = None
            for _ in range(3):
                piece = rest.astype(jnp.bfloat16)
                rest = rest - piece.astype(jnp.float32)
                product = jnp.dot(piece, stencil[...], preferred_element_type=jnp.float32)
                total = product if total is None else total + product
            for n, (i, _, k) in enumerate(spots):
                along[i, k, pl.ds(first, rows), :] = total[n * rows : (n + 1) * rows]
            return carry

        lax.fori_loop(0, NZ // unroll, layers_of, 0)

    differentiate_x(X_PARTS, sigma, 0, NY, 4)

    def arrived(ref, recv):
        remote(ref, ref, s_send.at[0], recv, {"gz": z}).wait_recv()

    def zero_z(first):
        sigma[:, pl.ds(first, 2), 8:40, :] = jnp.zeros((6, 2, NY, NX), jnp.float32)
        vel[:, pl.ds(first, 2), 8:40, :] = jnp.zeros((3, 2, NY, NX), jnp.float32)

    def zero_y(first):
        def layer(k, carry):
            for c in Y_SENT:
                sigma[c, 2 + k, first : first + 8, :] = zero
            for c in range(3):
                vel[c, 2 + k, first : first + 8, :] = zero
            return carry

        lax.fori_loop(0, NZ, layer, 0)
        for m in range(6):
            terrain[m, first : first + 8, :] = jnp.zeros((8, 32), jnp.int32)

    def zero_x(side, slot):
        halo_s[side] = jnp.zeros((2, NY, NX), jnp.float32)
        halo_v[side] = jnp.zeros((2, NY, NX), jnp.float32)
        terrain[slot, 8:40, :] = jnp.zeros((32, 32), jnp.int32)

    when(z == 0, lambda: zero_z(0))
    when(z == GZ - 1, lambda: zero_z(18))
    when(y == 0, lambda: zero_y(0))
    when(y == GY - 1, lambda: zero_y(40))
    when(x == 0, lambda: zero_x(0, 0))
    when(x == GX - 1, lambda: zero_x(1, 5))

    elevation_in.wait()
    for d in range(1, GZ):
        g = (z + d) % GZ
        arrived(terrain.at[1 + g, 8:40, :], t_recv.at[1 + g])
    when(x_low, lambda: arrived(terrain.at[0, 8:40, :], t_recv.at[0]))
    when(x_high, lambda: arrived(terrain.at[5, 8:40, :], t_recv.at[5]))
    edge_up = send(y_high, remote(terrain.at[:, 32:40, :], terrain.at[:, 0:8, :], edge_send.at[0], edge_recv.at[0], up_y), now=False)
    when(y_high & ~before_gap, edge_up.start)
    send(y_low, remote(terrain.at[:, 8:16, :], terrain.at[:, 40:48, :], edge_send.at[1], edge_recv.at[1], down_y))

    def heights(row):
        rows = pl.ds(row, 8)
        held = [terrain[m, rows, :].astype(jnp.float32) / 200.0 for m in range(6)]
        blank = jnp.zeros((8, 96), jnp.float32)
        wide[0, rows, :] = jnp.concatenate([blank, held[0]], axis=1)
        wide[1, rows, :] = jnp.concatenate(held[1:5], axis=1)
        wide[2, rows, :] = jnp.concatenate([held[5], blank], axis=1)

    binomial = (1.0, 4.0, 6.0, 4.0, 1.0)

    def metrics(first, rows):
        along_y = []
        for part in range(3):
            total = jnp.zeros((rows + 8, NX), jnp.float32)
            for d, factor in enumerate(binomial):
                total = total + factor * wide[part, pl.ds(first + 2 + d, rows + 8), :]
            along_y.append(total / 16.0)
        row = jnp.concatenate(along_y, axis=1)
        total = jnp.zeros_like(row)
        for d, factor in enumerate(binomial):
            total = total + factor * (row if d == 2 else pltpu.roll(row, (2 - d) % 384, 1))
        total = total / 16.0
        for part in range(3):
            surf[part, 0 : rows + 8, :] = total[:, 128 * part : 128 * part + 128]
        own = jnp.concatenate([surf[part, 4 : 4 + rows, :] for part in range(3)], axis=1)
        height = own[:, 128:256]
        shifted = [pltpu.roll(own, d % 384, 1)[:, 128:256] for d in (2, 1, -1, -2)]
        slope_x = centred_12(*shifted) / 12.0
        slope_y = centred_12(*[surf[1, 4 + d : 4 + d + rows, :] for d in (-2, -1, 1, 2)]) / 12.0

        def above(step, total):
            for layer in [4 * step + i for i in range(4)]:
                base, follow = layers[0, pl.ds(layer, 1), :], layers[1, pl.ds(layer, 1), :]
                total = total + follow * (base * jnp.exp(follow * height))
            return total

        upper = lax.fori_loop(0, (NZ // 4) * z, above, jnp.zeros((rows, NX), jnp.float32))

        def layer(step, total):
            for k in [4 * step + i for i in range(4)]:
                base, follow = layers[0, pl.ds(NZ * z + k, 1), :], layers[1, pl.ds(NZ * z + k, 1), :]
                thickness = base * jnp.exp(follow * height)
                weighted = follow * thickness
                inverse = 1.0 / thickness
                factor = (total + 0.5 * weighted - 1.0) * inverse
                at = pl.ds(first, rows)
                metric[0, k, at, :] = slope_x * factor
                metric[1, k, at, :] = slope_y * factor
                metric[2, k, at, :] = inverse
                total = total + weighted
            return total

        lax.fori_loop(0, NZ // 4, layer, upper)

    def d_k(field, c, k, first, rows):
        return centred_12(*[field[c, k + 2 + d, pl.ds(8 + first, rows), :] for d in (-2, -1, 1, 2)])

    def d_y(field, c, k, first, rows):
        return centred_12(*[field[c, k + 2, pl.ds(8 + first + d, rows), :] for d in (-2, -1, 1, 2)])

    def d_x(c, k, first, rows, halo, i):
        side = lax.broadcasted_iota(jnp.int32, (rows, NX), 1)
        at = 4 * (k + (NZ if i == 1 else 0))
        fix = pltpu.roll(halo[0, i // 2, pl.ds(first, rows), :], 126 - at, 1)
        return along[i, k, pl.ds(first, rows), :] + jnp.where((side < 2) | (side >= 126), fix, 0.0)

    def join(halo, first, rows):
        spot = lax.broadcasted_iota(jnp.int32, (rows, NX), 1) % 4
        at = pl.ds(first, rows)
        for i in range(2):
            change = jnp.where(spot < 2, halo[0, i, at, :], halo[1, i, at, :])
            low = 8.0 * jnp.where(spot == 1, pltpu.roll(change, 127, 1), 0.0) - pltpu.roll(change, 126, 1)
            high = pltpu.roll(change, 2, 1) - 8.0 * jnp.where(spot == 2, pltpu.roll(change, 1, 1), 0.0)
            halo[0, i, at, :] = jnp.where(spot < 2, low, high)

    def velocity_rows(first, rows, unroll):
        blocks = rows // 8

        def velocity_layer(step, carried):
            held, last = list(carried[0]), carried[1]
            at = pl.ds(first, rows)
            ks = [unroll * step + i for i in range(unroll)]
            pack_rows(held, [k - unroll for k in ks], last)
            made = []
            for k in ks:
                m_x, m_y, m_z = (metric[i, k, at, :] for i in range(3))
                grad_k = [d_k(sigma, c, k, first, rows) for c in range(6)]
                grad_x = [d_x(c, k, first, rows, halo_s, i) for i, c in enumerate(X_PARTS)]
                grad_y = [d_y(sigma, c, k, first, rows) for c in Y_PARTS]
                scale = props[0, k, at, :]
                row = []
                for c, (a, b, d) in enumerate(((0, 3, 4), (3, 1, 5), (4, 5, 2))):
                    accel = (grad_x[c] - m_x * grad_k[a]) + (grad_y[c] - m_y * grad_k[b]) + m_z * grad_k[d]
                    new = v_out[c, k, at, :] + scale * accel
                    v_out[c, k, at, :] = new
                    vel[c, 2 + k, pl.ds(8 + first, rows), :] = new
                    row.append(new)
                made.append(row)
            return tuple(held), made

        def pack_rows(held, ks, made):
            for k, row in zip(ks, made):
                for c in range(3):
                    spot_at, spot = pack_spot(k, c)
                    pack_layer(held, [row[c][8 * r : 8 * r + 8] for r in range(blocks)], c, k, spot_at, spot)

        nothing = jnp.zeros((rows, NX), jnp.float32)
        start = ((zero,) * (2 * blocks), [[nothing] * 3 for _ in range(unroll)])
        held, last = lax.fori_loop(0, NZ // unroll, velocity_layer, start)
        held = list(held)
        pack_rows(held, range(NZ - unroll, NZ), last)
        for j in range(2 * blocks):
            packs[1, j // blocks, pl.ds(first + 8 * (j % blocks), 8), :] = held[j]

    def send_rows(part, first, rows):
        at = pl.ds(first, rows)
        send(x_high, remote(packs.at[1, :, at, :], halo_v.at[0, :, at, :], x_send.at[0, part], x_recv.at[0, part], {"gx": x + 1}))
        send(x_low, remote(packs.at[1, :, at, :], halo_v.at[1, :, at, :], x_send.at[1, part], x_recv.at[1, part], {"gx": x - 1}))
        at = pl.ds(8 + first, rows)
        send(z_high, remote(vel.at[:, 16:18, at, :], vel.at[:, 0:2, at, :], z_send.at[0, part], z_recv.at[0, part], {"gz": z + 1}))
        send(z_low, remote(vel.at[:, 2:4, at, :], vel.at[:, 18:20, at, :], z_send.at[1, part], z_recv.at[1, part], {"gz": z - 1}))

    def wait_x(part, first, rows):
        at = pl.ds(first, rows)
        when(x_low, lambda: arrived(halo_v.at[0, :, at, :], x_recv.at[0, part]))
        when(x_high, lambda: arrived(halo_v.at[1, :, at, :], x_recv.at[1, part]))
        join(halo_v, first, rows)

    def wait_z(part, first, rows):
        at = pl.ds(8 + first, rows)
        when(z_low, lambda: arrived(vel.at[:, 0:2, at, :], z_recv.at[0, part]))
        when(z_high, lambda: arrived(vel.at[:, 18:20, at, :], z_recv.at[1, part]))

    for row in range(8, 40, 8):
        heights(row)
    for d in range(1, GZ):
        g = (z + d) % GZ
        arrived(layers.at[:, pl.ds(NZ * g, NZ), :], layer_recv.at[g])
    metrics(8, 16)

    def start_far():
        pl.semaphore_wait(far_sem, 1)
        edge_up.start()
        start_up()

    for copy in (stress_in[1], stress_in[2], stress_in[5], velocity_in):
        copy.wait()
    when(x_low, lambda: arrived(halo_s.at[0], s_recv.at[0]))
    when(x_high, lambda: arrived(halo_s.at[1], s_recv.at[1]))
    join(halo_s, 0, NY)
    def wait_stress_z(part, condition):
        _, first, rows = z_parts[part]
        to = pl.ds(8 + first, rows)
        when(condition & z_low, lambda: arrived(sigma.at[:, 0:2, to, :], zs_recv.at[0, part]))
        when(condition & z_high, lambda: arrived(sigma.at[:, 18:20, to, :], zs_recv.at[1, part]))

    gap_copy = remote(gap_out, gap_in, gap_sem.at[0], gap_sem.at[1], down_y)
    sends.append((after_gap, gap_copy))

    def gap_package():
        top = lax.broadcasted_iota(jnp.int32, (8, NX), 0) == 0

        def layers_of(step, carry):
            for k in (2 * step, 2 * step + 1):
                scale = props[0, k, 0:8, :]
                for c in range(6):
                    gap_out[3 + c, k] = (scale * d_k(sigma, c, k, 0, 8))[0:2]
                gap_out[9, k] = scale[0:2]
                for i, (c_x, c_y) in enumerate(zip(X_PARTS, Y_PARTS)):
                    here, after_1, after_2 = (sigma[c_y, k + 2, 8 + d : 16 + d, :] for d in range(3))
                    before_1 = jnp.where(top, 0.0, pltpu.roll(here, 1, 0))
                    grad_y = 8.0 * (after_1 - before_1) - after_2
                    known = v_out[i, k, 0:8, :] + scale * (d_x(c_x, k, 0, 8, halo_s, i) + grad_y)
                    gap_out[i, k] = known[0:2]
            return carry

        lax.fori_loop(0, NZ // 2, layers_of, 0)
        gap_copy.start()

    def gap_velocity():
        arrived(gap_in, gap_sem.at[1])

        def layers_of(step, carry):
            for k in (2 * step, 2 * step + 1):
                m_x, m_y, m_z = (metric[i, k, NY : NY + 2, :] for i in range(3))
                for i, (a, b, d) in enumerate(((0, 3, 4), (3, 1, 5), (4, 5, 2))):
                    edge = sigma[Y_PARTS[i], k + 2, 38:40, :]
                    beyond = jnp.concatenate([edge[0:1] - 8.0 * edge[1:2], edge[1:2]], axis=0)
                    known = gap_in[i, k] + gap_in[9, k] * beyond
                    vel[i, 2 + k, 40:42, :] = known - m_x * gap_in[3 + a, k] - m_y * gap_in[3 + b, k] + m_z * gap_in[3 + d, k]
            return carry

        lax.fori_loop(0, NZ // 2, layers_of, 0)

    def gap_metrics():
        for part in range(3):
            wide[part, 48:64, :] = jnp.zeros((16, NX), jnp.float32)
        metrics(NY, 8)

    wait_stress_z(2, after_gap)
    when(after_gap, gap_package)
    wait_stress_z(0, z >= 0)
    velocity_rows(8, 16, 2)
    send_rows(0, 8, 16)
    differentiate_x(range(3), vel, 8, 16, 4)
    when(before_gap, start_far)

    low_copy = remote(vel.at[:, 2:18, 8:10, :], vel.at[:, 2:18, 40:42, :], vy_send.at[1], vy_recv.at[1], down_y)
    high_copy = remote(vel.at[:, 2:18, 38:40, :], vel.at[:, 2:18, 6:8, :], vy_send.at[0], vy_recv.at[0], up_y)
    sends.append((y_low & ~after_gap, low_copy))
    sends.append((y_high, high_copy))
    for part, low, first, outer in strips:
        when(low & y_low, lambda: arrived(terrain.at[:, 0:8, :], edge_recv.at[0]))
        when(~low & y_high, lambda: arrived(terrain.at[:, 40:48, :], edge_recv.at[1]))
        heights(outer)
        metrics(first, 8)
        for i, c in enumerate(Y_SENT):
            when(low & y_low, lambda: arrived(sigma.at[c, 2:18, 6:8, :], y_recv.at[0, i]))
            when(~low & y_high, lambda: arrived(sigma.at[c, 2:18, 40:42, :], y_recv.at[1, i]))
        wait_stress_z(part, (z >= 0) if part == 1 else ~after_gap)
        velocity_rows(first, 8, 4)
        when(low & y_low & ~after_gap, low_copy.start)
        when(~low & y_high, high_copy.start)
        send_rows(part, first, 8)
    for _, _, first, _ in strips:
        differentiate_x(range(3), vel, first, 8, 8)
    when(before_gap, gap_metrics)

    memory_in.wait()

    def stress_rows(first, rows, unroll, steps, stride=1):
        at = pl.ds(first, rows)

        def stress_layer(step, carry):
            for k in [unroll * stride * step + i for i in range(unroll)]:
                grad_x = [d_x(c, k, first, rows, halo_v, c) for c in range(3)]
                m_x, m_y, m_z = (metric[i, k, at, :] for i in range(3))
                along_k = [d_k(vel, c, k, first, rows) for c in range(3)]
                along_x = [grad_x[c] - m_x * along_k[c] for c in range(3)]
                along_y = [d_y(vel, c, k, first, rows) - m_y * along_k[c] for c in range(3)]
                along_z = [m_z * along_k[c] for c in range(3)]
                lam, mu, kept, gain = (props[i, k, at, :] for i in range(1, 5))
                volume = lam * (along_x[0] + along_y[1] + along_z[2])
                twice = mu + mu
                rates = (
                    volume + twice * along_x[0],
                    volume + twice * along_y[1],
                    volume + twice * along_z[2],
                    mu * (along_y[0] + along_x[1]),
                    mu * (along_z[0] + along_x[2]),
                    mu * (along_z[1] + along_y[2]),
                )
                for c, rate in enumerate(rates):
                    new = kept * m_out[c, k, at, :] + gain * rate
                    m_out[c, k, at, :] = new
                    s_out[c, k, at, :] = sigma[c, 2 + k, pl.ds(8 + first, rows), :] + STEP * (rate - new)
            return carry

        lax.fori_loop(steps[0], steps[1], stress_layer, 0)

    wait_x(0, 8, 16)
    stress_rows(8, 16, 2, (1, NZ // 2 - 1))
    wait_z(0, 8, 16)
    stress_rows(8, 16, 2, (0, 2), NZ // 2 - 1)
    for part, low, first, outer in strips:
        wait_x(part, first, 8)
        wait_z(part, first, 8)
        when(low & y_low, lambda: arrived(vel.at[:, 2:18, 6:8, :], vy_recv.at[0]))
        when(~low & y_high & ~before_gap, lambda: arrived(vel.at[:, 2:18, 40:42, :], vy_recv.at[1]))
        if part == 2:
            when(before_gap, gap_velocity)
        stress_rows(first, 8, 4, (0, NZ // 4))
    for condition, copy in sends:
        when(condition, copy.wait_send)


def write_out(v_in, s_in, m_in, v_ref, s_ref, m_ref, sems):
    pairs = [(v_in, v_ref, c) for c in range(3)] + [(a, b, c) for a, b in ((s_in, s_ref), (m_in, m_ref)) for c in range(6)]
    copies = [pltpu.make_async_copy(a.at[c], b.at[c], sems.at[i]) for i, (a, b, c) in enumerate(pairs)]
    for copy in copies:
        copy.start()
    for copy in copies:
        copy.wait()


def local(*arrays):
    held = [pltpu.with_memory_space_constraint(array, pltpu.HBM) for array in arrays]
    f32, vmem, dma = jnp.float32, pltpu.VMEM, pltpu.SemaphoreType.DMA
    outputs = [(n, NZ, NY, NX) for n in (3, 6, 6)]
    results = pl.pallas_call(
        kernel,
        out_shape=tuple(vmem(shape, f32) for shape in outputs),
        in_specs=[pl.BlockSpec(memory_space=pltpu.HBM)] * len(held),
        out_specs=tuple(pl.BlockSpec(memory_space=vmem) for _ in outputs),
        scratch_shapes=[
            vmem((6, 20, 48, NX), f32),
            vmem((3, 20, 48, NX), f32),
            vmem((6, 48, 32), jnp.int32),
            vmem((3, 64, NX), f32),
            vmem((3, 24, NX), f32),
            vmem((2, GZ * NZ, NX), f32),
            vmem((NZ, NY, NX), jnp.int32),
            vmem((5, 8, NX), f32),
            vmem((5, NZ, NY, NX), f32),
            vmem((NX, NX), jnp.bfloat16),
            vmem((3, NZ, NY, NX), f32),
            vmem((3, NZ, NY + 8, NX), f32),
            vmem((2, 2, NY, NX), f32),
            vmem((2, 2, NY, NX), f32),
            vmem((2, 2, NY, NX), f32),
            pltpu.SMEM((7, 16), f32),
            dma((17,)), dma((4,)), dma((4,)), dma((2, 3)), dma((2, 3)), dma((3,)), dma((4,)), dma((7,)), dma((6,)), dma((2,)), dma((2,)),
            dma((2, 3)), dma((2, 3)), dma((2, 3)), dma((2, 3)), dma((2,)), dma((2,)),
            dma((2, 3)), dma((2, 3)),
            vmem((10, NZ, 2, NX), f32),
            vmem((10, NZ, 2, NX), f32),
            dma((2,)),
            pltpu.SemaphoreType.REGULAR,
        ],
        compiler_params=pltpu.CompilerParams(
            collective_id=0, has_side_effects=True, vmem_limit_bytes=24 << 20
        ),
    )(*held)
    return pl.pallas_call(
        write_out,
        out_shape=tuple(jax.ShapeDtypeStruct(shape, f32) for shape in outputs),
        in_specs=[pl.BlockSpec(memory_space=vmem)] * 3,
        out_specs=tuple(pl.BlockSpec(memory_space=pltpu.HBM) for _ in outputs),
        scratch_shapes=[dma((15,))],
        compiler_params=pltpu.CompilerParams(vmem_limit_bytes=8 << 20),
    )(*results)


def solution(mesh):
    field = P(None, "gz", "gy", "gx")
    return jax.shard_map(
        local,
        mesh=mesh,
        in_specs=(
            P("gy", ("gx", "gz")), P("gz"), P("gz"), P("gz", "gy", "gx"),
            P(), P(), P(), P(), P(), field, field, field,
        ),
        out_specs=(field, field, field),
        check_vma=False,
    )
```

```python
import functools

import jax
import jax.numpy as jnp
from jax import lax
from jax.experimental import pallas as pl
from jax.experimental.pallas import tpu as pltpu
from jax.sharding import PartitionSpec as P

MESH = pl.DeviceIdType.MESH
STEP = 0.3
GX, GY, GZ = 4, 16, 4
NZ, NY, NX = 16, 32, 128
X_PARTS = (0, 3, 4)
Y_PARTS = (3, 1, 5)
Y_SENT = (1, 3, 5)


def when(condition, action):
    if condition is None:
        action()
    else:
        pl.when(condition)(lambda: action())


def centred_12(before_2, before_1, after_1, after_2):
    return 8.0 * (after_1 - before_1) - (after_2 - before_2)


def kernel(
    elevation, layer_base, stretch, material, buoyancy, lame, shear, relax, weight, velocity, stress, memory,
    v_out, s_out, m_out,
    sigma, vel, terrain, wide, surf, layers, mat, tables, props, stencil, along, metric, packs, halo_s, halo_v,
    small, local_sem, s_send, s_recv, y_send, y_recv, layer_send, layer_recv, t_send, t_recv, edge_send, edge_recv,
    z_send, z_recv, x_send, x_recv, vy_send, vy_recv, zs_send, zs_recv, gap_out, gap_in, gap_sem, pass_send, pass_recv, far_sem,
):
    x, y, z = lax.axis_index("gx"), lax.axis_index("gy"), lax.axis_index("gz")
    x_low, x_high = x > 0, x < GX - 1
    y_low, y_high = y > 0, y < GY - 1
    z_low, z_high = z > 0, z < GZ - 1
    before_gap, after_gap = y == GY // 2 - 1, y == GY // 2
    at_gap = before_gap | after_gap
    lane = lax.broadcasted_iota(jnp.int32, (8, NX), 1)

    own_slot = 1 + z
    tables_in = (buoyancy, lame, shear, relax, weight, layer_base, stretch)
    scalars = [pltpu.make_async_copy(ref, small.at[i], local_sem.at[i]) for i, ref in enumerate(tables_in)]
    for copy in scalars:
        copy.start()
    stress_in = {
        c: pltpu.make_async_copy(stress.at[c], sigma.at[c, 2:18, 8:40, :], local_sem.at[7 + c])
        for c in (0, 3, 4, 1, 2, 5)
    }
    for c in (0, 3, 4):
        stress_in[c].start()
    material_in = pltpu.make_async_copy(material, mat, local_sem.at[15])
    material_in.start()
    for c in (1, 2, 5):
        stress_in[c].start()
    elevation_in = pltpu.make_async_copy(elevation, terrain.at[own_slot, 8:40, :], local_sem.at[13])
    velocity_in = pltpu.make_async_copy(velocity, v_out, local_sem.at[14])
    memory_in = pltpu.make_async_copy(memory, m_out, local_sem.at[16])
    for copy in (elevation_in, velocity_in, memory_in):
        copy.start()

    barrier = pltpu.get_barrier_semaphore()
    beside = [(None, {"gz": (z + d) % GZ}) for d in range(1, GZ)]
    for g in range(GZ):
        beside.append((x_high & ((z == g) | (z == GZ - 1) | (g == 0)), {"gx": x + 1, "gz": g}))
        beside.append((x_low & ((z == g) | (z == 0) | (g == GZ - 1)), {"gx": x - 1, "gz": g}))
    up_y, down_y = {"gy": y + 1}, {"gy": y - 1}
    for condition, target in [(y_high, up_y), (y_low & ~after_gap, down_y)] + beside:
        when(condition, lambda target=target: pl.semaphore_signal(barrier, inc=1, device_id=target, device_id_type=MESH))
    expected = [y_low, y_high & ~before_gap] + [condition for condition, _ in beside]

    pl.semaphore_wait(barrier, sum(1 if c is None else c.astype(jnp.int32) for c in expected))
    when(after_gap, lambda: pl.semaphore_signal(far_sem, inc=1, device_id=down_y, device_id_type=MESH))

    def remote(source, to, send, recv, target):
        return pltpu.make_async_remote_copy(
            src_ref=source, dst_ref=to, send_sem=send, recv_sem=recv, device_id=target, device_id_type=MESH
        )

    sends = []

    def send(condition, copy, now=True):
        sends.append((condition, copy))
        if now:
            when(condition, copy.start)
        return copy

    for d in range(1, GZ):
        send(None, remote(elevation, terrain.at[own_slot, 8:40, :], t_send.at[d - 1], t_recv.at[own_slot], {"gz": (z + d) % GZ}))
    for g in range(GZ):
        send(x_high & (z == GZ - 1), remote(elevation, terrain.at[0, 8:40, :], t_send.at[3 + g], t_recv.at[0], {"gx": x + 1, "gz": g}))
        send(x_low & (z == 0), remote(elevation, terrain.at[5, 8:40, :], t_send.at[3 + g], t_recv.at[5], {"gx": x - 1, "gz": g}))
    gap_terrain = terrain.at[own_slot, 40:48, :]
    send(after_gap, remote(elevation.at[0:8, :], gap_terrain, gap_sem.at[2], gap_sem.at[3], down_y))
    up_copies = [
        send(y_high, remote(stress.at[c, :, 30:32, :], sigma.at[c, 2:18, 6:8, :], y_send.at[0, i], y_recv.at[0, i], up_y), now=False)
        for i, c in enumerate(Y_SENT)
    ]

    def start_up():
        for copy in up_copies:
            copy.start()

    when(y_high & ~before_gap, start_up)
    for i, c in enumerate(Y_SENT):
        send(y_low, remote(stress.at[c, :, 0:2, :], sigma.at[c, 2:18, 40:42, :], y_send.at[1, i], y_recv.at[1, i], down_y))
    odd = y % 2
    strips = []
    for part in (1, 2):
        low = (odd == 1) if part == 1 else (odd == 0)
        side = odd if part == 1 else 1 - odd
        strips.append((part, low, pl.multiple_of(24 - 24 * side, 8), pl.multiple_of(40 - 40 * side, 8)))
    z_parts = [(0, 8, 16)] + [(part, first, 8) for part, _, first, _ in strips]
    z_copies = []
    for part, first, rows in z_parts:
        at, to = pl.ds(first, rows), pl.ds(8 + first, rows)
        z_copies.append((
            send(z_high, remote(stress.at[:, 14:16, at, :], sigma.at[:, 0:2, to, :], zs_send.at[0, part], zs_recv.at[0, part], {"gz": z + 1}), now=False),
            send(z_low, remote(stress.at[:, 0:2, at, :], sigma.at[:, 18:20, to, :], zs_send.at[1, part], zs_recv.at[1, part], {"gz": z - 1}), now=False),
        ))

    def start_z(part, condition):
        when(z_high if condition is None else condition & z_high, z_copies[part][0].start)
        when(z_low if condition is None else condition & z_low, z_copies[part][1].start)

    start_z(2, after_gap)
    start_z(0, None)
    start_z(1, None)
    start_z(2, ~after_gap)

    zero = jnp.zeros((8, NX), jnp.float32)

    def pack_spot(k, i):
        at = 4 * (k + (NZ if i == 1 else 0))
        return at, (lane >= at) & (lane < at + 4)

    def pack_layer(held, blocks, i, k, at, spot):
        for r, block in enumerate(blocks):
            j = len(blocks) * (i // 2) + r
            held[j] = jnp.where(spot, pltpu.roll(block, at + 2, 1), held[j])

    def pack_stress(step, held):
        held = list(held)
        for k in (2 * step, 2 * step + 1):
            for i, c in enumerate(X_PARTS):
                at, spot = pack_spot(k, i)
                pack_layer(held, [sigma[c, 2 + k, 8 + 8 * r : 16 + 8 * r, :] for r in range(4)], i, k, at, spot)
        return tuple(held)

    for copy in scalars:
        copy.wait()
    for k in range(NZ):
        for row in range(2):
            layers[row, pl.ds(NZ * z + k, 1), :] = jnp.full((1, NX), small[5 + row, k], jnp.float32)

    for c in X_PARTS:
        stress_in[c].wait()
    held = lax.fori_loop(0, NZ // 2, pack_stress, (zero,) * 8)
    for j in range(8):
        packs[0, j // 4, 8 * (j % 4) : 8 * (j % 4) + 8, :] = held[j]

    mine = pl.ds(NZ * z, NZ)
    for d in range(1, GZ):
        send(None, remote(layers.at[:, mine, :], layers.at[:, mine, :], layer_send.at[d - 1], layer_recv.at[z], {"gz": (z + d) % GZ}))
    columns = []
    for i in range(5):
        column = zero
        for block_id in range(16):
            column = jnp.where(lane == block_id, small[i, block_id], column)
        columns.append(column)
    keep = jnp.exp(-STEP / jnp.where(lane < 16, columns[3], 1.0))
    tables[0] = columns[0] * (STEP / 12.0)
    tables[1] = columns[1] * (1.0 / 12.0)
    tables[2] = columns[2] * (1.0 / 12.0)
    tables[3] = keep
    tables[4] = (1.0 - keep) * columns[4]

    send(x_high, remote(packs.at[0], halo_s.at[0], s_send.at[0], s_recv.at[0], {"gx": x + 1}))
    send(x_low, remote(packs.at[0], halo_s.at[1], s_send.at[1], s_recv.at[1], {"gx": x - 1}))
    material_in.wait()

    def property_layer(k, carry):
        for r in range(4):
            rows = slice(8 * r, 8 * r + 8)
            block_id = mat[k, rows, :]
            for i in range(5):
                props[i, k, rows, :] = jnp.take_along_axis(tables[i], block_id, axis=1)
        return carry

    lax.fori_loop(0, NZ, property_layer, 0)

    offset = lax.broadcasted_iota(jnp.int32, (NX, NX), 0) - lax.broadcasted_iota(jnp.int32, (NX, NX), 1)
    weights = jnp.zeros((NX, NX), jnp.float32)
    for distance, factor in ((-2, 1.0), (-1, -8.0), (1, 8.0), (2, -1.0)):
        weights = jnp.where(offset == distance, factor, weights)
    stencil[...] = weights.astype(jnp.bfloat16)

    def differentiate_x(parts, field, first, rows, unroll):
        def layers_of(step, carry):
            spots = [(i, c, unroll * step + n) for i, c in enumerate(parts) for n in range(unroll)]
            rest = jnp.concatenate([field[c, k + 2, pl.ds(8 + first, rows), :] for _, c, k in spots], axis=0)
            total = None
            for _ in range(3):
                piece = rest.astype(jnp.bfloat16)
                rest = rest - piece.astype(jnp.float32)
                product = jnp.dot(piece, stencil[...], preferred_element_type=jnp.float32)
                total = product if total is None else total + product
            for n, (i, _, k) in enumerate(spots):
                along[i, k, pl.ds(first, rows), :] = total[n * rows : (n + 1) * rows]
            return carry

        lax.fori_loop(0, NZ // unroll, layers_of, 0)

    differentiate_x(X_PARTS, sigma, 0, NY, 4)

    def arrived(ref, recv):
        remote(ref, ref, s_send.at[0], recv, {"gz": z}).wait_recv()

    def zero_z(first):
        sigma[:, pl.ds(first, 2), 8:40, :] = jnp.zeros((6, 2, NY, NX), jnp.float32)
        vel[:, pl.ds(first, 2), 8:40, :] = jnp.zeros((3, 2, NY, NX), jnp.float32)

    def zero_y(first):
        def layer(k, carry):
            for c in Y_SENT:
                sigma[c, 2 + k, first : first + 8, :] = zero
            for c in range(3):
                vel[c, 2 + k, first : first + 8, :] = zero
            return carry

        lax.fori_loop(0, NZ, layer, 0)
        for m in range(6):
            terrain[m, first : first + 8, :] = jnp.zeros((8, 32), jnp.int32)

    def zero_x(side, slot):
        halo_s[side] = jnp.zeros((2, NY, NX), jnp.float32)
        halo_v[side] = jnp.zeros((2, NY, NX), jnp.float32)
        terrain[slot, 8:40, :] = jnp.zeros((32, 32), jnp.int32)

        def zero_top():
            terrain[slot, 40:48, :] = jnp.zeros((8, 32), jnp.int32)

        when(before_gap, zero_top)

    when(z == 0, lambda: zero_z(0))
    when(z == GZ - 1, lambda: zero_z(18))
    when(y == 0, lambda: zero_y(0))
    when(y == GY - 1, lambda: zero_y(40))
    when(x == 0, lambda: zero_x(0, 0))
    when(x == GX - 1, lambda: zero_x(1, 5))

    def d_k(field, c, k, first, rows):
        return centred_12(*[field[c, k + 2 + d, pl.ds(8 + first, rows), :] for d in (-2, -1, 1, 2)])

    def d_y(field, c, k, first, rows):
        return centred_12(*[field[c, k + 2, pl.ds(8 + first + d, rows), :] for d in (-2, -1, 1, 2)])

    def d_x(c, k, first, rows, halo, i):
        side = lax.broadcasted_iota(jnp.int32, (rows, NX), 1)
        at = 4 * (k + (NZ if i == 1 else 0))
        fix = pltpu.roll(halo[0, i // 2, pl.ds(first, rows), :], 126 - at, 1)
        return along[i, k, pl.ds(first, rows), :] + jnp.where((side < 2) | (side >= 126), fix, 0.0)

    def join(halo, first, rows):
        spot = lax.broadcasted_iota(jnp.int32, (rows, NX), 1) % 4
        at = pl.ds(first, rows)
        for i in range(2):
            change = jnp.where(spot < 2, halo[0, i, at, :], halo[1, i, at, :])
            low = 8.0 * jnp.where(spot == 1, pltpu.roll(change, 127, 1), 0.0) - pltpu.roll(change, 126, 1)
            high = pltpu.roll(change, 2, 1) - 8.0 * jnp.where(spot == 2, pltpu.roll(change, 1, 1), 0.0)
            halo[0, i, at, :] = jnp.where(spot < 2, low, high)

    for copy in (stress_in[1], stress_in[2], stress_in[5], velocity_in):
        copy.wait()
    when(x_low, lambda: arrived(halo_s.at[0], s_recv.at[0]))
    when(x_high, lambda: arrived(halo_s.at[1], s_recv.at[1]))
    join(halo_s, 0, NY)
    def wait_stress_z(part, condition):
        _, first, rows = z_parts[part]
        to = pl.ds(8 + first, rows)
        when(condition & z_low, lambda: arrived(sigma.at[:, 0:2, to, :], zs_recv.at[0, part]))
        when(condition & z_high, lambda: arrived(sigma.at[:, 18:20, to, :], zs_recv.at[1, part]))

    gap_copy = remote(gap_out, gap_in, gap_sem.at[0], gap_sem.at[1], down_y)
    sends.append((after_gap, gap_copy))

    def gap_package():
        top = lax.broadcasted_iota(jnp.int32, (8, NX), 0) == 0

        def layers_of(step, carry):
            for k in (2 * step, 2 * step + 1):
                scale = props[0, k, 0:8, :]
                for c in range(6):
                    gap_out[3 + c, k] = (scale * d_k(sigma, c, k, 0, 8))[0:2]
                gap_out[9, k] = scale[0:2]
                for i, (c_x, c_y) in enumerate(zip(X_PARTS, Y_PARTS)):
                    here, after_1, after_2 = (sigma[c_y, k + 2, 8 + d : 16 + d, :] for d in range(3))
                    before_1 = jnp.where(top, 0.0, pltpu.roll(here, 1, 0))
                    grad_y = 8.0 * (after_1 - before_1) - after_2
                    known = v_out[i, k, 0:8, :] + scale * (d_x(c_x, k, 0, 8, halo_s, i) + grad_y)
                    gap_out[i, k] = known[0:2]
            return carry

        lax.fori_loop(0, NZ // 2, layers_of, 0)
        gap_copy.start()

    wait_stress_z(2, after_gap)
    when(after_gap, gap_package)

    elevation_in.wait()
    for d in range(1, GZ):
        g = (z + d) % GZ
        arrived(terrain.at[1 + g, 8:40, :], t_recv.at[1 + g])
    when(x_low, lambda: arrived(terrain.at[0, 8:40, :], t_recv.at[0]))
    when(x_high, lambda: arrived(terrain.at[5, 8:40, :], t_recv.at[5]))
    edge_up = send(y_high, remote(terrain.at[:, 32:40, :], terrain.at[:, 0:8, :], edge_send.at[0], edge_recv.at[0], up_y), now=False)
    when(y_high & ~before_gap, edge_up.start)
    send(y_low & ~after_gap, remote(terrain.at[:, 8:16, :], terrain.at[:, 40:48, :], edge_send.at[1], edge_recv.at[1], down_y))

    def heights(row):
        rows = pl.ds(row, 8)
        held = [terrain[m, rows, :].astype(jnp.float32) / 200.0 for m in range(6)]
        blank = jnp.zeros((8, 96), jnp.float32)
        wide[0, rows, :] = jnp.concatenate([blank, held[0]], axis=1)
        wide[1, rows, :] = jnp.concatenate(held[1:5], axis=1)
        wide[2, rows, :] = jnp.concatenate([held[5], blank], axis=1)

    binomial = (1.0, 4.0, 6.0, 4.0, 1.0)

    def metrics(first, rows):
        along_y = []
        for part in range(3):
            total = jnp.zeros((rows + 8, NX), jnp.float32)
            for d, factor in enumerate(binomial):
                total = total + factor * wide[part, pl.ds(first + 2 + d, rows + 8), :]
            along_y.append(total / 16.0)
        row = jnp.concatenate(along_y, axis=1)
        total = jnp.zeros_like(row)
        for d, factor in enumerate(binomial):
            total = total + factor * (row if d == 2 else pltpu.roll(row, (2 - d) % 384, 1))
        total = total / 16.0
        for part in range(3):
            surf[part, 0 : rows + 8, :] = total[:, 128 * part : 128 * part + 128]
        own = jnp.concatenate([surf[part, 4 : 4 + rows, :] for part in range(3)], axis=1)
        height = own[:, 128:256]
        shifted = [pltpu.roll(own, d % 384, 1)[:, 128:256] for d in (2, 1, -1, -2)]
        slope_x = centred_12(*shifted) / 12.0
        slope_y = centred_12(*[surf[1, 4 + d : 4 + d + rows, :] for d in (-2, -1, 1, 2)]) / 12.0

        def above(step, total):
            for layer in [4 * step + i for i in range(4)]:
                base, follow = layers[0, pl.ds(layer, 1), :], layers[1, pl.ds(layer, 1), :]
                total = total + follow * (base * jnp.exp(follow * height))
            return total

        upper = lax.fori_loop(0, (NZ // 4) * z, above, jnp.zeros((rows, NX), jnp.float32))

        def layer(step, total):
            for k in [4 * step + i for i in range(4)]:
                base, follow = layers[0, pl.ds(NZ * z + k, 1), :], layers[1, pl.ds(NZ * z + k, 1), :]
                thickness = base * jnp.exp(follow * height)
                weighted = follow * thickness
                inverse = 1.0 / thickness
                factor = (total + 0.5 * weighted - 1.0) * inverse
                at = pl.ds(first, rows)
                metric[0, k, at, :] = slope_x * factor
                metric[1, k, at, :] = slope_y * factor
                metric[2, k, at, :] = inverse
                total = total + weighted
            return total

        lax.fori_loop(0, NZ // 4, layer, upper)

    def velocity_rows(first, rows, unroll):
        blocks = rows // 8

        def velocity_layer(step, carried):
            held, last = list(carried[0]), carried[1]
            at = pl.ds(first, rows)
            ks = [unroll * step + i for i in range(unroll)]
            pack_rows(held, [k - unroll for k in ks], last)
            made = []
            for k in ks:
                m_x, m_y, m_z = (metric[i, k, at, :] for i in range(3))
                grad_k = [d_k(sigma, c, k, first, rows) for c in range(6)]
                grad_x = [d_x(c, k, first, rows, halo_s, i) for i, c in enumerate(X_PARTS)]
                grad_y = [d_y(sigma, c, k, first, rows) for c in Y_PARTS]
                scale = props[0, k, at, :]
                row = []
                for c, (a, b, d) in enumerate(((0, 3, 4), (3, 1, 5), (4, 5, 2))):
                    accel = (grad_x[c] - m_x * grad_k[a]) + (grad_y[c] - m_y * grad_k[b]) + m_z * grad_k[d]
                    new = v_out[c, k, at, :] + scale * accel
                    v_out[c, k, at, :] = new
                    vel[c, 2 + k, pl.ds(8 + first, rows), :] = new
                    row.append(new)
                made.append(row)
            return tuple(held), made

        def pack_rows(held, ks, made):
            for k, row in zip(ks, made):
                for c in range(3):
                    spot_at, spot = pack_spot(k, c)
                    pack_layer(held, [row[c][8 * r : 8 * r + 8] for r in range(blocks)], c, k, spot_at, spot)

        nothing = jnp.zeros((rows, NX), jnp.float32)
        start = ((zero,) * (2 * blocks), [[nothing] * 3 for _ in range(unroll)])
        held, last = lax.fori_loop(0, NZ // unroll, velocity_layer, start)
        held = list(held)
        pack_rows(held, range(NZ - unroll, NZ), last)
        for j in range(2 * blocks):
            packs[1, j // blocks, pl.ds(first + 8 * (j % blocks), 8), :] = held[j]

    def send_rows(part, first, rows):
        at = pl.ds(first, rows)
        send(x_high, remote(packs.at[1, :, at, :], halo_v.at[0, :, at, :], x_send.at[0, part], x_recv.at[0, part], {"gx": x + 1}))
        send(x_low, remote(packs.at[1, :, at, :], halo_v.at[1, :, at, :], x_send.at[1, part], x_recv.at[1, part], {"gx": x - 1}))
        at = pl.ds(8 + first, rows)
        send(z_high, remote(vel.at[:, 16:18, at, :], vel.at[:, 0:2, at, :], z_send.at[0, part], z_recv.at[0, part], {"gz": z + 1}))
        send(z_low, remote(vel.at[:, 2:4, at, :], vel.at[:, 18:20, at, :], z_send.at[1, part], z_recv.at[1, part], {"gz": z - 1}))

    def wait_x(part, first, rows):
        at = pl.ds(first, rows)
        when(x_low, lambda: arrived(halo_v.at[0, :, at, :], x_recv.at[0, part]))
        when(x_high, lambda: arrived(halo_v.at[1, :, at, :], x_recv.at[1, part]))
        join(halo_v, first, rows)

    def wait_z(part, first, rows):
        at = pl.ds(8 + first, rows)
        when(z_low, lambda: arrived(vel.at[:, 0:2, at, :], z_recv.at[0, part]))
        when(z_high, lambda: arrived(vel.at[:, 18:20, at, :], z_recv.at[1, part]))

    for row in range(8, 40, 8):
        heights(row)
    for d in range(1, GZ):
        g = (z + d) % GZ
        arrived(layers.at[:, pl.ds(NZ * g, NZ), :], layer_recv.at[g])
    metrics(8, 16)

    def start_far():
        pl.semaphore_wait(far_sem, 1)
        edge_up.start()
        start_up()

    def gap_velocity():
        arrived(gap_in, gap_sem.at[1])

        def layers_of(step, carry):
            for k in (2 * step, 2 * step + 1):
                m_x, m_y, m_z = (metric[i, k, NY : NY + 2, :] for i in range(3))
                for i, (a, b, d) in enumerate(((0, 3, 4), (3, 1, 5), (4, 5, 2))):
                    edge = sigma[Y_PARTS[i], k + 2, 38:40, :]
                    beyond = jnp.concatenate([edge[0:1] - 8.0 * edge[1:2], edge[1:2]], axis=0)
                    known = gap_in[i, k] + gap_in[9, k] * beyond
                    vel[i, 2 + k, 40:42, :] = known - m_x * gap_in[3 + a, k] - m_y * gap_in[3 + b, k] + m_z * gap_in[3 + d, k]
            return carry

        lax.fori_loop(0, NZ // 2, layers_of, 0)

    def gap_metrics():
        for part in range(3):
            wide[part, 48:64, :] = jnp.zeros((16, NX), jnp.float32)
        metrics(NY, 8)

    wait_stress_z(0, z >= 0)
    velocity_rows(8, 16, 2)
    send_rows(0, 8, 16)
    differentiate_x(range(3), vel, 8, 16, 4)
    when(before_gap, start_far)
    when(before_gap, lambda: arrived(gap_terrain, gap_sem.at[3]))
    for d in range(1, GZ):
        send(before_gap, remote(gap_terrain, gap_terrain, pass_send.at[d - 1], pass_recv.at[own_slot], {"gz": (z + d) % GZ}))
    for g in range(GZ):
        send(before_gap & x_high & (z == GZ - 1), remote(gap_terrain, terrain.at[0, 40:48, :], pass_send.at[3 + g], pass_recv.at[0], {"gx": x + 1, "gz": g}))
        send(before_gap & x_low & (z == 0), remote(gap_terrain, terrain.at[5, 40:48, :], pass_send.at[3 + g], pass_recv.at[5], {"gx": x - 1, "gz": g}))

    def gap_terrain_arrived():
        for d in range(1, GZ):
            slot = 1 + (z + d) % GZ
            arrived(terrain.at[slot, 40:48, :], pass_recv.at[slot])
        when(x_low, lambda: arrived(terrain.at[0, 40:48, :], pass_recv.at[0]))
        when(x_high, lambda: arrived(terrain.at[5, 40:48, :], pass_recv.at[5]))

    low_copy = remote(vel.at[:, 2:18, 8:10, :], vel.at[:, 2:18, 40:42, :], vy_send.at[1], vy_recv.at[1], down_y)
    high_copy = remote(vel.at[:, 2:18, 38:40, :], vel.at[:, 2:18, 6:8, :], vy_send.at[0], vy_recv.at[0], up_y)
    sends.append((y_low & ~after_gap, low_copy))
    sends.append((y_high, high_copy))

    def stress_rows(first, rows, unroll, steps, stride=1):
        at = pl.ds(first, rows)

        def stress_layer(step, carry):
            for k in [unroll * stride * step + i for i in range(unroll)]:
                grad_x = [d_x(c, k, first, rows, halo_v, c) for c in range(3)]
                m_x, m_y, m_z = (metric[i, k, at, :] for i in range(3))
                along_k = [d_k(vel, c, k, first, rows) for c in range(3)]
                along_x = [grad_x[c] - m_x * along_k[c] for c in range(3)]
                along_y = [d_y(vel, c, k, first, rows) - m_y * along_k[c] for c in range(3)]
                along_z = [m_z * along_k[c] for c in range(3)]
                lam, mu, kept, gain = (props[i, k, at, :] for i in range(1, 5))
                volume = lam * (along_x[0] + along_y[1] + along_z[2])
                twice = mu + mu
                rates = (
                    volume + twice * along_x[0],
                    volume + twice * along_y[1],
                    volume + twice * along_z[2],
                    mu * (along_y[0] + along_x[1]),
                    mu * (along_z[0] + along_x[2]),
                    mu * (along_z[1] + along_y[2]),
                )
                for c, rate in enumerate(rates):
                    new = kept * m_out[c, k, at, :] + gain * rate
                    m_out[c, k, at, :] = new
                    s_out[c, k, at, :] = sigma[c, 2 + k, pl.ds(8 + first, rows), :] + STEP * (rate - new)
            return carry

        lax.fori_loop(steps[0], steps[1], stress_layer, 0)

    def stress_beside(part):
        _, low, first, _ = strips[part - 1]
        wait_x(part, first, 8)
        wait_z(part, first, 8)
        when(low & y_low, lambda: arrived(vel.at[:, 2:18, 6:8, :], vy_recv.at[0]))
        when(~low & y_high & ~before_gap, lambda: arrived(vel.at[:, 2:18, 40:42, :], vy_recv.at[1]))
        if part == 2:
            when(before_gap, gap_velocity)
        stress_rows(first, 8, 4, (0, NZ // 4))

    inner_near = pl.multiple_of(16 - 8 * odd, 8)
    inner_far = pl.multiple_of(8 + 8 * odd, 8)

    def early_stress():
        differentiate_x(range(3), vel, strips[0][2], 8, 8)
        memory_in.wait()
        wait_x(0, 8, 16)
        wait_z(0, 8, 16)
        stress_rows(inner_near, 8, 4, (0, NZ // 4))
        stress_beside(1)

    def late_stress():
        differentiate_x(range(3), vel, strips[0][2], 8, 8)
        memory_in.wait()
        wait_x(0, 8, 16)
        stress_rows(8, 16, 2, (1, NZ // 2 - 1))
        wait_z(0, 8, 16)
        stress_rows(8, 16, 2, (0, 2), NZ // 2 - 1)
        stress_beside(1)

    for part, low, first, outer in strips:
        if part == 2:
            when(at_gap, early_stress)
        when(low & y_low, lambda: arrived(terrain.at[:, 0:8, :], edge_recv.at[0]))
        when(~low & y_high & ~before_gap, lambda: arrived(terrain.at[:, 40:48, :], edge_recv.at[1]))
        if part == 2:
            when(before_gap, gap_terrain_arrived)
        heights(outer)
        metrics(first, 8)
        for i, c in enumerate(Y_SENT):
            when(low & y_low, lambda: arrived(sigma.at[c, 2:18, 6:8, :], y_recv.at[0, i]))
            when(~low & y_high, lambda: arrived(sigma.at[c, 2:18, 40:42, :], y_recv.at[1, i]))
        wait_stress_z(part, (z >= 0) if part == 1 else ~after_gap)
        velocity_rows(first, 8, 4)
        when(low & y_low & ~after_gap, low_copy.start)
        when(~low & y_high, high_copy.start)
        send_rows(part, first, 8)
    differentiate_x(range(3), vel, strips[1][2], 8, 8)
    when(before_gap, gap_metrics)
    when(~at_gap, late_stress)
    when(at_gap, lambda: stress_rows(inner_far, 8, 4, (0, NZ // 4)))
    stress_beside(2)
    for condition, copy in sends:
        when(condition, copy.wait_send)


def write_out(v_in, s_in, m_in, v_ref, s_ref, m_ref, sems):
    pairs = [(v_in, v_ref, c) for c in range(3)] + [(a, b, c) for a, b in ((s_in, s_ref), (m_in, m_ref)) for c in range(6)]
    copies = [pltpu.make_async_copy(a.at[c], b.at[c], sems.at[i]) for i, (a, b, c) in enumerate(pairs)]
    for copy in copies:
        copy.start()
    for copy in copies:
        copy.wait()


def local(*arrays):
    held = [pltpu.with_memory_space_constraint(array, pltpu.HBM) for array in arrays]
    f32, vmem, dma = jnp.float32, pltpu.VMEM, pltpu.SemaphoreType.DMA
    outputs = [(n, NZ, NY, NX) for n in (3, 6, 6)]
    results = pl.pallas_call(
        kernel,
        out_shape=tuple(vmem(shape, f32) for shape in outputs),
        in_specs=[pl.BlockSpec(memory_space=pltpu.HBM)] * len(held),
        out_specs=tuple(pl.BlockSpec(memory_space=vmem) for _ in outputs),
        scratch_shapes=[
            vmem((6, 20, 48, NX), f32),
            vmem((3, 20, 48, NX), f32),
            vmem((6, 48, 32), jnp.int32),
            vmem((3, 64, NX), f32),
            vmem((3, 24, NX), f32),
            vmem((2, GZ * NZ, NX), f32),
            vmem((NZ, NY, NX), jnp.int32),
            vmem((5, 8, NX), f32),
            vmem((5, NZ, NY, NX), f32),
            vmem((NX, NX), jnp.bfloat16),
            vmem((3, NZ, NY, NX), f32),
            vmem((3, NZ, NY + 8, NX), f32),
            vmem((2, 2, NY, NX), f32),
            vmem((2, 2, NY, NX), f32),
            vmem((2, 2, NY, NX), f32),
            pltpu.SMEM((7, 16), f32),
            dma((17,)), dma((4,)), dma((4,)), dma((2, 3)), dma((2, 3)), dma((3,)), dma((4,)), dma((7,)), dma((6,)), dma((2,)), dma((2,)),
            dma((2, 3)), dma((2, 3)), dma((2, 3)), dma((2, 3)), dma((2,)), dma((2,)),
            dma((2, 3)), dma((2, 3)),
            vmem((10, NZ, 2, NX), f32),
            vmem((10, NZ, 2, NX), f32),
            dma((4,)), dma((7,)), dma((6,)),
            pltpu.SemaphoreType.REGULAR,
        ],
        compiler_params=pltpu.CompilerParams(
            collective_id=0, has_side_effects=True, vmem_limit_bytes=24 << 20
        ),
    )(*held)
    return pl.pallas_call(
        write_out,
        out_shape=tuple(jax.ShapeDtypeStruct(shape, f32) for shape in outputs),
        in_specs=[pl.BlockSpec(memory_space=vmem)] * 3,
        out_specs=tuple(pl.BlockSpec(memory_space=pltpu.HBM) for _ in outputs),
        scratch_shapes=[dma((15,))],
        compiler_params=pltpu.CompilerParams(vmem_limit_bytes=8 << 20),
    )(*results)


def solution(mesh):
    field = P(None, "gz", "gy", "gx")
    return jax.shard_map(
        local,
        mesh=mesh,
        in_specs=(
            P("gy", ("gx", "gz")), P("gz"), P("gz"), P("gz", "gy", "gx"),
            P(), P(), P(), P(), P(), field, field, field,
        ),
        out_specs=(field, field, field),
        check_vma=False,
    )
```

```python
import functools

import jax
import jax.numpy as jnp
from jax import lax
from jax.experimental import pallas as pl
from jax.experimental.pallas import tpu as pltpu
from jax.sharding import PartitionSpec as P

MESH = pl.DeviceIdType.MESH
STEP = 0.3
GX, GY, GZ = 4, 16, 4
NZ, NY, NX = 16, 32, 128
X_PARTS = (0, 3, 4)
Y_PARTS = (3, 1, 5)
Y_SENT = (1, 3, 5)


def when(condition, action):
    if condition is None:
        action()
    else:
        pl.when(condition)(lambda: action())


def centred_12(before_2, before_1, after_1, after_2):
    return 8.0 * (after_1 - before_1) - (after_2 - before_2)


def kernel(
    elevation, layer_base, stretch, material, buoyancy, lame, shear, relax, weight, velocity, stress, memory,
    v_out, s_out, m_out,
    sigma, vel, terrain, wide, surf, layers, mat, tables, props, stencil, along, metric, packs, halo_s, halo_v,
    small, local_sem, s_send, s_recv, y_send, y_recv, layer_send, layer_recv, t_send, t_recv, edge_send, edge_recv,
    z_send, z_recv, x_send, x_recv, vy_send, vy_recv, zs_send, zs_recv, gap_out, gap_in, gap_sem, pass_send, pass_recv, far_sem,
):
    x, y, z = lax.axis_index("gx"), lax.axis_index("gy"), lax.axis_index("gz")
    x_low, x_high = x > 0, x < GX - 1
    y_low, y_high = y > 0, y < GY - 1
    z_low, z_high = z > 0, z < GZ - 1
    before_gap, after_gap = y == GY // 2 - 1, y == GY // 2
    at_gap = before_gap | after_gap
    lane = lax.broadcasted_iota(jnp.int32, (8, NX), 1)

    own_slot = 1 + z
    tables_in = (buoyancy, lame, shear, relax, weight, layer_base, stretch)
    scalars = [pltpu.make_async_copy(ref, small.at[i], local_sem.at[i]) for i, ref in enumerate(tables_in)]
    for copy in scalars:
        copy.start()
    stress_in = {
        c: pltpu.make_async_copy(stress.at[c], sigma.at[c, 2:18, 8:40, :], local_sem.at[7 + c])
        for c in (0, 3, 4, 1, 2, 5)
    }
    for c in (0, 3, 4):
        stress_in[c].start()
    material_in = pltpu.make_async_copy(material, mat, local_sem.at[15])
    material_in.start()
    for c in (1, 2, 5):
        stress_in[c].start()
    elevation_in = pltpu.make_async_copy(elevation, terrain.at[own_slot, 8:40, :], local_sem.at[13])
    velocity_in = pltpu.make_async_copy(velocity, v_out, local_sem.at[14])
    memory_in = pltpu.make_async_copy(memory, m_out, local_sem.at[16])
    for copy in (elevation_in, velocity_in, memory_in):
        copy.start()

    barrier = pltpu.get_barrier_semaphore()
    beside = [(None, {"gz": (z + d) % GZ}) for d in range(1, GZ)]
    for g in range(GZ):
        beside.append((x_high & ((z == g) | (z == GZ - 1) | (g == 0)), {"gx": x + 1, "gz": g}))
        beside.append((x_low & ((z == g) | (z == 0) | (g == GZ - 1)), {"gx": x - 1, "gz": g}))
    up_y, down_y = {"gy": y + 1}, {"gy": y - 1}
    for condition, target in [(y_high, up_y), (y_low & ~after_gap, down_y)] + beside:
        when(condition, lambda target=target: pl.semaphore_signal(barrier, inc=1, device_id=target, device_id_type=MESH))
    expected = [y_low, y_high & ~before_gap] + [condition for condition, _ in beside]

    pl.semaphore_wait(barrier, sum(1 if c is None else c.astype(jnp.int32) for c in expected))
    when(after_gap, lambda: pl.semaphore_signal(far_sem, inc=1, device_id=down_y, device_id_type=MESH))

    def remote(source, to, send, recv, target):
        return pltpu.make_async_remote_copy(
            src_ref=source, dst_ref=to, send_sem=send, recv_sem=recv, device_id=target, device_id_type=MESH
        )

    sends = []

    def send(condition, copy, now=True):
        sends.append((condition, copy))
        if now:
            when(condition, copy.start)
        return copy

    for d in range(1, GZ):
        send(None, remote(elevation, terrain.at[own_slot, 8:40, :], t_send.at[d - 1], t_recv.at[own_slot], {"gz": (z + d) % GZ}))
    for g in range(GZ):
        send(x_high & (z == GZ - 1), remote(elevation, terrain.at[0, 8:40, :], t_send.at[3 + g], t_recv.at[0], {"gx": x + 1, "gz": g}))
        send(x_low & (z == 0), remote(elevation, terrain.at[5, 8:40, :], t_send.at[3 + g], t_recv.at[5], {"gx": x - 1, "gz": g}))
    gap_terrain = terrain.at[own_slot, 40:48, :]
    send(after_gap, remote(elevation.at[0:8, :], gap_terrain, gap_sem.at[2], gap_sem.at[3], down_y))
    up_copies = [
        send(y_high, remote(stress.at[c, :, 30:32, :], sigma.at[c, 2:18, 6:8, :], y_send.at[0, i], y_recv.at[0, i], up_y), now=False)
        for i, c in enumerate(Y_SENT)
    ]

    def start_up():
        for copy in up_copies:
            copy.start()

    when(y_high & ~before_gap, start_up)
    for i, c in enumerate(Y_SENT):
        send(y_low, remote(stress.at[c, :, 0:2, :], sigma.at[c, 2:18, 40:42, :], y_send.at[1, i], y_recv.at[1, i], down_y))
    odd = y % 2
    strips = []
    for part in (1, 2):
        low = (odd == 1) if part == 1 else (odd == 0)
        side = odd if part == 1 else 1 - odd
        strips.append((part, low, pl.multiple_of(24 - 24 * side, 8), pl.multiple_of(40 - 40 * side, 8)))
    z_parts = [(0, 8, 16)] + [(part, first, 8) for part, _, first, _ in strips]
    z_copies = []
    for part, first, rows in z_parts:
        at, to = pl.ds(first, rows), pl.ds(8 + first, rows)
        z_copies.append((
            send(z_high, remote(stress.at[:, 14:16, at, :], sigma.at[:, 0:2, to, :], zs_send.at[0, part], zs_recv.at[0, part], {"gz": z + 1}), now=False),
            send(z_low, remote(stress.at[:, 0:2, at, :], sigma.at[:, 18:20, to, :], zs_send.at[1, part], zs_recv.at[1, part], {"gz": z - 1}), now=False),
        ))

    def start_z(part, condition):
        when(z_high if condition is None else condition & z_high, z_copies[part][0].start)
        when(z_low if condition is None else condition & z_low, z_copies[part][1].start)

    start_z(2, at_gap)
    start_z(0, None)
    start_z(1, None)
    start_z(2, ~at_gap)

    zero = jnp.zeros((8, NX), jnp.float32)

    def pack_spot(k, i):
        at = 4 * (k + (NZ if i == 1 else 0))
        return at, (lane >= at) & (lane < at + 4)

    def pack_layer(held, blocks, i, k, at, spot):
        for r, block in enumerate(blocks):
            j = len(blocks) * (i // 2) + r
            held[j] = jnp.where(spot, pltpu.roll(block, at + 2, 1), held[j])

    def pack_stress(step, held):
        held = list(held)
        for k in (2 * step, 2 * step + 1):
            for i, c in enumerate(X_PARTS):
                at, spot = pack_spot(k, i)
                pack_layer(held, [sigma[c, 2 + k, 8 + 8 * r : 16 + 8 * r, :] for r in range(4)], i, k, at, spot)
        return tuple(held)

    for copy in scalars:
        copy.wait()
    for k in range(NZ):
        for row in range(2):
            layers[row, pl.ds(NZ * z + k, 1), :] = jnp.full((1, NX), small[5 + row, k], jnp.float32)

    for c in X_PARTS:
        stress_in[c].wait()
    held = lax.fori_loop(0, NZ // 2, pack_stress, (zero,) * 8)
    for j in range(8):
        packs[0, j // 4, 8 * (j % 4) : 8 * (j % 4) + 8, :] = held[j]

    mine = pl.ds(NZ * z, NZ)
    for d in range(1, GZ):
        send(None, remote(layers.at[:, mine, :], layers.at[:, mine, :], layer_send.at[d - 1], layer_recv.at[z], {"gz": (z + d) % GZ}))
    columns = []
    for i in range(5):
        column = zero
        for block_id in range(16):
            column = jnp.where(lane == block_id, small[i, block_id], column)
        columns.append(column)
    keep = jnp.exp(-STEP / jnp.where(lane < 16, columns[3], 1.0))
    tables[0] = columns[0] * (STEP / 12.0)
    tables[1] = columns[1] * (1.0 / 12.0)
    tables[2] = columns[2] * (1.0 / 12.0)
    tables[3] = keep
    tables[4] = (1.0 - keep) * columns[4]

    send(x_high, remote(packs.at[0], halo_s.at[0], s_send.at[0], s_recv.at[0], {"gx": x + 1}))
    send(x_low, remote(packs.at[0], halo_s.at[1], s_send.at[1], s_recv.at[1], {"gx": x - 1}))
    material_in.wait()

    def property_layer(k, carry):
        for r in range(4):
            rows = slice(8 * r, 8 * r + 8)
            block_id = mat[k, rows, :]
            for i in range(5):
                props[i, k, rows, :] = jnp.take_along_axis(tables[i], block_id, axis=1)
        return carry

    lax.fori_loop(0, NZ, property_layer, 0)

    offset = lax.broadcasted_iota(jnp.int32, (NX, NX), 0) - lax.broadcasted_iota(jnp.int32, (NX, NX), 1)
    weights = jnp.zeros((NX, NX), jnp.float32)
    for distance, factor in ((-2, 1.0), (-1, -8.0), (1, 8.0), (2, -1.0)):
        weights = jnp.where(offset == distance, factor, weights)
    stencil[...] = weights.astype(jnp.bfloat16)

    def differentiate_x(parts, field, first, rows, unroll):
        def layers_of(step, carry):
            spots = [(i, c, unroll * step + n) for i, c in enumerate(parts) for n in range(unroll)]
            rest = jnp.concatenate([field[c, k + 2, pl.ds(8 + first, rows), :] for _, c, k in spots], axis=0)
            total = None
            for _ in range(3):
                piece = rest.astype(jnp.bfloat16)
                rest = rest - piece.astype(jnp.float32)
                product = jnp.dot(piece, stencil[...], preferred_element_type=jnp.float32)
                total = product if total is None else total + product
            for n, (i, _, k) in enumerate(spots):
                along[i, k, pl.ds(first, rows), :] = total[n * rows : (n + 1) * rows]
            return carry

        lax.fori_loop(0, NZ // unroll, layers_of, 0)

    differentiate_x(X_PARTS, sigma, 0, NY, 4)

    def arrived(ref, recv):
        remote(ref, ref, s_send.at[0], recv, {"gz": z}).wait_recv()

    def zero_z(first):
        sigma[:, pl.ds(first, 2), 8:40, :] = jnp.zeros((6, 2, NY, NX), jnp.float32)
        vel[:, pl.ds(first, 2), 8:40, :] = jnp.zeros((3, 2, NY, NX), jnp.float32)

    def zero_y(first):
        def layer(k, carry):
            for c in Y_SENT:
                sigma[c, 2 + k, first : first + 8, :] = zero
            for c in range(3):
                vel[c, 2 + k, first : first + 8, :] = zero
            return carry

        lax.fori_loop(0, NZ, layer, 0)
        for m in range(6):
            terrain[m, first : first + 8, :] = jnp.zeros((8, 32), jnp.int32)

    def zero_x(side, slot):
        halo_s[side] = jnp.zeros((2, NY, NX), jnp.float32)
        halo_v[side] = jnp.zeros((2, NY, NX), jnp.float32)
        terrain[slot, 8:40, :] = jnp.zeros((32, 32), jnp.int32)

        def zero_top():
            terrain[slot, 40:48, :] = jnp.zeros((8, 32), jnp.int32)

        when(before_gap, zero_top)

    when(z == 0, lambda: zero_z(0))
    when(z == GZ - 1, lambda: zero_z(18))
    when(y == 0, lambda: zero_y(0))
    when(y == GY - 1, lambda: zero_y(40))
    when(x == 0, lambda: zero_x(0, 0))
    when(x == GX - 1, lambda: zero_x(1, 5))

    def d_k(field, c, k, first, rows):
        return centred_12(*[field[c, k + 2 + d, pl.ds(8 + first, rows), :] for d in (-2, -1, 1, 2)])

    def d_y(field, c, k, first, rows):
        return centred_12(*[field[c, k + 2, pl.ds(8 + first + d, rows), :] for d in (-2, -1, 1, 2)])

    def d_x(c, k, first, rows, halo, i):
        side = lax.broadcasted_iota(jnp.int32, (rows, NX), 1)
        at = 4 * (k + (NZ if i == 1 else 0))
        fix = pltpu.roll(halo[0, i // 2, pl.ds(first, rows), :], 126 - at, 1)
        return along[i, k, pl.ds(first, rows), :] + jnp.where((side < 2) | (side >= 126), fix, 0.0)

    def join(halo, first, rows):
        spot = lax.broadcasted_iota(jnp.int32, (rows, NX), 1) % 4
        at = pl.ds(first, rows)
        for i in range(2):
            change = jnp.where(spot < 2, halo[0, i, at, :], halo[1, i, at, :])
            low = 8.0 * jnp.where(spot == 1, pltpu.roll(change, 127, 1), 0.0) - pltpu.roll(change, 126, 1)
            high = pltpu.roll(change, 2, 1) - 8.0 * jnp.where(spot == 2, pltpu.roll(change, 1, 1), 0.0)
            halo[0, i, at, :] = jnp.where(spot < 2, low, high)

    for copy in (stress_in[1], stress_in[2], stress_in[5], velocity_in):
        copy.wait()
    when(x_low, lambda: arrived(halo_s.at[0], s_recv.at[0]))
    when(x_high, lambda: arrived(halo_s.at[1], s_recv.at[1]))
    join(halo_s, 0, NY)
    def wait_stress_z(part, condition):
        _, first, rows = z_parts[part]
        to = pl.ds(8 + first, rows)
        when(condition & z_low, lambda: arrived(sigma.at[:, 0:2, to, :], zs_recv.at[0, part]))
        when(condition & z_high, lambda: arrived(sigma.at[:, 18:20, to, :], zs_recv.at[1, part]))

    gap_down = remote(gap_out, gap_in, gap_sem.at[0], gap_sem.at[1], down_y)
    gap_up = remote(gap_out, gap_in, gap_sem.at[0], gap_sem.at[1], up_y)
    sends.append((after_gap, gap_down))
    sends.append((before_gap, gap_up))

    def gap_package(first, kept):
        row = lax.broadcasted_iota(jnp.int32, (8, NX), 0)

        def layers_of(step, carry):
            for k in (2 * step, 2 * step + 1):
                scale = props[0, k, first : first + 8, :]
                for c in range(6):
                    gap_out[3 + c, k] = (scale * d_k(sigma, c, k, first, 8))[kept]
                gap_out[9, k] = scale[kept]
                for i, (c_x, c_y) in enumerate(zip(X_PARTS, Y_PARTS)):
                    if first == 0:
                        here, beside_1, beside_2 = (sigma[c_y, k + 2, 8 + d : 16 + d, :] for d in range(3))
                        grad_y = 8.0 * (beside_1 - jnp.where(row == 0, 0.0, pltpu.roll(here, 1, 0))) - beside_2
                    else:
                        here, beside_1, beside_2 = (sigma[c_y, k + 2, 32 - d : 40 - d, :] for d in range(3))
                        grad_y = 8.0 * (jnp.where(row == 7, 0.0, pltpu.roll(here, 7, 0)) - beside_1) + beside_2
                    known = v_out[i, k, first : first + 8, :] + scale * (d_x(c_x, k, first, 8, halo_s, i) + grad_y)
                    gap_out[i, k] = known[kept]
            return carry

        lax.fori_loop(0, NZ // 2, layers_of, 0)

    def package_down():
        gap_package(0, slice(0, 2))
        gap_down.start()

    wait_stress_z(2, at_gap)
    when(after_gap, package_down)
    when(before_gap, lambda: gap_package(24, slice(6, 8)))

    elevation_in.wait()
    for d in range(1, GZ):
        g = (z + d) % GZ
        arrived(terrain.at[1 + g, 8:40, :], t_recv.at[1 + g])
    when(x_low, lambda: arrived(terrain.at[0, 8:40, :], t_recv.at[0]))
    when(x_high, lambda: arrived(terrain.at[5, 8:40, :], t_recv.at[5]))
    edge_up = send(y_high, remote(terrain.at[:, 32:40, :], terrain.at[:, 0:8, :], edge_send.at[0], edge_recv.at[0], up_y), now=False)
    when(y_high & ~before_gap, edge_up.start)
    send(y_low & ~after_gap, remote(terrain.at[:, 8:16, :], terrain.at[:, 40:48, :], edge_send.at[1], edge_recv.at[1], down_y))

    def heights(row):
        held = [terrain[m, pl.ds(row, 8), :].astype(jnp.float32) / 200.0 for m in range(6)]
        rows = pl.ds(row + 8, 8)
        blank = jnp.zeros((8, 96), jnp.float32)
        wide[0, rows, :] = jnp.concatenate([blank, held[0]], axis=1)
        wide[1, rows, :] = jnp.concatenate(held[1:5], axis=1)
        wide[2, rows, :] = jnp.concatenate([held[5], blank], axis=1)

    binomial = (1.0, 4.0, 6.0, 4.0, 1.0)

    def metrics(first, rows):
        along_y = []
        for part in range(3):
            total = jnp.zeros((rows + 8, NX), jnp.float32)
            for d, factor in enumerate(binomial):
                total = total + factor * wide[part, pl.ds(first + 10 + d, rows + 8), :]
            along_y.append(total / 16.0)
        row = jnp.concatenate(along_y, axis=1)
        total = jnp.zeros_like(row)
        for d, factor in enumerate(binomial):
            total = total + factor * (row if d == 2 else pltpu.roll(row, (2 - d) % 384, 1))
        total = total / 16.0
        for part in range(3):
            surf[part, 0 : rows + 8, :] = total[:, 128 * part : 128 * part + 128]
        own = jnp.concatenate([surf[part, 4 : 4 + rows, :] for part in range(3)], axis=1)
        height = own[:, 128:256]
        shifted = [pltpu.roll(own, d % 384, 1)[:, 128:256] for d in (2, 1, -1, -2)]
        slope_x = centred_12(*shifted) / 12.0
        slope_y = centred_12(*[surf[1, 4 + d : 4 + d + rows, :] for d in (-2, -1, 1, 2)]) / 12.0

        def above(step, total):
            for layer in [4 * step + i for i in range(4)]:
                base, follow = layers[0, pl.ds(layer, 1), :], layers[1, pl.ds(layer, 1), :]
                total = total + follow * (base * jnp.exp(follow * height))
            return total

        upper = lax.fori_loop(0, (NZ // 4) * z, above, jnp.zeros((rows, NX), jnp.float32))

        def layer(step, total):
            for k in [4 * step + i for i in range(4)]:
                base, follow = layers[0, pl.ds(NZ * z + k, 1), :], layers[1, pl.ds(NZ * z + k, 1), :]
                thickness = base * jnp.exp(follow * height)
                weighted = follow * thickness
                inverse = 1.0 / thickness
                factor = (total + 0.5 * weighted - 1.0) * inverse
                at = pl.ds(8 + first, rows)
                metric[0, k, at, :] = slope_x * factor
                metric[1, k, at, :] = slope_y * factor
                metric[2, k, at, :] = inverse
                total = total + weighted
            return total

        lax.fori_loop(0, NZ // 4, layer, upper)

    def velocity_rows(first, rows, unroll):
        blocks = rows // 8

        def velocity_layer(step, carried):
            held, last = list(carried[0]), carried[1]
            at = pl.ds(first, rows)
            ks = [unroll * step + i for i in range(unroll)]
            pack_rows(held, [k - unroll for k in ks], last)
            made = []
            for k in ks:
                m_x, m_y, m_z = (metric[i, k, pl.ds(8 + first, rows), :] for i in range(3))
                grad_k = [d_k(sigma, c, k, first, rows) for c in range(6)]
                grad_x = [d_x(c, k, first, rows, halo_s, i) for i, c in enumerate(X_PARTS)]
                grad_y = [d_y(sigma, c, k, first, rows) for c in Y_PARTS]
                scale = props[0, k, at, :]
                row = []
                for c, (a, b, d) in enumerate(((0, 3, 4), (3, 1, 5), (4, 5, 2))):
                    accel = (grad_x[c] - m_x * grad_k[a]) + (grad_y[c] - m_y * grad_k[b]) + m_z * grad_k[d]
                    new = v_out[c, k, at, :] + scale * accel
                    v_out[c, k, at, :] = new
                    vel[c, 2 + k, pl.ds(8 + first, rows), :] = new
                    row.append(new)
                made.append(row)
            return tuple(held), made

        def pack_rows(held, ks, made):
            for k, row in zip(ks, made):
                for c in range(3):
                    spot_at, spot = pack_spot(k, c)
                    pack_layer(held, [row[c][8 * r : 8 * r + 8] for r in range(blocks)], c, k, spot_at, spot)

        nothing = jnp.zeros((rows, NX), jnp.float32)
        start = ((zero,) * (2 * blocks), [[nothing] * 3 for _ in range(unroll)])
        held, last = lax.fori_loop(0, NZ // unroll, velocity_layer, start)
        held = list(held)
        pack_rows(held, range(NZ - unroll, NZ), last)
        for j in range(2 * blocks):
            packs[1, j // blocks, pl.ds(first + 8 * (j % blocks), 8), :] = held[j]

    def send_rows(part, first, rows):
        at = pl.ds(first, rows)
        send(x_high, remote(packs.at[1, :, at, :], halo_v.at[0, :, at, :], x_send.at[0, part], x_recv.at[0, part], {"gx": x + 1}))
        send(x_low, remote(packs.at[1, :, at, :], halo_v.at[1, :, at, :], x_send.at[1, part], x_recv.at[1, part], {"gx": x - 1}))
        at = pl.ds(8 + first, rows)
        send(z_high, remote(vel.at[:, 16:18, at, :], vel.at[:, 0:2, at, :], z_send.at[0, part], z_recv.at[0, part], {"gz": z + 1}))
        send(z_low, remote(vel.at[:, 2:4, at, :], vel.at[:, 18:20, at, :], z_send.at[1, part], z_recv.at[1, part], {"gz": z - 1}))

    def wait_x(part, first, rows):
        at = pl.ds(first, rows)
        when(x_low, lambda: arrived(halo_v.at[0, :, at, :], x_recv.at[0, part]))
        when(x_high, lambda: arrived(halo_v.at[1, :, at, :], x_recv.at[1, part]))
        join(halo_v, first, rows)

    def wait_z(part, first, rows):
        at = pl.ds(8 + first, rows)
        when(z_low, lambda: arrived(vel.at[:, 0:2, at, :], z_recv.at[0, part]))
        when(z_high, lambda: arrived(vel.at[:, 18:20, at, :], z_recv.at[1, part]))

    for row in range(8, 40, 8):
        heights(row)
    for d in range(1, GZ):
        g = (z + d) % GZ
        arrived(layers.at[:, pl.ds(NZ * g, NZ), :], layer_recv.at[g])
    metrics(8, 16)

    def start_far():
        pl.semaphore_wait(far_sem, 1)
        edge_up.start()
        start_up()
        gap_up.start()

    def gap_velocity(row, own):
        arrived(gap_in, gap_sem.at[1])

        def layers_of(step, carry):
            for k in (2 * step, 2 * step + 1):
                m_x, m_y, m_z = (metric[i, k, 8 + row : 10 + row, :] for i in range(3))
                for i, (a, b, d) in enumerate(((0, 3, 4), (3, 1, 5), (4, 5, 2))):
                    edge = sigma[Y_PARTS[i], k + 2, 8 + own : 10 + own, :]
                    if own:
                        beyond = jnp.concatenate([edge[0:1] - 8.0 * edge[1:2], edge[1:2]], axis=0)
                    else:
                        beyond = jnp.concatenate([-edge[0:1], 8.0 * edge[0:1] - edge[1:2]], axis=0)
                    known = gap_in[i, k] + gap_in[9, k] * beyond
                    new = known - m_x * gap_in[3 + a, k] - m_y * gap_in[3 + b, k] + m_z * gap_in[3 + d, k]
                    vel[i, 2 + k, 8 + row : 10 + row, :] = new
            return carry

        lax.fori_loop(0, NZ // 2, layers_of, 0)

    def gap_metrics(first, blank):
        for part in range(3):
            wide[part, blank, :] = jnp.zeros((8, NX), jnp.float32)
        metrics(first, 8)

    wait_stress_z(0, z >= 0)
    velocity_rows(8, 16, 2)
    send_rows(0, 8, 16)
    differentiate_x(range(3), vel, 8, 16, 4)
    when(before_gap, start_far)
    when(before_gap, lambda: arrived(gap_terrain, gap_sem.at[3]))
    for d in range(1, GZ):
        send(before_gap, remote(gap_terrain, gap_terrain, pass_send.at[d - 1], pass_recv.at[own_slot], {"gz": (z + d) % GZ}))
    for g in range(GZ):
        send(before_gap & x_high & (z == GZ - 1), remote(gap_terrain, terrain.at[0, 40:48, :], pass_send.at[3 + g], pass_recv.at[0], {"gx": x + 1, "gz": g}))
        send(before_gap & x_low & (z == 0), remote(gap_terrain, terrain.at[5, 40:48, :], pass_send.at[3 + g], pass_recv.at[5], {"gx": x - 1, "gz": g}))

    def gap_terrain_arrived():
        for d in range(1, GZ):
            slot = 1 + (z + d) % GZ
            arrived(terrain.at[slot, 40:48, :], pass_recv.at[slot])
        when(x_low, lambda: arrived(terrain.at[0, 40:48, :], pass_recv.at[0]))
        when(x_high, lambda: arrived(terrain.at[5, 40:48, :], pass_recv.at[5]))

    low_copy = remote(vel.at[:, 2:18, 8:10, :], vel.at[:, 2:18, 40:42, :], vy_send.at[1], vy_recv.at[1], down_y)
    high_copy = remote(vel.at[:, 2:18, 38:40, :], vel.at[:, 2:18, 6:8, :], vy_send.at[0], vy_recv.at[0], up_y)
    sends.append((y_low & ~after_gap, low_copy))
    sends.append((y_high & ~before_gap, high_copy))

    def stress_rows(first, rows, unroll, steps, stride=1):
        at = pl.ds(first, rows)

        def stress_layer(step, carry):
            for k in [unroll * stride * step + i for i in range(unroll)]:
                grad_x = [d_x(c, k, first, rows, halo_v, c) for c in range(3)]
                m_x, m_y, m_z = (metric[i, k, pl.ds(8 + first, rows), :] for i in range(3))
                along_k = [d_k(vel, c, k, first, rows) for c in range(3)]
                along_x = [grad_x[c] - m_x * along_k[c] for c in range(3)]
                along_y = [d_y(vel, c, k, first, rows) - m_y * along_k[c] for c in range(3)]
                along_z = [m_z * along_k[c] for c in range(3)]
                lam, mu, kept, gain = (props[i, k, at, :] for i in range(1, 5))
                volume = lam * (along_x[0] + along_y[1] + along_z[2])
                twice = mu + mu
                rates = (
                    volume + twice * along_x[0],
                    volume + twice * along_y[1],
                    volume + twice * along_z[2],
                    mu * (along_y[0] + along_x[1]),
                    mu * (along_z[0] + along_x[2]),
                    mu * (along_z[1] + along_y[2]),
                )
                for c, rate in enumerate(rates):
                    new = kept * m_out[c, k, at, :] + gain * rate
                    m_out[c, k, at, :] = new
                    s_out[c, k, at, :] = sigma[c, 2 + k, pl.ds(8 + first, rows), :] + STEP * (rate - new)
            return carry

        lax.fori_loop(steps[0], steps[1], stress_layer, 0)

    def stress_beside(part):
        _, low, first, _ = strips[part - 1]
        wait_x(part, first, 8)
        wait_z(part, first, 8)
        when(low & y_low & ~after_gap, lambda: arrived(vel.at[:, 2:18, 6:8, :], vy_recv.at[0]))
        when(~low & y_high & ~before_gap, lambda: arrived(vel.at[:, 2:18, 40:42, :], vy_recv.at[1]))
        if part == 2:
            when(before_gap, lambda: gap_velocity(NY, NY - 2))
            when(after_gap, lambda: gap_velocity(-2, 0))
        stress_rows(first, 8, 4, (0, NZ // 4))

    inner_near = pl.multiple_of(16 - 8 * odd, 8)
    inner_far = pl.multiple_of(8 + 8 * odd, 8)

    def early_stress():
        differentiate_x(range(3), vel, strips[0][2], 8, 8)
        memory_in.wait()
        wait_x(0, 8, 16)
        wait_z(0, 8, 16)
        stress_rows(inner_near, 8, 4, (0, NZ // 4))
        stress_beside(1)

    def late_stress():
        differentiate_x(range(3), vel, strips[0][2], 8, 8)
        memory_in.wait()
        wait_x(0, 8, 16)
        stress_rows(8, 16, 2, (1, NZ // 2 - 1))
        wait_z(0, 8, 16)
        stress_rows(8, 16, 2, (0, 2), NZ // 2 - 1)
        stress_beside(1)

    for part, low, first, outer in strips:
        if part == 2:
            when(at_gap, early_stress)
        when(low & y_low, lambda: arrived(terrain.at[:, 0:8, :], edge_recv.at[0]))
        when(~low & y_high & ~before_gap, lambda: arrived(terrain.at[:, 40:48, :], edge_recv.at[1]))
        if part == 2:
            when(before_gap, gap_terrain_arrived)
        heights(outer)
        metrics(first, 8)
        for i, c in enumerate(Y_SENT):
            when(low & y_low, lambda: arrived(sigma.at[c, 2:18, 6:8, :], y_recv.at[0, i]))
            when(~low & y_high, lambda: arrived(sigma.at[c, 2:18, 40:42, :], y_recv.at[1, i]))
        wait_stress_z(part, (z >= 0) if part == 1 else ~at_gap)
        velocity_rows(first, 8, 4)
        when(low & y_low & ~after_gap, low_copy.start)
        when(~low & y_high & ~before_gap, high_copy.start)
        send_rows(part, first, 8)
    differentiate_x(range(3), vel, strips[1][2], 8, 8)
    when(before_gap, lambda: gap_metrics(NY, slice(56, 64)))
    when(after_gap, lambda: gap_metrics(-8, slice(0, 8)))
    when(~at_gap, late_stress)
    when(at_gap, lambda: stress_rows(inner_far, 8, 4, (0, NZ // 4)))
    stress_beside(2)
    for condition, copy in sends:
        when(condition, copy.wait_send)


def write_out(v_in, s_in, m_in, v_ref, s_ref, m_ref, sems):
    pairs = [(v_in, v_ref, c) for c in range(3)] + [(a, b, c) for a, b in ((s_in, s_ref), (m_in, m_ref)) for c in range(6)]
    copies = [pltpu.make_async_copy(a.at[c], b.at[c], sems.at[i]) for i, (a, b, c) in enumerate(pairs)]
    for copy in copies:
        copy.start()
    for copy in copies:
        copy.wait()


def local(*arrays):
    held = [pltpu.with_memory_space_constraint(array, pltpu.HBM) for array in arrays]
    f32, vmem, dma = jnp.float32, pltpu.VMEM, pltpu.SemaphoreType.DMA
    outputs = [(n, NZ, NY, NX) for n in (3, 6, 6)]
    results = pl.pallas_call(
        kernel,
        out_shape=tuple(vmem(shape, f32) for shape in outputs),
        in_specs=[pl.BlockSpec(memory_space=pltpu.HBM)] * len(held),
        out_specs=tuple(pl.BlockSpec(memory_space=vmem) for _ in outputs),
        scratch_shapes=[
            vmem((6, 20, 48, NX), f32),
            vmem((3, 20, 48, NX), f32),
            vmem((6, 48, 32), jnp.int32),
            vmem((3, 64, NX), f32),
            vmem((3, 24, NX), f32),
            vmem((2, GZ * NZ, NX), f32),
            vmem((NZ, NY, NX), jnp.int32),
            vmem((5, 8, NX), f32),
            vmem((5, NZ, NY, NX), f32),
            vmem((NX, NX), jnp.bfloat16),
            vmem((3, NZ, NY, NX), f32),
            vmem((3, NZ, NY + 16, NX), f32),
            vmem((2, 2, NY, NX), f32),
            vmem((2, 2, NY, NX), f32),
            vmem((2, 2, NY, NX), f32),
            pltpu.SMEM((7, 16), f32),
            dma((17,)), dma((4,)), dma((4,)), dma((2, 3)), dma((2, 3)), dma((3,)), dma((4,)), dma((7,)), dma((6,)), dma((2,)), dma((2,)),
            dma((2, 3)), dma((2, 3)), dma((2, 3)), dma((2, 3)), dma((2,)), dma((2,)),
            dma((2, 3)), dma((2, 3)),
            vmem((10, NZ, 2, NX), f32),
            vmem((10, NZ, 2, NX), f32),
            dma((4,)), dma((7,)), dma((6,)),
            pltpu.SemaphoreType.REGULAR,
        ],
        compiler_params=pltpu.CompilerParams(
            collective_id=0, has_side_effects=True, vmem_limit_bytes=24 << 20
        ),
    )(*held)
    return pl.pallas_call(
        write_out,
        out_shape=tuple(jax.ShapeDtypeStruct(shape, f32) for shape in outputs),
        in_specs=[pl.BlockSpec(memory_space=vmem)] * 3,
        out_specs=tuple(pl.BlockSpec(memory_space=pltpu.HBM) for _ in outputs),
        scratch_shapes=[dma((15,))],
        compiler_params=pltpu.CompilerParams(vmem_limit_bytes=8 << 20),
    )(*results)


def solution(mesh):
    field = P(None, "gz", "gy", "gx")
    return jax.shard_map(
        local,
        mesh=mesh,
        in_specs=(
            P("gy", ("gx", "gz")), P("gz"), P("gz"), P("gz", "gy", "gx"),
            P(), P(), P(), P(), P(), field, field, field,
        ),
        out_specs=(field, field, field),
        check_vma=False,
    )
```

```python
import functools

import jax
import jax.numpy as jnp
from jax import lax
from jax.experimental import pallas as pl
from jax.experimental.pallas import tpu as pltpu
from jax.sharding import PartitionSpec as P

MESH = pl.DeviceIdType.MESH
STEP = 0.3
GX, GY, GZ = 4, 16, 4
NZ, NY, NX = 16, 32, 128
X_PARTS = (0, 3, 4)
Y_PARTS = (3, 1, 5)
Y_SENT = (1, 3, 5)


def when(condition, action):
    if condition is None:
        action()
    else:
        pl.when(condition)(lambda: action())


def centred_12(before_2, before_1, after_1, after_2):
    return 8.0 * (after_1 - before_1) - (after_2 - before_2)


def kernel(
    elevation, layer_base, stretch, material, buoyancy, lame, shear, relax, weight, velocity, stress, memory,
    v_out, s_out, m_out,
    sigma, vel, terrain, wide, surf, layers, mat, tables, props, stencil, along, metric, packs, halo_s, halo_v,
    small, local_sem, s_send, s_recv, y_send, y_recv, layer_send, layer_recv, t_send, t_recv, edge_send, edge_recv,
    z_send, z_recv, x_send, x_recv, vy_send, vy_recv, zs_send, zs_recv, gap_out, gap_in, gap_sem, pass_send, pass_recv, far_sem,
):
    x, y, z = lax.axis_index("gx"), lax.axis_index("gy"), lax.axis_index("gz")
    x_low, x_high = x > 0, x < GX - 1
    y_low, y_high = y > 0, y < GY - 1
    z_low, z_high = z > 0, z < GZ - 1
    before_gap, after_gap = y == GY // 2 - 1, y == GY // 2
    at_gap = before_gap | after_gap
    lane = lax.broadcasted_iota(jnp.int32, (8, NX), 1)

    own_slot = 1 + z
    tables_in = (buoyancy, lame, shear, relax, weight, layer_base, stretch)
    scalars = [pltpu.make_async_copy(ref, small.at[i], local_sem.at[i]) for i, ref in enumerate(tables_in)]
    for copy in scalars:
        copy.start()
    stress_in = {
        c: pltpu.make_async_copy(stress.at[c], sigma.at[c, 2:18, 8:40, :], local_sem.at[7 + c])
        for c in (0, 3, 4, 1, 2, 5)
    }
    for c in (0, 3, 4):
        stress_in[c].start()
    material_in = pltpu.make_async_copy(material, mat, local_sem.at[15])
    material_in.start()
    for c in (1, 2, 5):
        stress_in[c].start()
    elevation_in = pltpu.make_async_copy(elevation, terrain.at[own_slot, 8:40, :], local_sem.at[13])
    velocity_in = pltpu.make_async_copy(velocity, v_out, local_sem.at[14])
    memory_in = pltpu.make_async_copy(memory, m_out, local_sem.at[16])
    for copy in (elevation_in, velocity_in, memory_in):
        copy.start()

    barrier = pltpu.get_barrier_semaphore()
    beside = [(None, {"gz": (z + d) % GZ}) for d in range(1, GZ)]
    for g in range(GZ):
        beside.append((x_high & ((z == g) | (z == GZ - 1) | (g == 0)), {"gx": x + 1, "gz": g}))
        beside.append((x_low & ((z == g) | (z == 0) | (g == GZ - 1)), {"gx": x - 1, "gz": g}))
    up_y, down_y = {"gy": y + 1}, {"gy": y - 1}
    for condition, target in [(y_high, up_y), (y_low & ~after_gap, down_y)] + beside:
        when(condition, lambda target=target: pl.semaphore_signal(barrier, inc=1, device_id=target, device_id_type=MESH))
    expected = [y_low, y_high & ~before_gap] + [condition for condition, _ in beside]

    pl.semaphore_wait(barrier, sum(1 if c is None else c.astype(jnp.int32) for c in expected))
    when(after_gap, lambda: pl.semaphore_signal(far_sem, inc=1, device_id=down_y, device_id_type=MESH))

    def remote(source, to, send, recv, target):
        return pltpu.make_async_remote_copy(
            src_ref=source, dst_ref=to, send_sem=send, recv_sem=recv, device_id=target, device_id_type=MESH
        )

    sends = []

    def send(condition, copy, now=True):
        sends.append((condition, copy))
        if now:
            when(condition, copy.start)
        return copy

    for d in range(1, GZ):
        send(None, remote(elevation, terrain.at[own_slot, 8:40, :], t_send.at[d - 1], t_recv.at[own_slot], {"gz": (z + d) % GZ}))
    for g in range(GZ):
        send(x_high & (z == GZ - 1), remote(elevation, terrain.at[0, 8:40, :], t_send.at[3 + g], t_recv.at[0], {"gx": x + 1, "gz": g}))
        send(x_low & (z == 0), remote(elevation, terrain.at[5, 8:40, :], t_send.at[3 + g], t_recv.at[5], {"gx": x - 1, "gz": g}))
    gap_terrain = terrain.at[own_slot, 40:48, :]
    send(after_gap, remote(elevation.at[0:8, :], gap_terrain, gap_sem.at[2], gap_sem.at[3], down_y))
    up_copies = [
        send(y_high, remote(stress.at[c, :, 30:32, :], sigma.at[c, 2:18, 6:8, :], y_send.at[0, i], y_recv.at[0, i], up_y), now=False)
        for i, c in enumerate(Y_SENT)
    ]

    def start_up():
        for copy in up_copies:
            copy.start()

    when(y_high & ~before_gap, start_up)
    for i, c in enumerate(Y_SENT):
        send(y_low, remote(stress.at[c, :, 0:2, :], sigma.at[c, 2:18, 40:42, :], y_send.at[1, i], y_recv.at[1, i], down_y))
    odd = y % 2
    strips = []
    for part in (1, 2):
        low = (odd == 1) if part == 1 else (odd == 0)
        side = odd if part == 1 else 1 - odd
        strips.append((part, low, pl.multiple_of(24 - 24 * side, 8), pl.multiple_of(40 - 40 * side, 8)))
    z_parts = [(0, 8, 16)] + [(part, first, 8) for part, _, first, _ in strips]
    z_copies = []
    for part, first, rows in z_parts:
        at, to = pl.ds(first, rows), pl.ds(8 + first, rows)
        z_copies.append((
            send(z_high, remote(stress.at[:, 14:16, at, :], sigma.at[:, 0:2, to, :], zs_send.at[0, part], zs_recv.at[0, part], {"gz": z + 1}), now=False),
            send(z_low, remote(stress.at[:, 0:2, at, :], sigma.at[:, 18:20, to, :], zs_send.at[1, part], zs_recv.at[1, part], {"gz": z - 1}), now=False),
        ))

    def start_z(part, condition):
        when(z_high if condition is None else condition & z_high, z_copies[part][0].start)
        when(z_low if condition is None else condition & z_low, z_copies[part][1].start)

    start_z(2, after_gap)
    start_z(0, None)
    start_z(1, None)
    start_z(2, ~after_gap)

    zero = jnp.zeros((8, NX), jnp.float32)

    def pack_spot(k, i):
        at = 4 * (k + (NZ if i == 1 else 0))
        return at, (lane >= at) & (lane < at + 4)

    def pack_layer(held, blocks, i, k, at, spot):
        for r, block in enumerate(blocks):
            j = len(blocks) * (i // 2) + r
            held[j] = jnp.where(spot, pltpu.roll(block, at + 2, 1), held[j])

    def pack_stress(step, held):
        held = list(held)
        for k in (2 * step, 2 * step + 1):
            for i, c in enumerate(X_PARTS):
                at, spot = pack_spot(k, i)
                pack_layer(held, [sigma[c, 2 + k, 8 + 8 * r : 16 + 8 * r, :] for r in range(4)], i, k, at, spot)
        return tuple(held)

    for copy in scalars:
        copy.wait()
    for k in range(NZ):
        for row in range(2):
            layers[row, pl.ds(NZ * z + k, 1), :] = jnp.full((1, NX), small[5 + row, k], jnp.float32)

    for c in X_PARTS:
        stress_in[c].wait()
    held = lax.fori_loop(0, NZ // 2, pack_stress, (zero,) * 8)
    for j in range(8):
        packs[0, j // 4, 8 * (j % 4) : 8 * (j % 4) + 8, :] = held[j]

    mine = pl.ds(NZ * z, NZ)
    for d in range(1, GZ):
        send(None, remote(layers.at[:, mine, :], layers.at[:, mine, :], layer_send.at[d - 1], layer_recv.at[z], {"gz": (z + d) % GZ}))
    columns = []
    for i in range(5):
        column = zero
        for block_id in range(16):
            column = jnp.where(lane == block_id, small[i, block_id], column)
        columns.append(column)
    keep = jnp.exp(-STEP / jnp.where(lane < 16, columns[3], 1.0))
    tables[0] = columns[0] * (STEP / 12.0)
    tables[1] = columns[1] * (1.0 / 12.0)
    tables[2] = columns[2] * (1.0 / 12.0)
    tables[3] = keep
    tables[4] = (1.0 - keep) * columns[4]

    send(x_high, remote(packs.at[0], halo_s.at[0], s_send.at[0], s_recv.at[0], {"gx": x + 1}))
    send(x_low, remote(packs.at[0], halo_s.at[1], s_send.at[1], s_recv.at[1], {"gx": x - 1}))
    material_in.wait()

    def property_layer(k, carry):
        for r in range(4):
            rows = slice(8 * r, 8 * r + 8)
            block_id = mat[k, rows, :]
            for i in range(5):
                props[i, k, rows, :] = jnp.take_along_axis(tables[i], block_id, axis=1)
        return carry

    lax.fori_loop(0, NZ, property_layer, 0)

    offset = lax.broadcasted_iota(jnp.int32, (NX, NX), 0) - lax.broadcasted_iota(jnp.int32, (NX, NX), 1)
    weights = jnp.zeros((NX, NX), jnp.float32)
    for distance, factor in ((-2, 1.0), (-1, -8.0), (1, 8.0), (2, -1.0)):
        weights = jnp.where(offset == distance, factor, weights)
    stencil[...] = weights.astype(jnp.bfloat16)

    def differentiate_x(parts, field, first, rows, unroll):
        def layers_of(step, carry):
            spots = [(i, c, unroll * step + n) for i, c in enumerate(parts) for n in range(unroll)]
            rest = jnp.concatenate([field[c, k + 2, pl.ds(8 + first, rows), :] for _, c, k in spots], axis=0)
            total = None
            for _ in range(3):
                piece = rest.astype(jnp.bfloat16)
                rest = rest - piece.astype(jnp.float32)
                product = jnp.dot(piece, stencil[...], preferred_element_type=jnp.float32)
                total = product if total is None else total + product
            for n, (i, _, k) in enumerate(spots):
                along[i, k, pl.ds(first, rows), :] = total[n * rows : (n + 1) * rows]
            return carry

        lax.fori_loop(0, NZ // unroll, layers_of, 0)

    differentiate_x(X_PARTS, sigma, 0, NY, 4)

    def arrived(ref, recv):
        remote(ref, ref, s_send.at[0], recv, {"gz": z}).wait_recv()

    def zero_z(first):
        sigma[:, pl.ds(first, 2), 8:40, :] = jnp.zeros((6, 2, NY, NX), jnp.float32)
        vel[:, pl.ds(first, 2), 8:40, :] = jnp.zeros((3, 2, NY, NX), jnp.float32)

    def zero_y(first):
        def layer(k, carry):
            for c in Y_SENT:
                sigma[c, 2 + k, first : first + 8, :] = zero
            for c in range(3):
                vel[c, 2 + k, first : first + 8, :] = zero
            return carry

        lax.fori_loop(0, NZ, layer, 0)
        for m in range(6):
            terrain[m, first : first + 8, :] = jnp.zeros((8, 32), jnp.int32)

    def zero_x(side, slot):
        halo_s[side] = jnp.zeros((2, NY, NX), jnp.float32)
        halo_v[side] = jnp.zeros((2, NY, NX), jnp.float32)
        terrain[slot, 8:40, :] = jnp.zeros((32, 32), jnp.int32)

        def zero_top():
            terrain[slot, 40:48, :] = jnp.zeros((8, 32), jnp.int32)

        when(before_gap, zero_top)

    when(z == 0, lambda: zero_z(0))
    when(z == GZ - 1, lambda: zero_z(18))
    when(y == 0, lambda: zero_y(0))
    when(y == GY - 1, lambda: zero_y(40))
    when(x == 0, lambda: zero_x(0, 0))
    when(x == GX - 1, lambda: zero_x(1, 5))

    def d_k(field, c, k, first, rows):
        return centred_12(*[field[c, k + 2 + d, pl.ds(8 + first, rows), :] for d in (-2, -1, 1, 2)])

    def d_y(field, c, k, first, rows):
        return centred_12(*[field[c, k + 2, pl.ds(8 + first + d, rows), :] for d in (-2, -1, 1, 2)])

    def d_x(c, k, first, rows, halo, i):
        side = lax.broadcasted_iota(jnp.int32, (rows, NX), 1)
        at = 4 * (k + (NZ if i == 1 else 0))
        fix = pltpu.roll(halo[0, i // 2, pl.ds(first, rows), :], 126 - at, 1)
        return along[i, k, pl.ds(first, rows), :] + jnp.where((side < 2) | (side >= 126), fix, 0.0)

    def join(halo, first, rows):
        spot = lax.broadcasted_iota(jnp.int32, (rows, NX), 1) % 4
        at = pl.ds(first, rows)
        for i in range(2):
            change = jnp.where(spot < 2, halo[0, i, at, :], halo[1, i, at, :])
            low = 8.0 * jnp.where(spot == 1, pltpu.roll(change, 127, 1), 0.0) - pltpu.roll(change, 126, 1)
            high = pltpu.roll(change, 2, 1) - 8.0 * jnp.where(spot == 2, pltpu.roll(change, 1, 1), 0.0)
            halo[0, i, at, :] = jnp.where(spot < 2, low, high)

    for copy in (stress_in[1], stress_in[2], stress_in[5], velocity_in):
        copy.wait()
    when(x_low, lambda: arrived(halo_s.at[0], s_recv.at[0]))
    when(x_high, lambda: arrived(halo_s.at[1], s_recv.at[1]))
    join(halo_s, 0, NY)
    def wait_stress_z(part, condition):
        _, first, rows = z_parts[part]
        to = pl.ds(8 + first, rows)
        when(condition & z_low, lambda: arrived(sigma.at[:, 0:2, to, :], zs_recv.at[0, part]))
        when(condition & z_high, lambda: arrived(sigma.at[:, 18:20, to, :], zs_recv.at[1, part]))

    gap_copy = remote(gap_out, gap_in, gap_sem.at[0], gap_sem.at[1], down_y)
    sends.append((after_gap, gap_copy))

    def gap_package():
        top = lax.broadcasted_iota(jnp.int32, (8, NX), 0) == 0

        def layers_of(step, carry):
            for k in (2 * step, 2 * step + 1):
                scale = props[0, k, 0:8, :]
                for c in range(6):
                    gap_out[3 + c, k] = (scale * d_k(sigma, c, k, 0, 8))[0:2]
                gap_out[9, k] = scale[0:2]
                for i, (c_x, c_y) in enumerate(zip(X_PARTS, Y_PARTS)):
                    here, after_1, after_2 = (sigma[c_y, k + 2, 8 + d : 16 + d, :] for d in range(3))
                    before_1 = jnp.where(top, 0.0, pltpu.roll(here, 1, 0))
                    grad_y = 8.0 * (after_1 - before_1) - after_2
                    known = v_out[i, k, 0:8, :] + scale * (d_x(c_x, k, 0, 8, halo_s, i) + grad_y)
                    gap_out[i, k] = known[0:2]
            return carry

        lax.fori_loop(0, NZ // 2, layers_of, 0)
        gap_copy.start()

    wait_stress_z(2, after_gap)
    when(after_gap, gap_package)

    elevation_in.wait()
    for d in range(1, GZ):
        g = (z + d) % GZ
        arrived(terrain.at[1 + g, 8:40, :], t_recv.at[1 + g])
    when(x_low, lambda: arrived(terrain.at[0, 8:40, :], t_recv.at[0]))
    when(x_high, lambda: arrived(terrain.at[5, 8:40, :], t_recv.at[5]))
    edge_up = send(y_high, remote(terrain.at[:, 32:40, :], terrain.at[:, 0:8, :], edge_send.at[0], edge_recv.at[0], up_y), now=False)
    when(y_high & ~before_gap, edge_up.start)
    send(y_low & ~after_gap, remote(terrain.at[:, 8:16, :], terrain.at[:, 40:48, :], edge_send.at[1], edge_recv.at[1], down_y))

    def heights(row):
        rows = pl.ds(row, 8)
        held = [terrain[m, rows, :].astype(jnp.float32) / 200.0 for m in range(6)]
        blank = jnp.zeros((8, 96), jnp.float32)
        wide[0, rows, :] = jnp.concatenate([blank, held[0]], axis=1)
        wide[1, rows, :] = jnp.concatenate(held[1:5], axis=1)
        wide[2, rows, :] = jnp.concatenate([held[5], blank], axis=1)

    binomial = (1.0, 4.0, 6.0, 4.0, 1.0)

    def metrics(first, rows):
        along_y = []
        for part in range(3):
            total = jnp.zeros((rows + 8, NX), jnp.float32)
            for d, factor in enumerate(binomial):
                total = total + factor * wide[part, pl.ds(first + 2 + d, rows + 8), :]
            along_y.append(total / 16.0)
        row = jnp.concatenate(along_y, axis=1)
        total = jnp.zeros_like(row)
        for d, factor in enumerate(binomial):
            total = total + factor * (row if d == 2 else pltpu.roll(row, (2 - d) % 384, 1))
        total = total / 16.0
        for part in range(3):
            surf[part, 0 : rows + 8, :] = total[:, 128 * part : 128 * part + 128]
        own = jnp.concatenate([surf[part, 4 : 4 + rows, :] for part in range(3)], axis=1)
        height = own[:, 128:256]
        shifted = [pltpu.roll(own, d % 384, 1)[:, 128:256] for d in (2, 1, -1, -2)]
        slope_x = centred_12(*shifted) / 12.0
        slope_y = centred_12(*[surf[1, 4 + d : 4 + d + rows, :] for d in (-2, -1, 1, 2)]) / 12.0

        def above(step, total):
            for layer in [4 * step + i for i in range(4)]:
                base, follow = layers[0, pl.ds(layer, 1), :], layers[1, pl.ds(layer, 1), :]
                total = total + follow * (base * jnp.exp(follow * height))
            return total

        upper = lax.fori_loop(0, (NZ // 4) * z, above, jnp.zeros((rows, NX), jnp.float32))

        def layer(step, total):
            for k in [4 * step + i for i in range(4)]:
                base, follow = layers[0, pl.ds(NZ * z + k, 1), :], layers[1, pl.ds(NZ * z + k, 1), :]
                thickness = base * jnp.exp(follow * height)
                weighted = follow * thickness
                inverse = 1.0 / thickness
                factor = (total + 0.5 * weighted - 1.0) * inverse
                at = pl.ds(first, rows)
                metric[0, k, at, :] = slope_x * factor
                metric[1, k, at, :] = slope_y * factor
                metric[2, k, at, :] = inverse
                total = total + weighted
            return total

        lax.fori_loop(0, NZ // 4, layer, upper)

    def velocity_rows(first, rows, unroll):
        blocks = rows // 8

        def velocity_layer(step, carried):
            held, last = list(carried[0]), carried[1]
            at = pl.ds(first, rows)
            ks = [unroll * step + i for i in range(unroll)]
            pack_rows(held, [k - unroll for k in ks], last)
            made = []
            for k in ks:
                m_x, m_y, m_z = (metric[i, k, at, :] for i in range(3))
                grad_k = [d_k(sigma, c, k, first, rows) for c in range(6)]
                grad_x = [d_x(c, k, first, rows, halo_s, i) for i, c in enumerate(X_PARTS)]
                grad_y = [d_y(sigma, c, k, first, rows) for c in Y_PARTS]
                scale = props[0, k, at, :]
                row = []
                for c, (a, b, d) in enumerate(((0, 3, 4), (3, 1, 5), (4, 5, 2))):
                    accel = (grad_x[c] - m_x * grad_k[a]) + (grad_y[c] - m_y * grad_k[b]) + m_z * grad_k[d]
                    new = v_out[c, k, at, :] + scale * accel
                    v_out[c, k, at, :] = new
                    vel[c, 2 + k, pl.ds(8 + first, rows), :] = new
                    row.append(new)
                made.append(row)
            return tuple(held), made

        def pack_rows(held, ks, made):
            for k, row in zip(ks, made):
                for c in range(3):
                    spot_at, spot = pack_spot(k, c)
                    pack_layer(held, [row[c][8 * r : 8 * r + 8] for r in range(blocks)], c, k, spot_at, spot)

        nothing = jnp.zeros((rows, NX), jnp.float32)
        start = ((zero,) * (2 * blocks), [[nothing] * 3 for _ in range(unroll)])
        held, last = lax.fori_loop(0, NZ // unroll, velocity_layer, start)
        held = list(held)
        pack_rows(held, range(NZ - unroll, NZ), last)
        for j in range(2 * blocks):
            packs[1, j // blocks, pl.ds(first + 8 * (j % blocks), 8), :] = held[j]

    def send_rows(part, first, rows):
        at = pl.ds(first, rows)
        send(x_high, remote(packs.at[1, :, at, :], halo_v.at[0, :, at, :], x_send.at[0, part], x_recv.at[0, part], {"gx": x + 1}))
        send(x_low, remote(packs.at[1, :, at, :], halo_v.at[1, :, at, :], x_send.at[1, part], x_recv.at[1, part], {"gx": x - 1}))
        at = pl.ds(8 + first, rows)
        send(z_high, remote(vel.at[:, 16:18, at, :], vel.at[:, 0:2, at, :], z_send.at[0, part], z_recv.at[0, part], {"gz": z + 1}))
        send(z_low, remote(vel.at[:, 2:4, at, :], vel.at[:, 18:20, at, :], z_send.at[1, part], z_recv.at[1, part], {"gz": z - 1}))

    def wait_x(part, first, rows):
        at = pl.ds(first, rows)
        when(x_low, lambda: arrived(halo_v.at[0, :, at, :], x_recv.at[0, part]))
        when(x_high, lambda: arrived(halo_v.at[1, :, at, :], x_recv.at[1, part]))
        join(halo_v, first, rows)

    def wait_z(part, first, rows):
        at = pl.ds(8 + first, rows)
        when(z_low, lambda: arrived(vel.at[:, 0:2, at, :], z_recv.at[0, part]))
        when(z_high, lambda: arrived(vel.at[:, 18:20, at, :], z_recv.at[1, part]))

    for row in range(8, 40, 8):
        heights(row)
    for d in range(1, GZ):
        g = (z + d) % GZ
        arrived(layers.at[:, pl.ds(NZ * g, NZ), :], layer_recv.at[g])
    metrics(8, 16)

    def start_far():
        pl.semaphore_wait(far_sem, 1)
        edge_up.start()
        start_up()

    def gap_velocity():
        arrived(gap_in, gap_sem.at[1])

        def layers_of(step, carry):
            for k in (2 * step, 2 * step + 1):
                m_x, m_y, m_z = (metric[i, k, NY : NY + 2, :] for i in range(3))
                for i, (a, b, d) in enumerate(((0, 3, 4), (3, 1, 5), (4, 5, 2))):
                    edge = sigma[Y_PARTS[i], k + 2, 38:40, :]
                    beyond = jnp.concatenate([edge[0:1] - 8.0 * edge[1:2], edge[1:2]], axis=0)
                    known = gap_in[i, k] + gap_in[9, k] * beyond
                    vel[i, 2 + k, 40:42, :] = known - m_x * gap_in[3 + a, k] - m_y * gap_in[3 + b, k] + m_z * gap_in[3 + d, k]
            return carry

        lax.fori_loop(0, NZ // 2, layers_of, 0)

    def gap_metrics():
        for part in range(3):
            wide[part, 48:64, :] = jnp.zeros((16, NX), jnp.float32)
        metrics(NY, 8)

    when(before_gap, start_far)
    wait_stress_z(0, z >= 0)
    velocity_rows(8, 16, 2)
    send_rows(0, 8, 16)
    differentiate_x(range(3), vel, 8, 16, 4)
    when(before_gap, lambda: arrived(gap_terrain, gap_sem.at[3]))
    for d in range(1, GZ):
        send(before_gap, remote(gap_terrain, gap_terrain, pass_send.at[d - 1], pass_recv.at[own_slot], {"gz": (z + d) % GZ}))
    for g in range(GZ):
        send(before_gap & x_high & (z == GZ - 1), remote(gap_terrain, terrain.at[0, 40:48, :], pass_send.at[3 + g], pass_recv.at[0], {"gx": x + 1, "gz": g}))
        send(before_gap & x_low & (z == 0), remote(gap_terrain, terrain.at[5, 40:48, :], pass_send.at[3 + g], pass_recv.at[5], {"gx": x - 1, "gz": g}))

    def gap_terrain_arrived():
        for d in range(1, GZ):
            slot = 1 + (z + d) % GZ
            arrived(terrain.at[slot, 40:48, :], pass_recv.at[slot])
        when(x_low, lambda: arrived(terrain.at[0, 40:48, :], pass_recv.at[0]))
        when(x_high, lambda: arrived(terrain.at[5, 40:48, :], pass_recv.at[5]))

    low_copy = remote(vel.at[:, 2:18, 8:10, :], vel.at[:, 2:18, 40:42, :], vy_send.at[1], vy_recv.at[1], down_y)
    high_copy = remote(vel.at[:, 2:18, 38:40, :], vel.at[:, 2:18, 6:8, :], vy_send.at[0], vy_recv.at[0], up_y)
    sends.append((y_low & ~after_gap, low_copy))
    sends.append((y_high, high_copy))

    def stress_rows(first, rows, unroll, steps, stride=1):
        at = pl.ds(first, rows)

        def stress_layer(step, carry):
            for k in [unroll * stride * step + i for i in range(unroll)]:
                grad_x = [d_x(c, k, first, rows, halo_v, c) for c in range(3)]
                m_x, m_y, m_z = (metric[i, k, at, :] for i in range(3))
                along_k = [d_k(vel, c, k, first, rows) for c in range(3)]
                along_x = [grad_x[c] - m_x * along_k[c] for c in range(3)]
                along_y = [d_y(vel, c, k, first, rows) - m_y * along_k[c] for c in range(3)]
                along_z = [m_z * along_k[c] for c in range(3)]
                lam, mu, kept, gain = (props[i, k, at, :] for i in range(1, 5))
                volume = lam * (along_x[0] + along_y[1] + along_z[2])
                twice = mu + mu
                rates = (
                    volume + twice * along_x[0],
                    volume + twice * along_y[1],
                    volume + twice * along_z[2],
                    mu * (along_y[0] + along_x[1]),
                    mu * (along_z[0] + along_x[2]),
                    mu * (along_z[1] + along_y[2]),
                )
                for c, rate in enumerate(rates):
                    new = kept * m_out[c, k, at, :] + gain * rate
                    m_out[c, k, at, :] = new
                    s_out[c, k, at, :] = sigma[c, 2 + k, pl.ds(8 + first, rows), :] + STEP * (rate - new)
            return carry

        lax.fori_loop(steps[0], steps[1], stress_layer, 0)

    def stress_beside(part):
        _, low, first, _ = strips[part - 1]
        wait_x(part, first, 8)
        wait_z(part, first, 8)
        when(low & y_low, lambda: arrived(vel.at[:, 2:18, 6:8, :], vy_recv.at[0]))
        when(~low & y_high & ~before_gap, lambda: arrived(vel.at[:, 2:18, 40:42, :], vy_recv.at[1]))
        if part == 2:
            when(before_gap, gap_velocity)
        stress_rows(first, 8, 4, (0, NZ // 4))

    inner_near = pl.multiple_of(16 - 8 * odd, 8)
    inner_far = pl.multiple_of(8 + 8 * odd, 8)

    def early_stress():
        differentiate_x(range(3), vel, strips[0][2], 8, 8)
        memory_in.wait()
        wait_x(0, 8, 16)
        wait_z(0, 8, 16)
        stress_rows(inner_near, 8, 4, (0, NZ // 4))

    def late_stress():
        differentiate_x(range(3), vel, strips[0][2], 8, 8)
        memory_in.wait()
        wait_x(0, 8, 16)
        stress_rows(8, 16, 2, (1, NZ // 2 - 1))
        wait_z(0, 8, 16)
        stress_rows(8, 16, 2, (0, 2), NZ // 2 - 1)

    for part, low, first, outer in strips:
        if part == 2:
            when(at_gap, early_stress)
        when(low & y_low, lambda: arrived(terrain.at[:, 0:8, :], edge_recv.at[0]))
        when(~low & y_high & ~before_gap, lambda: arrived(terrain.at[:, 40:48, :], edge_recv.at[1]))
        if part == 2:
            when(before_gap, gap_terrain_arrived)
        heights(outer)
        metrics(first, 8)
        for i, c in enumerate(Y_SENT):
            when(low & y_low, lambda: arrived(sigma.at[c, 2:18, 6:8, :], y_recv.at[0, i]))
            when(~low & y_high, lambda: arrived(sigma.at[c, 2:18, 40:42, :], y_recv.at[1, i]))
        wait_stress_z(part, (z >= 0) if part == 1 else ~after_gap)
        velocity_rows(first, 8, 4)
        when(low & y_low & ~after_gap, low_copy.start)
        when(~low & y_high, high_copy.start)
        send_rows(part, first, 8)
    differentiate_x(range(3), vel, strips[1][2], 8, 8)
    when(before_gap, gap_metrics)
    when(~at_gap, late_stress)
    when(at_gap, lambda: stress_rows(inner_far, 8, 4, (0, NZ // 4)))
    stress_beside(1)
    stress_beside(2)
    for condition, copy in sends:
        when(condition, copy.wait_send)


def write_out(v_in, s_in, m_in, v_ref, s_ref, m_ref, sems):
    pairs = [(v_in, v_ref, c) for c in range(3)] + [(a, b, c) for a, b in ((s_in, s_ref), (m_in, m_ref)) for c in range(6)]
    copies = [pltpu.make_async_copy(a.at[c], b.at[c], sems.at[i]) for i, (a, b, c) in enumerate(pairs)]
    for copy in copies:
        copy.start()
    for copy in copies:
        copy.wait()


def local(*arrays):
    held = [pltpu.with_memory_space_constraint(array, pltpu.HBM) for array in arrays]
    f32, vmem, dma = jnp.float32, pltpu.VMEM, pltpu.SemaphoreType.DMA
    outputs = [(n, NZ, NY, NX) for n in (3, 6, 6)]
    results = pl.pallas_call(
        kernel,
        out_shape=tuple(vmem(shape, f32) for shape in outputs),
        in_specs=[pl.BlockSpec(memory_space=pltpu.HBM)] * len(held),
        out_specs=tuple(pl.BlockSpec(memory_space=vmem) for _ in outputs),
        scratch_shapes=[
            vmem((6, 20, 48, NX), f32),
            vmem((3, 20, 48, NX), f32),
            vmem((6, 48, 32), jnp.int32),
            vmem((3, 64, NX), f32),
            vmem((3, 24, NX), f32),
            vmem((2, GZ * NZ, NX), f32),
            vmem((NZ, NY, NX), jnp.int32),
            vmem((5, 8, NX), f32),
            vmem((5, NZ, NY, NX), f32),
            vmem((NX, NX), jnp.bfloat16),
            vmem((3, NZ, NY, NX), f32),
            vmem((3, NZ, NY + 8, NX), f32),
            vmem((2, 2, NY, NX), f32),
            vmem((2, 2, NY, NX), f32),
            vmem((2, 2, NY, NX), f32),
            pltpu.SMEM((7, 16), f32),
            dma((17,)), dma((4,)), dma((4,)), dma((2, 3)), dma((2, 3)), dma((3,)), dma((4,)), dma((7,)), dma((6,)), dma((2,)), dma((2,)),
            dma((2, 3)), dma((2, 3)), dma((2, 3)), dma((2, 3)), dma((2,)), dma((2,)),
            dma((2, 3)), dma((2, 3)),
            vmem((10, NZ, 2, NX), f32),
            vmem((10, NZ, 2, NX), f32),
            dma((4,)), dma((7,)), dma((6,)),
            pltpu.SemaphoreType.REGULAR,
        ],
        compiler_params=pltpu.CompilerParams(
            collective_id=0, has_side_effects=True, vmem_limit_bytes=24 << 20
        ),
    )(*held)
    return pl.pallas_call(
        write_out,
        out_shape=tuple(jax.ShapeDtypeStruct(shape, f32) for shape in outputs),
        in_specs=[pl.BlockSpec(memory_space=vmem)] * 3,
        out_specs=tuple(pl.BlockSpec(memory_space=pltpu.HBM) for _ in outputs),
        scratch_shapes=[dma((15,))],
        compiler_params=pltpu.CompilerParams(vmem_limit_bytes=8 << 20),
    )(*results)


def solution(mesh):
    field = P(None, "gz", "gy", "gx")
    return jax.shard_map(
        local,
        mesh=mesh,
        in_specs=(
            P("gy", ("gx", "gz")), P("gz"), P("gz"), P("gz", "gy", "gx"),
            P(), P(), P(), P(), P(), field, field, field,
        ),
        out_specs=(field, field, field),
        check_vma=False,
    )
```

```python
import functools

import jax
import jax.numpy as jnp
from jax import lax
from jax.experimental import pallas as pl
from jax.experimental.pallas import tpu as pltpu
from jax.sharding import PartitionSpec as P

MESH = pl.DeviceIdType.MESH
STEP = 0.3
GX, GY, GZ = 4, 16, 4
NZ, NY, NX = 16, 32, 128
X_PARTS = (0, 3, 4)
Y_PARTS = (3, 1, 5)
Y_SENT = (1, 3, 5)


def when(condition, action):
    if condition is None:
        action()
    else:
        pl.when(condition)(lambda: action())


def centred_12(before_2, before_1, after_1, after_2):
    return 8.0 * (after_1 - before_1) - (after_2 - before_2)


def d_k(field, c, k, first, rows):
    return centred_12(*[field[c, k + 2 + d, pl.ds(8 + first, rows), :] for d in (-2, -1, 1, 2)])


def d_y(field, c, k, first, rows):
    return centred_12(*[field[c, k + 2, pl.ds(8 + first + d, rows), :] for d in (-2, -1, 1, 2)])


def d_x_of(along, c, k, first, rows, halo, i):
    side = lax.broadcasted_iota(jnp.int32, (rows, NX), 1)
    at = 4 * (k + (NZ if i == 1 else 0))
    fix = pltpu.roll(halo[0, i // 2, pl.ds(first, rows), :], 126 - at, 1)
    return along[i, k, pl.ds(first, rows), :] + jnp.where((side < 2) | (side >= 126), fix, 0.0)


def stress_layer_of(memory, sigma, vel, along, halo_v, metric, props, k, first, rows):
    at = pl.ds(first, rows)
    grad_x = [d_x_of(along, c, k, first, rows, halo_v, c) for c in range(3)]
    m_x, m_y, m_z = (metric[i, k, at, :] for i in range(3))
    along_k = [d_k(vel, c, k, first, rows) for c in range(3)]
    along_x = [grad_x[c] - m_x * along_k[c] for c in range(3)]
    along_y = [d_y(vel, c, k, first, rows) - m_y * along_k[c] for c in range(3)]
    along_z = [m_z * along_k[c] for c in range(3)]
    lam, mu, kept, gain = (props[i, k, at, :] for i in range(1, 5))
    volume = lam * (along_x[0] + along_y[1] + along_z[2])
    twice = mu + mu
    rates = (
        volume + twice * along_x[0],
        volume + twice * along_y[1],
        volume + twice * along_z[2],
        mu * (along_y[0] + along_x[1]),
        mu * (along_z[0] + along_x[2]),
        mu * (along_z[1] + along_y[2]),
    )
    for c, rate in enumerate(rates):
        new = kept * memory[c, k, at, :] + gain * rate
        yield c, new, sigma[c, 2 + k, pl.ds(8 + first, rows), :] + STEP * (rate - new)


def kernel(
    elevation, layer_base, stretch, material, buoyancy, lame, shear, relax, weight, velocity, stress, memory,
    v_out, s_out, m_out, sigma, vel, along, halo_v, metric, props,
    terrain, wide, surf, layers, mat, tables, stencil, packs, halo_s,
    small, local_sem, s_send, s_recv, y_send, y_recv, layer_send, layer_recv, t_send, t_recv, edge_send, edge_recv,
    z_send, z_recv, x_send, x_recv, vy_send, vy_recv, zs_send, zs_recv, gap_out, gap_in, gap_sem, pass_send, pass_recv, far_sem,
):
    x, y, z = lax.axis_index("gx"), lax.axis_index("gy"), lax.axis_index("gz")
    x_low, x_high = x > 0, x < GX - 1
    y_low, y_high = y > 0, y < GY - 1
    z_low, z_high = z > 0, z < GZ - 1
    before_gap, after_gap = y == GY // 2 - 1, y == GY // 2
    at_gap = before_gap | after_gap
    lane = lax.broadcasted_iota(jnp.int32, (8, NX), 1)

    own_slot = 1 + z
    tables_in = (buoyancy, lame, shear, relax, weight, layer_base, stretch)
    scalars = [pltpu.make_async_copy(ref, small.at[i], local_sem.at[i]) for i, ref in enumerate(tables_in)]
    for copy in scalars:
        copy.start()
    stress_in = {
        c: pltpu.make_async_copy(stress.at[c], sigma.at[c, 2:18, 8:40, :], local_sem.at[7 + c])
        for c in (0, 3, 4, 1, 2, 5)
    }
    for c in (0, 3, 4):
        stress_in[c].start()
    material_in = pltpu.make_async_copy(material, mat, local_sem.at[15])
    material_in.start()
    for c in (1, 2, 5):
        stress_in[c].start()
    elevation_in = pltpu.make_async_copy(elevation, terrain.at[own_slot, 8:40, :], local_sem.at[13])
    velocity_in = pltpu.make_async_copy(velocity, v_out, local_sem.at[14])
    memory_in = pltpu.make_async_copy(memory, m_out, local_sem.at[16])
    for copy in (elevation_in, velocity_in, memory_in):
        copy.start()

    barrier = pltpu.get_barrier_semaphore()
    beside = [(None, {"gz": (z + d) % GZ}) for d in range(1, GZ)]
    for g in range(GZ):
        beside.append((x_high & ((z == g) | (z == GZ - 1) | (g == 0)), {"gx": x + 1, "gz": g}))
        beside.append((x_low & ((z == g) | (z == 0) | (g == GZ - 1)), {"gx": x - 1, "gz": g}))
    up_y, down_y = {"gy": y + 1}, {"gy": y - 1}
    for condition, target in [(y_high, up_y), (y_low & ~after_gap, down_y)] + beside:
        when(condition, lambda target=target: pl.semaphore_signal(barrier, inc=1, device_id=target, device_id_type=MESH))
    expected = [y_low, y_high & ~before_gap] + [condition for condition, _ in beside]

    pl.semaphore_wait(barrier, sum(1 if c is None else c.astype(jnp.int32) for c in expected))
    when(after_gap, lambda: pl.semaphore_signal(far_sem, inc=1, device_id=down_y, device_id_type=MESH))

    def remote(source, to, send, recv, target):
        return pltpu.make_async_remote_copy(
            src_ref=source, dst_ref=to, send_sem=send, recv_sem=recv, device_id=target, device_id_type=MESH
        )

    sends = []

    def send(condition, copy, now=True):
        sends.append((condition, copy))
        if now:
            when(condition, copy.start)
        return copy

    for d in range(1, GZ):
        send(None, remote(elevation, terrain.at[own_slot, 8:40, :], t_send.at[d - 1], t_recv.at[own_slot], {"gz": (z + d) % GZ}))
    for g in range(GZ):
        send(x_high & (z == GZ - 1), remote(elevation, terrain.at[0, 8:40, :], t_send.at[3 + g], t_recv.at[0], {"gx": x + 1, "gz": g}))
        send(x_low & (z == 0), remote(elevation, terrain.at[5, 8:40, :], t_send.at[3 + g], t_recv.at[5], {"gx": x - 1, "gz": g}))
    gap_terrain = terrain.at[own_slot, 40:48, :]
    send(after_gap, remote(elevation.at[0:8, :], gap_terrain, gap_sem.at[2], gap_sem.at[3], down_y))
    up_copies = [
        send(y_high, remote(stress.at[c, :, 30:32, :], sigma.at[c, 2:18, 6:8, :], y_send.at[0, i], y_recv.at[0, i], up_y), now=False)
        for i, c in enumerate(Y_SENT)
    ]

    def start_up():
        for copy in up_copies:
            copy.start()

    when(y_high & ~before_gap, start_up)
    for i, c in enumerate(Y_SENT):
        send(y_low, remote(stress.at[c, :, 0:2, :], sigma.at[c, 2:18, 40:42, :], y_send.at[1, i], y_recv.at[1, i], down_y))
    odd = y % 2
    strips = []
    for part in (1, 2):
        low = (odd == 1) if part == 1 else (odd == 0)
        side = odd if part == 1 else 1 - odd
        strips.append((part, low, pl.multiple_of(24 - 24 * side, 8), pl.multiple_of(40 - 40 * side, 8)))
    z_parts = [(0, 8, 16)] + [(part, first, 8) for part, _, first, _ in strips]
    z_copies = []
    for part, first, rows in z_parts:
        at, to = pl.ds(first, rows), pl.ds(8 + first, rows)
        z_copies.append((
            send(z_high, remote(stress.at[:, 14:16, at, :], sigma.at[:, 0:2, to, :], zs_send.at[0, part], zs_recv.at[0, part], {"gz": z + 1}), now=False),
            send(z_low, remote(stress.at[:, 0:2, at, :], sigma.at[:, 18:20, to, :], zs_send.at[1, part], zs_recv.at[1, part], {"gz": z - 1}), now=False),
        ))

    def start_z(part, condition):
        when(z_high if condition is None else condition & z_high, z_copies[part][0].start)
        when(z_low if condition is None else condition & z_low, z_copies[part][1].start)

    start_z(2, after_gap)
    start_z(0, None)
    start_z(1, None)
    start_z(2, ~after_gap)

    zero = jnp.zeros((8, NX), jnp.float32)

    def pack_spot(k, i):
        at = 4 * (k + (NZ if i == 1 else 0))
        return at, (lane >= at) & (lane < at + 4)

    def pack_layer(held, blocks, i, k, at, spot):
        for r, block in enumerate(blocks):
            j = len(blocks) * (i // 2) + r
            held[j] = jnp.where(spot, pltpu.roll(block, at + 2, 1), held[j])

    def pack_stress(step, held):
        held = list(held)
        for k in (2 * step, 2 * step + 1):
            for i, c in enumerate(X_PARTS):
                at, spot = pack_spot(k, i)
                pack_layer(held, [sigma[c, 2 + k, 8 + 8 * r : 16 + 8 * r, :] for r in range(4)], i, k, at, spot)
        return tuple(held)

    for copy in scalars:
        copy.wait()
    for k in range(NZ):
        for row in range(2):
            layers[row, pl.ds(NZ * z + k, 1), :] = jnp.full((1, NX), small[5 + row, k], jnp.float32)

    for c in X_PARTS:
        stress_in[c].wait()
    held = lax.fori_loop(0, NZ // 2, pack_stress, (zero,) * 8)
    for j in range(8):
        packs[0, j // 4, 8 * (j % 4) : 8 * (j % 4) + 8, :] = held[j]

    mine = pl.ds(NZ * z, NZ)
    for d in range(1, GZ):
        send(None, remote(layers.at[:, mine, :], layers.at[:, mine, :], layer_send.at[d - 1], layer_recv.at[z], {"gz": (z + d) % GZ}))
    columns = []
    for i in range(5):
        column = zero
        for block_id in range(16):
            column = jnp.where(lane == block_id, small[i, block_id], column)
        columns.append(column)
    keep = jnp.exp(-STEP / jnp.where(lane < 16, columns[3], 1.0))
    tables[0] = columns[0] * (STEP / 12.0)
    tables[1] = columns[1] * (1.0 / 12.0)
    tables[2] = columns[2] * (1.0 / 12.0)
    tables[3] = keep
    tables[4] = (1.0 - keep) * columns[4]

    send(x_high, remote(packs.at[0], halo_s.at[0], s_send.at[0], s_recv.at[0], {"gx": x + 1}))
    send(x_low, remote(packs.at[0], halo_s.at[1], s_send.at[1], s_recv.at[1], {"gx": x - 1}))
    material_in.wait()

    def property_layer(k, carry):
        for r in range(4):
            rows = slice(8 * r, 8 * r + 8)
            block_id = mat[k, rows, :]
            for i in range(5):
                props[i, k, rows, :] = jnp.take_along_axis(tables[i], block_id, axis=1)
        return carry

    lax.fori_loop(0, NZ, property_layer, 0)

    offset = lax.broadcasted_iota(jnp.int32, (NX, NX), 0) - lax.broadcasted_iota(jnp.int32, (NX, NX), 1)
    weights = jnp.zeros((NX, NX), jnp.float32)
    for distance, factor in ((-2, 1.0), (-1, -8.0), (1, 8.0), (2, -1.0)):
        weights = jnp.where(offset == distance, factor, weights)
    stencil[...] = weights.astype(jnp.bfloat16)

    def differentiate_x(parts, field, first, rows, unroll):
        def layers_of(step, carry):
            spots = [(i, c, unroll * step + n) for i, c in enumerate(parts) for n in range(unroll)]
            rest = jnp.concatenate([field[c, k + 2, pl.ds(8 + first, rows), :] for _, c, k in spots], axis=0)
            total = None
            for _ in range(3):
                piece = rest.astype(jnp.bfloat16)
                rest = rest - piece.astype(jnp.float32)
                product = jnp.dot(piece, stencil[...], preferred_element_type=jnp.float32)
                total = product if total is None else total + product
            for n, (i, _, k) in enumerate(spots):
                along[i, k, pl.ds(first, rows), :] = total[n * rows : (n + 1) * rows]
            return carry

        lax.fori_loop(0, NZ // unroll, layers_of, 0)

    differentiate_x(X_PARTS, sigma, 0, NY, 4)

    def arrived(ref, recv):
        remote(ref, ref, s_send.at[0], recv, {"gz": z}).wait_recv()

    def zero_z(first):
        sigma[:, pl.ds(first, 2), 8:40, :] = jnp.zeros((6, 2, NY, NX), jnp.float32)
        vel[:, pl.ds(first, 2), 8:40, :] = jnp.zeros((3, 2, NY, NX), jnp.float32)

    def zero_y(first):
        def layer(k, carry):
            for c in Y_SENT:
                sigma[c, 2 + k, first : first + 8, :] = zero
            for c in range(3):
                vel[c, 2 + k, first : first + 8, :] = zero
            return carry

        lax.fori_loop(0, NZ, layer, 0)
        for m in range(6):
            terrain[m, first : first + 8, :] = jnp.zeros((8, 32), jnp.int32)

    def zero_x(side, slot):
        halo_s[side] = jnp.zeros((2, NY, NX), jnp.float32)
        halo_v[side] = jnp.zeros((2, NY, NX), jnp.float32)
        terrain[slot, 8:40, :] = jnp.zeros((32, 32), jnp.int32)

        def zero_top():
            terrain[slot, 40:48, :] = jnp.zeros((8, 32), jnp.int32)

        when(before_gap, zero_top)

    when(z == 0, lambda: zero_z(0))
    when(z == GZ - 1, lambda: zero_z(18))
    when(y == 0, lambda: zero_y(0))
    when(y == GY - 1, lambda: zero_y(40))
    when(x == 0, lambda: zero_x(0, 0))
    when(x == GX - 1, lambda: zero_x(1, 5))

    d_x = functools.partial(d_x_of, along)

    def join(halo, first, rows):
        spot = lax.broadcasted_iota(jnp.int32, (rows, NX), 1) % 4
        at = pl.ds(first, rows)
        for i in range(2):
            change = jnp.where(spot < 2, halo[0, i, at, :], halo[1, i, at, :])
            low = 8.0 * jnp.where(spot == 1, pltpu.roll(change, 127, 1), 0.0) - pltpu.roll(change, 126, 1)
            high = pltpu.roll(change, 2, 1) - 8.0 * jnp.where(spot == 2, pltpu.roll(change, 1, 1), 0.0)
            halo[0, i, at, :] = jnp.where(spot < 2, low, high)

    for copy in (stress_in[1], stress_in[2], stress_in[5], velocity_in):
        copy.wait()
    when(x_low, lambda: arrived(halo_s.at[0], s_recv.at[0]))
    when(x_high, lambda: arrived(halo_s.at[1], s_recv.at[1]))
    join(halo_s, 0, NY)
    def wait_stress_z(part, condition):
        _, first, rows = z_parts[part]
        to = pl.ds(8 + first, rows)
        when(condition & z_low, lambda: arrived(sigma.at[:, 0:2, to, :], zs_recv.at[0, part]))
        when(condition & z_high, lambda: arrived(sigma.at[:, 18:20, to, :], zs_recv.at[1, part]))

    gap_copy = remote(gap_out, gap_in, gap_sem.at[0], gap_sem.at[1], down_y)
    sends.append((after_gap, gap_copy))

    def gap_package():
        top = lax.broadcasted_iota(jnp.int32, (8, NX), 0) == 0

        def layers_of(step, carry):
            for k in (2 * step, 2 * step + 1):
                scale = props[0, k, 0:8, :]
                for c in range(6):
                    gap_out[3 + c, k] = (scale * d_k(sigma, c, k, 0, 8))[0:2]
                gap_out[9, k] = scale[0:2]
                for i, (c_x, c_y) in enumerate(zip(X_PARTS, Y_PARTS)):
                    here, after_1, after_2 = (sigma[c_y, k + 2, 8 + d : 16 + d, :] for d in range(3))
                    before_1 = jnp.where(top, 0.0, pltpu.roll(here, 1, 0))
                    grad_y = 8.0 * (after_1 - before_1) - after_2
                    known = v_out[i, k, 0:8, :] + scale * (d_x(c_x, k, 0, 8, halo_s, i) + grad_y)
                    gap_out[i, k] = known[0:2]
            return carry

        lax.fori_loop(0, NZ // 2, layers_of, 0)
        gap_copy.start()

    wait_stress_z(2, after_gap)
    when(after_gap, gap_package)

    elevation_in.wait()
    for d in range(1, GZ):
        g = (z + d) % GZ
        arrived(terrain.at[1 + g, 8:40, :], t_recv.at[1 + g])
    when(x_low, lambda: arrived(terrain.at[0, 8:40, :], t_recv.at[0]))
    when(x_high, lambda: arrived(terrain.at[5, 8:40, :], t_recv.at[5]))
    edge_up = send(y_high, remote(terrain.at[:, 32:40, :], terrain.at[:, 0:8, :], edge_send.at[0], edge_recv.at[0], up_y), now=False)
    when(y_high & ~before_gap, edge_up.start)
    send(y_low & ~after_gap, remote(terrain.at[:, 8:16, :], terrain.at[:, 40:48, :], edge_send.at[1], edge_recv.at[1], down_y))

    def heights(row):
        rows = pl.ds(row, 8)
        held = [terrain[m, rows, :].astype(jnp.float32) / 200.0 for m in range(6)]
        blank = jnp.zeros((8, 96), jnp.float32)
        wide[0, rows, :] = jnp.concatenate([blank, held[0]], axis=1)
        wide[1, rows, :] = jnp.concatenate(held[1:5], axis=1)
        wide[2, rows, :] = jnp.concatenate([held[5], blank], axis=1)

    binomial = (1.0, 4.0, 6.0, 4.0, 1.0)

    def metrics(first, rows):
        along_y = []
        for part in range(3):
            total = jnp.zeros((rows + 8, NX), jnp.float32)
            for d, factor in enumerate(binomial):
                total = total + factor * wide[part, pl.ds(first + 2 + d, rows + 8), :]
            along_y.append(total / 16.0)
        row = jnp.concatenate(along_y, axis=1)
        total = jnp.zeros_like(row)
        for d, factor in enumerate(binomial):
            total = total + factor * (row if d == 2 else pltpu.roll(row, (2 - d) % 384, 1))
        total = total / 16.0
        for part in range(3):
            surf[part, 0 : rows + 8, :] = total[:, 128 * part : 128 * part + 128]
        own = jnp.concatenate([surf[part, 4 : 4 + rows, :] for part in range(3)], axis=1)
        height = own[:, 128:256]
        shifted = [pltpu.roll(own, d % 384, 1)[:, 128:256] for d in (2, 1, -1, -2)]
        slope_x = centred_12(*shifted) / 12.0
        slope_y = centred_12(*[surf[1, 4 + d : 4 + d + rows, :] for d in (-2, -1, 1, 2)]) / 12.0

        def above(step, total):
            for layer in [4 * step + i for i in range(4)]:
                base, follow = layers[0, pl.ds(layer, 1), :], layers[1, pl.ds(layer, 1), :]
                total = total + follow * (base * jnp.exp(follow * height))
            return total

        upper = lax.fori_loop(0, (NZ // 4) * z, above, jnp.zeros((rows, NX), jnp.float32))

        def layer(step, total):
            for k in [4 * step + i for i in range(4)]:
                base, follow = layers[0, pl.ds(NZ * z + k, 1), :], layers[1, pl.ds(NZ * z + k, 1), :]
                thickness = base * jnp.exp(follow * height)
                weighted = follow * thickness
                inverse = 1.0 / thickness
                factor = (total + 0.5 * weighted - 1.0) * inverse
                at = pl.ds(first, rows)
                metric[0, k, at, :] = slope_x * factor
                metric[1, k, at, :] = slope_y * factor
                metric[2, k, at, :] = inverse
                total = total + weighted
            return total

        lax.fori_loop(0, NZ // 4, layer, upper)

    def velocity_rows(first, rows, unroll):
        blocks = rows // 8

        def velocity_layer(step, carried):
            held, last = list(carried[0]), carried[1]
            at = pl.ds(first, rows)
            ks = [unroll * step + i for i in range(unroll)]
            pack_rows(held, [k - unroll for k in ks], last)
            made = []
            for k in ks:
                m_x, m_y, m_z = (metric[i, k, at, :] for i in range(3))
                grad_k = [d_k(sigma, c, k, first, rows) for c in range(6)]
                grad_x = [d_x(c, k, first, rows, halo_s, i) for i, c in enumerate(X_PARTS)]
                grad_y = [d_y(sigma, c, k, first, rows) for c in Y_PARTS]
                scale = props[0, k, at, :]
                row = []
                for c, (a, b, d) in enumerate(((0, 3, 4), (3, 1, 5), (4, 5, 2))):
                    accel = (grad_x[c] - m_x * grad_k[a]) + (grad_y[c] - m_y * grad_k[b]) + m_z * grad_k[d]
                    new = v_out[c, k, at, :] + scale * accel
                    v_out[c, k, at, :] = new
                    vel[c, 2 + k, pl.ds(8 + first, rows), :] = new
                    row.append(new)
                made.append(row)
            return tuple(held), made

        def pack_rows(held, ks, made):
            for k, row in zip(ks, made):
                for c in range(3):
                    spot_at, spot = pack_spot(k, c)
                    pack_layer(held, [row[c][8 * r : 8 * r + 8] for r in range(blocks)], c, k, spot_at, spot)

        nothing = jnp.zeros((rows, NX), jnp.float32)
        start = ((zero,) * (2 * blocks), [[nothing] * 3 for _ in range(unroll)])
        held, last = lax.fori_loop(0, NZ // unroll, velocity_layer, start)
        held = list(held)
        pack_rows(held, range(NZ - unroll, NZ), last)
        for j in range(2 * blocks):
            packs[1, j // blocks, pl.ds(first + 8 * (j % blocks), 8), :] = held[j]

    def send_rows(part, first, rows):
        at = pl.ds(first, rows)
        send(x_high, remote(packs.at[1, :, at, :], halo_v.at[0, :, at, :], x_send.at[0, part], x_recv.at[0, part], {"gx": x + 1}))
        send(x_low, remote(packs.at[1, :, at, :], halo_v.at[1, :, at, :], x_send.at[1, part], x_recv.at[1, part], {"gx": x - 1}))
        at = pl.ds(8 + first, rows)
        send(z_high, remote(vel.at[:, 16:18, at, :], vel.at[:, 0:2, at, :], z_send.at[0, part], z_recv.at[0, part], {"gz": z + 1}))
        send(z_low, remote(vel.at[:, 2:4, at, :], vel.at[:, 18:20, at, :], z_send.at[1, part], z_recv.at[1, part], {"gz": z - 1}))

    def wait_x(part, first, rows):
        at = pl.ds(first, rows)
        when(x_low, lambda: arrived(halo_v.at[0, :, at, :], x_recv.at[0, part]))
        when(x_high, lambda: arrived(halo_v.at[1, :, at, :], x_recv.at[1, part]))
        join(halo_v, first, rows)

    def wait_z(part, first, rows):
        at = pl.ds(8 + first, rows)
        when(z_low, lambda: arrived(vel.at[:, 0:2, at, :], z_recv.at[0, part]))
        when(z_high, lambda: arrived(vel.at[:, 18:20, at, :], z_recv.at[1, part]))

    for row in range(8, 40, 8):
        heights(row)
    for d in range(1, GZ):
        g = (z + d) % GZ
        arrived(layers.at[:, pl.ds(NZ * g, NZ), :], layer_recv.at[g])
    metrics(8, 16)

    def start_far():
        pl.semaphore_wait(far_sem, 1)
        edge_up.start()
        start_up()

    def gap_velocity():
        arrived(gap_in, gap_sem.at[1])

        def layers_of(step, carry):
            for k in (2 * step, 2 * step + 1):
                m_x, m_y, m_z = (metric[i, k, NY : NY + 2, :] for i in range(3))
                for i, (a, b, d) in enumerate(((0, 3, 4), (3, 1, 5), (4, 5, 2))):
                    edge = sigma[Y_PARTS[i], k + 2, 38:40, :]
                    beyond = jnp.concatenate([edge[0:1] - 8.0 * edge[1:2], edge[1:2]], axis=0)
                    known = gap_in[i, k] + gap_in[9, k] * beyond
                    vel[i, 2 + k, 40:42, :] = known - m_x * gap_in[3 + a, k] - m_y * gap_in[3 + b, k] + m_z * gap_in[3 + d, k]
            return carry

        lax.fori_loop(0, NZ // 2, layers_of, 0)

    def gap_metrics():
        for part in range(3):
            wide[part, 48:64, :] = jnp.zeros((16, NX), jnp.float32)
        metrics(NY, 8)

    when(before_gap, start_far)
    wait_stress_z(0, z >= 0)
    velocity_rows(8, 16, 2)
    send_rows(0, 8, 16)
    differentiate_x(range(3), vel, 8, 16, 4)
    when(before_gap, lambda: arrived(gap_terrain, gap_sem.at[3]))
    for d in range(1, GZ):
        send(before_gap, remote(gap_terrain, gap_terrain, pass_send.at[d - 1], pass_recv.at[own_slot], {"gz": (z + d) % GZ}))
    for g in range(GZ):
        send(before_gap & x_high & (z == GZ - 1), remote(gap_terrain, terrain.at[0, 40:48, :], pass_send.at[3 + g], pass_recv.at[0], {"gx": x + 1, "gz": g}))
        send(before_gap & x_low & (z == 0), remote(gap_terrain, terrain.at[5, 40:48, :], pass_send.at[3 + g], pass_recv.at[5], {"gx": x - 1, "gz": g}))

    def gap_terrain_arrived():
        for d in range(1, GZ):
            slot = 1 + (z + d) % GZ
            arrived(terrain.at[slot, 40:48, :], pass_recv.at[slot])
        when(x_low, lambda: arrived(terrain.at[0, 40:48, :], pass_recv.at[0]))
        when(x_high, lambda: arrived(terrain.at[5, 40:48, :], pass_recv.at[5]))

    low_copy = remote(vel.at[:, 2:18, 8:10, :], vel.at[:, 2:18, 40:42, :], vy_send.at[1], vy_recv.at[1], down_y)
    high_copy = remote(vel.at[:, 2:18, 38:40, :], vel.at[:, 2:18, 6:8, :], vy_send.at[0], vy_recv.at[0], up_y)
    sends.append((y_low & ~after_gap, low_copy))
    sends.append((y_high, high_copy))

    def stress_rows(first, rows, unroll, steps, stride=1):
        at = pl.ds(first, rows)

        def stress_layer(step, carry):
            for k in [unroll * stride * step + i for i in range(unroll)]:
                for c, new, total in stress_layer_of(m_out, sigma, vel, along, halo_v, metric, props, k, first, rows):
                    m_out[c, k, at, :] = new
                    s_out[c, k, at, :] = total
            return carry

        lax.fori_loop(steps[0], steps[1], stress_layer, 0)

    def stress_beside(part):
        _, low, first, _ = strips[part - 1]
        wait_x(part, first, 8)
        wait_z(part, first, 8)
        when(low & y_low, lambda: arrived(vel.at[:, 2:18, 6:8, :], vy_recv.at[0]))
        when(~low & y_high & ~before_gap, lambda: arrived(vel.at[:, 2:18, 40:42, :], vy_recv.at[1]))
        if part == 2:
            when(before_gap, gap_velocity)
        if part == 1:
            stress_rows(first, 8, 4, (0, NZ // 4))

    inner_near = pl.multiple_of(16 - 8 * odd, 8)
    inner_far = pl.multiple_of(8 + 8 * odd, 8)

    def early_stress():
        differentiate_x(range(3), vel, strips[0][2], 8, 8)
        memory_in.wait()
        wait_x(0, 8, 16)
        wait_z(0, 8, 16)
        stress_rows(inner_near, 8, 4, (0, NZ // 4))

    def late_stress():
        differentiate_x(range(3), vel, strips[0][2], 8, 8)
        memory_in.wait()
        wait_x(0, 8, 16)
        stress_rows(8, 16, 2, (1, NZ // 2 - 1))
        wait_z(0, 8, 16)
        stress_rows(8, 16, 2, (0, 2), NZ // 2 - 1)

    for part, low, first, outer in strips:
        if part == 2:
            when(at_gap, early_stress)
        when(low & y_low, lambda: arrived(terrain.at[:, 0:8, :], edge_recv.at[0]))
        when(~low & y_high & ~before_gap, lambda: arrived(terrain.at[:, 40:48, :], edge_recv.at[1]))
        if part == 2:
            when(before_gap, gap_terrain_arrived)
        heights(outer)
        metrics(first, 8)
        for i, c in enumerate(Y_SENT):
            when(low & y_low, lambda: arrived(sigma.at[c, 2:18, 6:8, :], y_recv.at[0, i]))
            when(~low & y_high, lambda: arrived(sigma.at[c, 2:18, 40:42, :], y_recv.at[1, i]))
        wait_stress_z(part, (z >= 0) if part == 1 else ~after_gap)
        velocity_rows(first, 8, 4)
        when(low & y_low & ~after_gap, low_copy.start)
        when(~low & y_high, high_copy.start)
        send_rows(part, first, 8)
    differentiate_x(range(3), vel, strips[1][2], 8, 8)
    when(before_gap, gap_metrics)
    when(~at_gap, late_stress)
    when(at_gap, lambda: stress_rows(inner_far, 8, 4, (0, NZ // 4)))
    stress_beside(1)
    stress_beside(2)
    for condition, copy in sends:
        when(condition, copy.wait_send)


def write_out(v_in, s_in, m_in, sigma, vel, along, halo_v, metric, props, v_ref, s_ref, m_ref, last, sems):
    odd = lax.axis_index("gy") % 2
    first = pl.multiple_of(24 * odd, 8)
    strip, rest = pl.ds(first, 8), pl.ds(pl.multiple_of(8 - 8 * odd, 8), 24)
    copies = [pltpu.make_async_copy(v_in.at[c], v_ref.at[c], sems.at[c]) for c in range(3)]
    for c in range(6):
        copies.append(pltpu.make_async_copy(s_in.at[c, :, rest, :], s_ref.at[c, :, rest, :], sems.at[3 + c]))
        copies.append(pltpu.make_async_copy(m_in.at[c, :, rest, :], m_ref.at[c, :, rest, :], sems.at[9 + c]))
    for copy in copies:
        copy.start()

    def layers_of(step, carry):
        for k in [4 * step + i for i in range(4)]:
            for c, new, total in stress_layer_of(m_in, sigma, vel, along, halo_v, metric, props, k, first, 8):
                last[c, k] = total
                last[6 + c, k] = new
        return carry

    lax.fori_loop(0, NZ // 4, layers_of, 0)
    late = []
    for c in range(6):
        late.append(pltpu.make_async_copy(last.at[c], s_ref.at[c, :, strip, :], sems.at[15 + c]))
        late.append(pltpu.make_async_copy(last.at[6 + c], m_ref.at[c, :, strip, :], sems.at[21 + c]))
    for copy in late:
        copy.start()
    for copy in copies + late:
        copy.wait()


def local(*arrays):
    held = [pltpu.with_memory_space_constraint(array, pltpu.HBM) for array in arrays]
    f32, vmem, dma = jnp.float32, pltpu.VMEM, pltpu.SemaphoreType.DMA
    outputs = [(n, NZ, NY, NX) for n in (3, 6, 6)]
    kept = [(6, 20, 48, NX), (3, 20, 48, NX), (3, NZ, NY, NX), (2, 2, NY, NX), (3, NZ, NY + 8, NX), (5, NZ, NY, NX)]
    results = pl.pallas_call(
        kernel,
        out_shape=tuple(vmem(shape, f32) for shape in outputs + kept),
        in_specs=[pl.BlockSpec(memory_space=pltpu.HBM)] * len(held),
        out_specs=tuple(pl.BlockSpec(memory_space=vmem) for _ in outputs + kept),
        scratch_shapes=[
            vmem((6, 48, 32), jnp.int32),
            vmem((3, 64, NX), f32),
            vmem((3, 24, NX), f32),
            vmem((2, GZ * NZ, NX), f32),
            vmem((NZ, NY, NX), jnp.int32),
            vmem((5, 8, NX), f32),
            vmem((NX, NX), jnp.bfloat16),
            vmem((2, 2, NY, NX), f32),
            vmem((2, 2, NY, NX), f32),
            pltpu.SMEM((7, 16), f32),
            dma((17,)), dma((4,)), dma((4,)), dma((2, 3)), dma((2, 3)), dma((3,)), dma((4,)), dma((7,)), dma((6,)), dma((2,)), dma((2,)),
            dma((2, 3)), dma((2, 3)), dma((2, 3)), dma((2, 3)), dma((2,)), dma((2,)),
            dma((2, 3)), dma((2, 3)),
            vmem((10, NZ, 2, NX), f32),
            vmem((10, NZ, 2, NX), f32),
            dma((4,)), dma((7,)), dma((6,)),
            pltpu.SemaphoreType.REGULAR,
        ],
        compiler_params=pltpu.CompilerParams(
            collective_id=0, has_side_effects=True, vmem_limit_bytes=24 << 20
        ),
    )(*held)
    return pl.pallas_call(
        write_out,
        out_shape=tuple(jax.ShapeDtypeStruct(shape, f32) for shape in outputs),
        in_specs=[pl.BlockSpec(memory_space=vmem)] * 9,
        out_specs=tuple(pl.BlockSpec(memory_space=pltpu.HBM) for _ in outputs),
        scratch_shapes=[vmem((12, NZ, 8, NX), f32), dma((27,))],
        compiler_params=pltpu.CompilerParams(vmem_limit_bytes=8 << 20),
    )(*results)


def solution(mesh):
    field = P(None, "gz", "gy", "gx")
    return jax.shard_map(
        local,
        mesh=mesh,
        in_specs=(
            P("gy", ("gx", "gz")), P("gz"), P("gz"), P("gz", "gy", "gx"),
            P(), P(), P(), P(), P(), field, field, field,
        ),
        out_specs=(field, field, field),
        check_vma=False,
    )
```

```python
import functools

import jax
import jax.numpy as jnp
from jax import lax
from jax.experimental import pallas as pl
from jax.experimental.pallas import tpu as pltpu
from jax.sharding import PartitionSpec as P

MESH = pl.DeviceIdType.MESH
STEP = 0.3
GX, GY, GZ = 4, 16, 4
NZ, NY, NX = 16, 32, 128
X_PARTS = (0, 3, 4)
Y_PARTS = (3, 1, 5)
Y_SENT = (1, 3, 5)


def when(condition, action):
    if condition is None:
        action()
    else:
        pl.when(condition)(lambda: action())


def centred_12(before_2, before_1, after_1, after_2):
    return 8.0 * (after_1 - before_1) - (after_2 - before_2)


def d_k(field, c, k, first, rows):
    return centred_12(*[field[c, k + 2 + d, pl.ds(8 + first, rows), :] for d in (-2, -1, 1, 2)])


def d_y(field, c, k, first, rows):
    return centred_12(*[field[c, k + 2, pl.ds(8 + first + d, rows), :] for d in (-2, -1, 1, 2)])


def d_x_of(along, c, k, first, rows, halo, i):
    side = lax.broadcasted_iota(jnp.int32, (rows, NX), 1)
    at = 4 * (k + (NZ if i == 1 else 0))
    fix = pltpu.roll(halo[0, i // 2, pl.ds(first, rows), :], 126 - at, 1)
    return along[i, k, pl.ds(first, rows), :] + jnp.where((side < 2) | (side >= 126), fix, 0.0)


def stress_layer_of(memory, sigma, vel, along, halo_v, metric, props, k, first, rows):
    at = pl.ds(first, rows)
    grad_x = [d_x_of(along, c, k, first, rows, halo_v, c) for c in range(3)]
    m_x, m_y, m_z = (metric[i, k, at, :] for i in range(3))
    along_k = [d_k(vel, c, k, first, rows) for c in range(3)]
    along_x = [grad_x[c] - m_x * along_k[c] for c in range(3)]
    along_y = [d_y(vel, c, k, first, rows) - m_y * along_k[c] for c in range(3)]
    along_z = [m_z * along_k[c] for c in range(3)]
    lam, mu, kept, gain = (props[i, k, at, :] for i in range(1, 5))
    volume = lam * (along_x[0] + along_y[1] + along_z[2])
    twice = mu + mu
    rates = (
        volume + twice * along_x[0],
        volume + twice * along_y[1],
        volume + twice * along_z[2],
        mu * (along_y[0] + along_x[1]),
        mu * (along_z[0] + along_x[2]),
        mu * (along_z[1] + along_y[2]),
    )
    for c, rate in enumerate(rates):
        new = kept * memory[c, k, at, :] + gain * rate
        yield c, new, sigma[c, 2 + k, pl.ds(8 + first, rows), :] + STEP * (rate - new)


def kernel(
    elevation, layer_base, stretch, material, buoyancy, lame, shear, relax, weight, velocity, stress, memory,
    v_out, s_out, m_out, sigma, vel, along, halo_v, metric, props,
    terrain, wide, surf, layers, mat, tables, stencil, packs, halo_s,
    small, local_sem, s_send, s_recv, y_send, y_recv, layer_send, layer_recv, t_send, t_recv, edge_send, edge_recv,
    z_send, z_recv, x_send, x_recv, vy_send, vy_recv, zs_send, zs_recv, gap_out, gap_in, gap_sem, pass_send, pass_recv, far_sem,
):
    x, y, z = lax.axis_index("gx"), lax.axis_index("gy"), lax.axis_index("gz")
    x_low, x_high = x > 0, x < GX - 1
    y_low, y_high = y > 0, y < GY - 1
    z_low, z_high = z > 0, z < GZ - 1
    before_gap, after_gap = y == GY // 2 - 1, y == GY // 2
    at_gap = before_gap | after_gap
    lane = lax.broadcasted_iota(jnp.int32, (8, NX), 1)

    barrier = pltpu.get_barrier_semaphore()
    beside = [(None, {"gz": (z + d) % GZ}) for d in range(1, GZ)]
    for g in range(GZ):
        beside.append((x_high & ((z == g) | (z == GZ - 1) | (g == 0)), {"gx": x + 1, "gz": g}))
        beside.append((x_low & ((z == g) | (z == 0) | (g == GZ - 1)), {"gx": x - 1, "gz": g}))
    up_y, down_y = {"gy": y + 1}, {"gy": y - 1}
    for condition, target in [(y_high, up_y), (y_low & ~after_gap, down_y)] + beside:
        when(condition, lambda target=target: pl.semaphore_signal(barrier, inc=1, device_id=target, device_id_type=MESH))
    expected = [y_low, y_high & ~before_gap] + [condition for condition, _ in beside]

    own_slot = 1 + z
    tables_in = (buoyancy, lame, shear, relax, weight, layer_base, stretch)
    scalars = [pltpu.make_async_copy(ref, small.at[i], local_sem.at[i]) for i, ref in enumerate(tables_in)]
    for copy in scalars:
        copy.start()
    stress_in = {
        c: pltpu.make_async_copy(stress.at[c], sigma.at[c, 2:18, 8:40, :], local_sem.at[7 + c])
        for c in (0, 3, 4, 1, 2, 5)
    }
    for c in (0, 3, 4):
        stress_in[c].start()
    material_in = pltpu.make_async_copy(material, mat, local_sem.at[15])
    material_in.start()
    for c in (1, 2, 5):
        stress_in[c].start()
    elevation_in = pltpu.make_async_copy(elevation, terrain.at[own_slot, 8:40, :], local_sem.at[13])
    velocity_in = pltpu.make_async_copy(velocity, v_out, local_sem.at[14])
    memory_in = pltpu.make_async_copy(memory, m_out, local_sem.at[16])
    for copy in (elevation_in, velocity_in, memory_in):
        copy.start()

    pl.semaphore_wait(barrier, sum(1 if c is None else c.astype(jnp.int32) for c in expected))
    when(after_gap, lambda: pl.semaphore_signal(far_sem, inc=1, device_id=down_y, device_id_type=MESH))

    def remote(source, to, send, recv, target):
        return pltpu.make_async_remote_copy(
            src_ref=source, dst_ref=to, send_sem=send, recv_sem=recv, device_id=target, device_id_type=MESH
        )

    sends = []

    def send(condition, copy, now=True):
        sends.append((condition, copy))
        if now:
            when(condition, copy.start)
        return copy

    for d in range(1, GZ):
        send(None, remote(elevation, terrain.at[own_slot, 8:40, :], t_send.at[d - 1], t_recv.at[own_slot], {"gz": (z + d) % GZ}))
    for g in range(GZ):
        send(x_high & (z == GZ - 1), remote(elevation, terrain.at[0, 8:40, :], t_send.at[3 + g], t_recv.at[0], {"gx": x + 1, "gz": g}))
        send(x_low & (z == 0), remote(elevation, terrain.at[5, 8:40, :], t_send.at[3 + g], t_recv.at[5], {"gx": x - 1, "gz": g}))
    gap_terrain = terrain.at[own_slot, 40:48, :]
    send(after_gap, remote(elevation.at[0:8, :], gap_terrain, gap_sem.at[2], gap_sem.at[3], down_y))
    up_copies = [
        send(y_high, remote(stress.at[c, :, 30:32, :], sigma.at[c, 2:18, 6:8, :], y_send.at[0, i], y_recv.at[0, i], up_y), now=False)
        for i, c in enumerate(Y_SENT)
    ]

    def start_up():
        for copy in up_copies:
            copy.start()

    when(y_high & ~before_gap, start_up)
    for i, c in enumerate(Y_SENT):
        send(y_low, remote(stress.at[c, :, 0:2, :], sigma.at[c, 2:18, 40:42, :], y_send.at[1, i], y_recv.at[1, i], down_y))
    odd = y % 2
    strips = []
    for part in (1, 2):
        low = (odd == 1) if part == 1 else (odd == 0)
        side = odd if part == 1 else 1 - odd
        strips.append((part, low, pl.multiple_of(24 - 24 * side, 8), pl.multiple_of(40 - 40 * side, 8)))
    z_parts = [(0, 8, 16)] + [(part, first, 8) for part, _, first, _ in strips]
    z_copies = []
    for part, first, rows in z_parts:
        at, to = pl.ds(first, rows), pl.ds(8 + first, rows)
        z_copies.append((
            send(z_high, remote(stress.at[:, 14:16, at, :], sigma.at[:, 0:2, to, :], zs_send.at[0, part], zs_recv.at[0, part], {"gz": z + 1}), now=False),
            send(z_low, remote(stress.at[:, 0:2, at, :], sigma.at[:, 18:20, to, :], zs_send.at[1, part], zs_recv.at[1, part], {"gz": z - 1}), now=False),
        ))

    def start_z(part, condition):
        when(z_high if condition is None else condition & z_high, z_copies[part][0].start)
        when(z_low if condition is None else condition & z_low, z_copies[part][1].start)

    start_z(2, after_gap)
    start_z(0, None)
    start_z(1, None)
    start_z(2, ~after_gap)

    zero = jnp.zeros((8, NX), jnp.float32)

    def pack_spot(k, i):
        at = 4 * (k + (NZ if i == 1 else 0))
        return at, (lane >= at) & (lane < at + 4)

    def pack_layer(held, blocks, i, k, at, spot):
        for r, block in enumerate(blocks):
            j = len(blocks) * (i // 2) + r
            held[j] = jnp.where(spot, pltpu.roll(block, at + 2, 1), held[j])

    def pack_stress(step, held):
        held = list(held)
        for k in (2 * step, 2 * step + 1):
            for i, c in enumerate(X_PARTS):
                at, spot = pack_spot(k, i)
                pack_layer(held, [sigma[c, 2 + k, 8 + 8 * r : 16 + 8 * r, :] for r in range(4)], i, k, at, spot)
        return tuple(held)

    for copy in scalars:
        copy.wait()
    for k in range(NZ):
        for row in range(2):
            layers[row, pl.ds(NZ * z + k, 1), :] = jnp.full((1, NX), small[5 + row, k], jnp.float32)

    for c in X_PARTS:
        stress_in[c].wait()
    held = lax.fori_loop(0, NZ // 2, pack_stress, (zero,) * 8)
    for j in range(8):
        packs[0, j // 4, 8 * (j % 4) : 8 * (j % 4) + 8, :] = held[j]

    mine = pl.ds(NZ * z, NZ)
    for d in range(1, GZ):
        send(None, remote(layers.at[:, mine, :], layers.at[:, mine, :], layer_send.at[d - 1], layer_recv.at[z], {"gz": (z + d) % GZ}))
    columns = []
    for i in range(5):
        column = zero
        for block_id in range(16):
            column = jnp.where(lane == block_id, small[i, block_id], column)
        columns.append(column)
    keep = jnp.exp(-STEP / jnp.where(lane < 16, columns[3], 1.0))
    tables[0] = columns[0] * (STEP / 12.0)
    tables[1] = columns[1] * (1.0 / 12.0)
    tables[2] = columns[2] * (1.0 / 12.0)
    tables[3] = keep
    tables[4] = (1.0 - keep) * columns[4]

    send(x_high, remote(packs.at[0], halo_s.at[0], s_send.at[0], s_recv.at[0], {"gx": x + 1}))
    send(x_low, remote(packs.at[0], halo_s.at[1], s_send.at[1], s_recv.at[1], {"gx": x - 1}))
    material_in.wait()

    def property_layer(k, carry):
        for r in range(4):
            rows = slice(8 * r, 8 * r + 8)
            block_id = mat[k, rows, :]
            for i in range(5):
                props[i, k, rows, :] = jnp.take_along_axis(tables[i], block_id, axis=1)
        return carry

    lax.fori_loop(0, NZ, property_layer, 0)

    offset = lax.broadcasted_iota(jnp.int32, (NX, NX), 0) - lax.broadcasted_iota(jnp.int32, (NX, NX), 1)
    weights = jnp.zeros((NX, NX), jnp.float32)
    for distance, factor in ((-2, 1.0), (-1, -8.0), (1, 8.0), (2, -1.0)):
        weights = jnp.where(offset == distance, factor, weights)
    stencil[...] = weights.astype(jnp.bfloat16)

    def differentiate_x(parts, field, first, rows, unroll):
        def layers_of(step, carry):
            spots = [(i, c, unroll * step + n) for i, c in enumerate(parts) for n in range(unroll)]
            rest = jnp.concatenate([field[c, k + 2, pl.ds(8 + first, rows), :] for _, c, k in spots], axis=0)
            total = None
            for _ in range(3):
                piece = rest.astype(jnp.bfloat16)
                rest = rest - piece.astype(jnp.float32)
                product = jnp.dot(piece, stencil[...], preferred_element_type=jnp.float32)
                total = product if total is None else total + product
            for n, (i, _, k) in enumerate(spots):
                along[i, k, pl.ds(first, rows), :] = total[n * rows : (n + 1) * rows]
            return carry

        lax.fori_loop(0, NZ // unroll, layers_of, 0)

    differentiate_x(X_PARTS, sigma, 0, NY, 4)

    def arrived(ref, recv):
        remote(ref, ref, s_send.at[0], recv, {"gz": z}).wait_recv()

    def zero_z(first):
        sigma[:, pl.ds(first, 2), 8:40, :] = jnp.zeros((6, 2, NY, NX), jnp.float32)
        vel[:, pl.ds(first, 2), 8:40, :] = jnp.zeros((3, 2, NY, NX), jnp.float32)

    def zero_y(first):
        def layer(k, carry):
            for c in Y_SENT:
                sigma[c, 2 + k, first : first + 8, :] = zero
            for c in range(3):
                vel[c, 2 + k, first : first + 8, :] = zero
            return carry

        lax.fori_loop(0, NZ, layer, 0)
        for m in range(6):
            terrain[m, first : first + 8, :] = jnp.zeros((8, 32), jnp.int32)

    def zero_x(side, slot):
        halo_s[side] = jnp.zeros((2, NY, NX), jnp.float32)
        halo_v[side] = jnp.zeros((2, NY, NX), jnp.float32)
        terrain[slot, 8:40, :] = jnp.zeros((32, 32), jnp.int32)

        def zero_top():
            terrain[slot, 40:48, :] = jnp.zeros((8, 32), jnp.int32)

        when(before_gap, zero_top)

    when(z == 0, lambda: zero_z(0))
    when(z == GZ - 1, lambda: zero_z(18))
    when(y == 0, lambda: zero_y(0))
    when(y == GY - 1, lambda: zero_y(40))
    when(x == 0, lambda: zero_x(0, 0))
    when(x == GX - 1, lambda: zero_x(1, 5))

    d_x = functools.partial(d_x_of, along)

    def join(halo, first, rows):
        spot = lax.broadcasted_iota(jnp.int32, (rows, NX), 1) % 4
        at = pl.ds(first, rows)
        for i in range(2):
            change = jnp.where(spot < 2, halo[0, i, at, :], halo[1, i, at, :])
            low = 8.0 * jnp.where(spot == 1, pltpu.roll(change, 127, 1), 0.0) - pltpu.roll(change, 126, 1)
            high = pltpu.roll(change, 2, 1) - 8.0 * jnp.where(spot == 2, pltpu.roll(change, 1, 1), 0.0)
            halo[0, i, at, :] = jnp.where(spot < 2, low, high)

    for copy in (stress_in[1], stress_in[2], stress_in[5], velocity_in):
        copy.wait()
    when(x_low, lambda: arrived(halo_s.at[0], s_recv.at[0]))
    when(x_high, lambda: arrived(halo_s.at[1], s_recv.at[1]))
    join(halo_s, 0, NY)
    def wait_stress_z(part, condition):
        _, first, rows = z_parts[part]
        to = pl.ds(8 + first, rows)
        when(condition & z_low, lambda: arrived(sigma.at[:, 0:2, to, :], zs_recv.at[0, part]))
        when(condition & z_high, lambda: arrived(sigma.at[:, 18:20, to, :], zs_recv.at[1, part]))

    gap_copy = remote(gap_out, gap_in, gap_sem.at[0], gap_sem.at[1], down_y)
    sends.append((after_gap, gap_copy))

    def gap_package():
        top = lax.broadcasted_iota(jnp.int32, (8, NX), 0) == 0

        def layers_of(step, carry):
            for k in (2 * step, 2 * step + 1):
                scale = props[0, k, 0:8, :]
                for c in range(6):
                    gap_out[3 + c, k] = (scale * d_k(sigma, c, k, 0, 8))[0:2]
                gap_out[9, k] = scale[0:2]
                for i, (c_x, c_y) in enumerate(zip(X_PARTS, Y_PARTS)):
                    here, after_1, after_2 = (sigma[c_y, k + 2, 8 + d : 16 + d, :] for d in range(3))
                    before_1 = jnp.where(top, 0.0, pltpu.roll(here, 1, 0))
                    grad_y = 8.0 * (after_1 - before_1) - after_2
                    known = v_out[i, k, 0:8, :] + scale * (d_x(c_x, k, 0, 8, halo_s, i) + grad_y)
                    gap_out[i, k] = known[0:2]
            return carry

        lax.fori_loop(0, NZ // 2, layers_of, 0)
        gap_copy.start()

    wait_stress_z(2, after_gap)
    when(after_gap, gap_package)

    elevation_in.wait()
    for d in range(1, GZ):
        g = (z + d) % GZ
        arrived(terrain.at[1 + g, 8:40, :], t_recv.at[1 + g])
    when(x_low, lambda: arrived(terrain.at[0, 8:40, :], t_recv.at[0]))
    when(x_high, lambda: arrived(terrain.at[5, 8:40, :], t_recv.at[5]))
    edge_up = send(y_high, remote(terrain.at[:, 32:40, :], terrain.at[:, 0:8, :], edge_send.at[0], edge_recv.at[0], up_y), now=False)
    when(y_high & ~before_gap, edge_up.start)
    send(y_low & ~after_gap, remote(terrain.at[:, 8:16, :], terrain.at[:, 40:48, :], edge_send.at[1], edge_recv.at[1], down_y))

    def heights(row):
        rows = pl.ds(row, 8)
        held = [terrain[m, rows, :].astype(jnp.float32) / 200.0 for m in range(6)]
        blank = jnp.zeros((8, 96), jnp.float32)
        wide[0, rows, :] = jnp.concatenate([blank, held[0]], axis=1)
        wide[1, rows, :] = jnp.concatenate(held[1:5], axis=1)
        wide[2, rows, :] = jnp.concatenate([held[5], blank], axis=1)

    binomial = (1.0, 4.0, 6.0, 4.0, 1.0)

    def metrics(first, rows):
        along_y = []
        for part in range(3):
            total = jnp.zeros((rows + 8, NX), jnp.float32)
            for d, factor in enumerate(binomial):
                total = total + factor * wide[part, pl.ds(first + 2 + d, rows + 8), :]
            along_y.append(total / 16.0)
        row = jnp.concatenate(along_y, axis=1)
        total = jnp.zeros_like(row)
        for d, factor in enumerate(binomial):
            total = total + factor * (row if d == 2 else pltpu.roll(row, (2 - d) % 384, 1))
        total = total / 16.0
        for part in range(3):
            surf[part, 0 : rows + 8, :] = total[:, 128 * part : 128 * part + 128]
        own = jnp.concatenate([surf[part, 4 : 4 + rows, :] for part in range(3)], axis=1)
        height = own[:, 128:256]
        shifted = [pltpu.roll(own, d % 384, 1)[:, 128:256] for d in (2, 1, -1, -2)]
        slope_x = centred_12(*shifted) / 12.0
        slope_y = centred_12(*[surf[1, 4 + d : 4 + d + rows, :] for d in (-2, -1, 1, 2)]) / 12.0

        def above(step, total):
            for layer in [4 * step + i for i in range(4)]:
                base, follow = layers[0, pl.ds(layer, 1), :], layers[1, pl.ds(layer, 1), :]
                total = total + follow * (base * jnp.exp(follow * height))
            return total

        upper = lax.fori_loop(0, (NZ // 4) * z, above, jnp.zeros((rows, NX), jnp.float32))

        def layer(step, total):
            for k in [4 * step + i for i in range(4)]:
                base, follow = layers[0, pl.ds(NZ * z + k, 1), :], layers[1, pl.ds(NZ * z + k, 1), :]
                thickness = base * jnp.exp(follow * height)
                weighted = follow * thickness
                inverse = 1.0 / thickness
                factor = (total + 0.5 * weighted - 1.0) * inverse
                at = pl.ds(first, rows)
                metric[0, k, at, :] = slope_x * factor
                metric[1, k, at, :] = slope_y * factor
                metric[2, k, at, :] = inverse
                total = total + weighted
            return total

        lax.fori_loop(0, NZ // 4, layer, upper)

    def velocity_rows(first, rows, unroll):
        blocks = rows // 8

        def velocity_layer(step, carried):
            held, last = list(carried[0]), carried[1]
            at = pl.ds(first, rows)
            ks = [unroll * step + i for i in range(unroll)]
            pack_rows(held, [k - unroll for k in ks], last)
            made = []
            for k in ks:
                m_x, m_y, m_z = (metric[i, k, at, :] for i in range(3))
                grad_k = [d_k(sigma, c, k, first, rows) for c in range(6)]
                grad_x = [d_x(c, k, first, rows, halo_s, i) for i, c in enumerate(X_PARTS)]
                grad_y = [d_y(sigma, c, k, first, rows) for c in Y_PARTS]
                scale = props[0, k, at, :]
                row = []
                for c, (a, b, d) in enumerate(((0, 3, 4), (3, 1, 5), (4, 5, 2))):
                    accel = (grad_x[c] - m_x * grad_k[a]) + (grad_y[c] - m_y * grad_k[b]) + m_z * grad_k[d]
                    new = v_out[c, k, at, :] + scale * accel
                    v_out[c, k, at, :] = new
                    vel[c, 2 + k, pl.ds(8 + first, rows), :] = new
                    row.append(new)
                made.append(row)
            return tuple(held), made

        def pack_rows(held, ks, made):
            for k, row in zip(ks, made):
                for c in range(3):
                    spot_at, spot = pack_spot(k, c)
                    pack_layer(held, [row[c][8 * r : 8 * r + 8] for r in range(blocks)], c, k, spot_at, spot)

        nothing = jnp.zeros((rows, NX), jnp.float32)
        start = ((zero,) * (2 * blocks), [[nothing] * 3 for _ in range(unroll)])
        held, last = lax.fori_loop(0, NZ // unroll, velocity_layer, start)
        held = list(held)
        pack_rows(held, range(NZ - unroll, NZ), last)
        for j in range(2 * blocks):
            packs[1, j // blocks, pl.ds(first + 8 * (j % blocks), 8), :] = held[j]

    def send_rows(part, first, rows):
        at = pl.ds(first, rows)
        send(x_high, remote(packs.at[1, :, at, :], halo_v.at[0, :, at, :], x_send.at[0, part], x_recv.at[0, part], {"gx": x + 1}))
        send(x_low, remote(packs.at[1, :, at, :], halo_v.at[1, :, at, :], x_send.at[1, part], x_recv.at[1, part], {"gx": x - 1}))
        at = pl.ds(8 + first, rows)
        send(z_high, remote(vel.at[:, 16:18, at, :], vel.at[:, 0:2, at, :], z_send.at[0, part], z_recv.at[0, part], {"gz": z + 1}))
        send(z_low, remote(vel.at[:, 2:4, at, :], vel.at[:, 18:20, at, :], z_send.at[1, part], z_recv.at[1, part], {"gz": z - 1}))

    def wait_x(part, first, rows):
        at = pl.ds(first, rows)
        when(x_low, lambda: arrived(halo_v.at[0, :, at, :], x_recv.at[0, part]))
        when(x_high, lambda: arrived(halo_v.at[1, :, at, :], x_recv.at[1, part]))
        join(halo_v, first, rows)

    def wait_z(part, first, rows):
        at = pl.ds(8 + first, rows)
        when(z_low, lambda: arrived(vel.at[:, 0:2, at, :], z_recv.at[0, part]))
        when(z_high, lambda: arrived(vel.at[:, 18:20, at, :], z_recv.at[1, part]))

    for row in range(8, 40, 8):
        heights(row)
    for d in range(1, GZ):
        g = (z + d) % GZ
        arrived(layers.at[:, pl.ds(NZ * g, NZ), :], layer_recv.at[g])
    metrics(8, 16)

    def start_far():
        pl.semaphore_wait(far_sem, 1)
        edge_up.start()
        start_up()

    def gap_velocity():
        arrived(gap_in, gap_sem.at[1])

        def layers_of(step, carry):
            for k in (2 * step, 2 * step + 1):
                m_x, m_y, m_z = (metric[i, k, NY : NY + 2, :] for i in range(3))
                for i, (a, b, d) in enumerate(((0, 3, 4), (3, 1, 5), (4, 5, 2))):
                    edge = sigma[Y_PARTS[i], k + 2, 38:40, :]
                    beyond = jnp.concatenate([edge[0:1] - 8.0 * edge[1:2], edge[1:2]], axis=0)
                    known = gap_in[i, k] + gap_in[9, k] * beyond
                    vel[i, 2 + k, 40:42, :] = known - m_x * gap_in[3 + a, k] - m_y * gap_in[3 + b, k] + m_z * gap_in[3 + d, k]
            return carry

        lax.fori_loop(0, NZ // 2, layers_of, 0)

    def gap_metrics():
        for part in range(3):
            wide[part, 48:64, :] = jnp.zeros((16, NX), jnp.float32)
        metrics(NY, 8)

    when(before_gap, start_far)
    wait_stress_z(0, z >= 0)
    velocity_rows(8, 16, 2)
    send_rows(0, 8, 16)
    differentiate_x(range(3), vel, 8, 16, 4)
    when(before_gap, lambda: arrived(gap_terrain, gap_sem.at[3]))
    for d in range(1, GZ):
        send(before_gap, remote(gap_terrain, gap_terrain, pass_send.at[d - 1], pass_recv.at[own_slot], {"gz": (z + d) % GZ}))
    for g in range(GZ):
        send(before_gap & x_high & (z == GZ - 1), remote(gap_terrain, terrain.at[0, 40:48, :], pass_send.at[3 + g], pass_recv.at[0], {"gx": x + 1, "gz": g}))
        send(before_gap & x_low & (z == 0), remote(gap_terrain, terrain.at[5, 40:48, :], pass_send.at[3 + g], pass_recv.at[5], {"gx": x - 1, "gz": g}))

    def gap_terrain_arrived():
        for d in range(1, GZ):
            slot = 1 + (z + d) % GZ
            arrived(terrain.at[slot, 40:48, :], pass_recv.at[slot])
        when(x_low, lambda: arrived(terrain.at[0, 40:48, :], pass_recv.at[0]))
        when(x_high, lambda: arrived(terrain.at[5, 40:48, :], pass_recv.at[5]))

    low_copy = remote(vel.at[:, 2:18, 8:10, :], vel.at[:, 2:18, 40:42, :], vy_send.at[1], vy_recv.at[1], down_y)
    high_copy = remote(vel.at[:, 2:18, 38:40, :], vel.at[:, 2:18, 6:8, :], vy_send.at[0], vy_recv.at[0], up_y)
    sends.append((y_low & ~after_gap, low_copy))
    sends.append((y_high, high_copy))

    def stress_rows(first, rows, unroll, steps, stride=1):
        at = pl.ds(first, rows)

        def stress_layer(step, carry):
            for k in [unroll * stride * step + i for i in range(unroll)]:
                for c, new, total in stress_layer_of(m_out, sigma, vel, along, halo_v, metric, props, k, first, rows):
                    m_out[c, k, at, :] = new
                    s_out[c, k, at, :] = total
            return carry

        lax.fori_loop(steps[0], steps[1], stress_layer, 0)

    def stress_beside(part):
        _, low, first, _ = strips[part - 1]
        wait_x(part, first, 8)
        wait_z(part, first, 8)
        when(low & y_low, lambda: arrived(vel.at[:, 2:18, 6:8, :], vy_recv.at[0]))
        when(~low & y_high & ~before_gap, lambda: arrived(vel.at[:, 2:18, 40:42, :], vy_recv.at[1]))
        if part == 2:
            when(before_gap, gap_velocity)
        if part == 1:
            stress_rows(first, 8, 4, (0, NZ // 4))

    inner_near = pl.multiple_of(16 - 8 * odd, 8)
    inner_far = pl.multiple_of(8 + 8 * odd, 8)

    def early_stress():
        differentiate_x(range(3), vel, strips[0][2], 8, 8)
        memory_in.wait()
        wait_x(0, 8, 16)
        wait_z(0, 8, 16)
        stress_rows(inner_near, 8, 4, (0, NZ // 4))

    def late_stress():
        differentiate_x(range(3), vel, strips[0][2], 8, 8)
        memory_in.wait()
        wait_x(0, 8, 16)
        stress_rows(8, 16, 2, (1, NZ // 2 - 1))
        wait_z(0, 8, 16)
        stress_rows(8, 16, 2, (0, 2), NZ // 2 - 1)

    for part, low, first, outer in strips:
        if part == 2:
            when(before_gap, early_stress)
        when(low & y_low, lambda: arrived(terrain.at[:, 0:8, :], edge_recv.at[0]))
        when(~low & y_high & ~before_gap, lambda: arrived(terrain.at[:, 40:48, :], edge_recv.at[1]))
        if part == 2:
            when(before_gap, gap_terrain_arrived)
        heights(outer)
        metrics(first, 8)
        for i, c in enumerate(Y_SENT):
            when(low & y_low, lambda: arrived(sigma.at[c, 2:18, 6:8, :], y_recv.at[0, i]))
            when(~low & y_high, lambda: arrived(sigma.at[c, 2:18, 40:42, :], y_recv.at[1, i]))
        wait_stress_z(part, (z >= 0) if part == 1 else ~after_gap)
        velocity_rows(first, 8, 4)
        when(low & y_low & ~after_gap, low_copy.start)
        when(~low & y_high, high_copy.start)
        send_rows(part, first, 8)
    differentiate_x(range(3), vel, strips[1][2], 8, 8)
    when(before_gap, gap_metrics)
    when(after_gap, early_stress)
    when(~at_gap, late_stress)
    when(at_gap, lambda: stress_rows(inner_far, 8, 4, (0, NZ // 4)))
    stress_beside(1)
    stress_beside(2)
    for condition, copy in sends:
        when(condition, copy.wait_send)


def write_out(v_in, s_in, m_in, sigma, vel, along, halo_v, metric, props, v_ref, s_ref, m_ref, last, sems):
    odd = lax.axis_index("gy") % 2
    first = pl.multiple_of(24 * odd, 8)
    strip, rest = pl.ds(first, 8), pl.ds(pl.multiple_of(8 - 8 * odd, 8), 24)
    copies = [pltpu.make_async_copy(v_in.at[c], v_ref.at[c], sems.at[c]) for c in range(3)]
    for c in range(6):
        copies.append(pltpu.make_async_copy(s_in.at[c, :, rest, :], s_ref.at[c, :, rest, :], sems.at[3 + c]))
        copies.append(pltpu.make_async_copy(m_in.at[c, :, rest, :], m_ref.at[c, :, rest, :], sems.at[9 + c]))
    for copy in copies:
        copy.start()

    def layers_of(step, carry):
        for k in [4 * step + i for i in range(4)]:
            for c, new, total in stress_layer_of(m_in, sigma, vel, along, halo_v, metric, props, k, first, 8):
                last[c, k] = total
                last[6 + c, k] = new
        return carry

    lax.fori_loop(0, NZ // 4, layers_of, 0)
    late = []
    for c in range(6):
        late.append(pltpu.make_async_copy(last.at[c], s_ref.at[c, :, strip, :], sems.at[15 + c]))
        late.append(pltpu.make_async_copy(last.at[6 + c], m_ref.at[c, :, strip, :], sems.at[21 + c]))
    for copy in late:
        copy.start()
    for copy in copies + late:
        copy.wait()


def local(*arrays):
    held = [pltpu.with_memory_space_constraint(array, pltpu.HBM) for array in arrays]
    f32, vmem, dma = jnp.float32, pltpu.VMEM, pltpu.SemaphoreType.DMA
    outputs = [(n, NZ, NY, NX) for n in (3, 6, 6)]
    kept = [(6, 20, 48, NX), (3, 20, 48, NX), (3, NZ, NY, NX), (2, 2, NY, NX), (3, NZ, NY + 8, NX), (5, NZ, NY, NX)]
    results = pl.pallas_call(
        kernel,
        out_shape=tuple(vmem(shape, f32) for shape in outputs + kept),
        in_specs=[pl.BlockSpec(memory_space=pltpu.HBM)] * len(held),
        out_specs=tuple(pl.BlockSpec(memory_space=vmem) for _ in outputs + kept),
        scratch_shapes=[
            vmem((6, 48, 32), jnp.int32),
            vmem((3, 64, NX), f32),
            vmem((3, 24, NX), f32),
            vmem((2, GZ * NZ, NX), f32),
            vmem((NZ, NY, NX), jnp.int32),
            vmem((5, 8, NX), f32),
            vmem((NX, NX), jnp.bfloat16),
            vmem((2, 2, NY, NX), f32),
            vmem((2, 2, NY, NX), f32),
            pltpu.SMEM((7, 16), f32),
            dma((17,)), dma((4,)), dma((4,)), dma((2, 3)), dma((2, 3)), dma((3,)), dma((4,)), dma((7,)), dma((6,)), dma((2,)), dma((2,)),
            dma((2, 3)), dma((2, 3)), dma((2, 3)), dma((2, 3)), dma((2,)), dma((2,)),
            dma((2, 3)), dma((2, 3)),
            vmem((10, NZ, 2, NX), f32),
            vmem((10, NZ, 2, NX), f32),
            dma((4,)), dma((7,)), dma((6,)),
            pltpu.SemaphoreType.REGULAR,
        ],
        compiler_params=pltpu.CompilerParams(
            collective_id=0, has_side_effects=True, vmem_limit_bytes=24 << 20
        ),
    )(*held)
    return pl.pallas_call(
        write_out,
        out_shape=tuple(jax.ShapeDtypeStruct(shape, f32) for shape in outputs),
        in_specs=[pl.BlockSpec(memory_space=vmem)] * 9,
        out_specs=tuple(pl.BlockSpec(memory_space=pltpu.HBM) for _ in outputs),
        scratch_shapes=[vmem((12, NZ, 8, NX), f32), dma((27,))],
        compiler_params=pltpu.CompilerParams(vmem_limit_bytes=8 << 20),
    )(*results)


def solution(mesh):
    field = P(None, "gz", "gy", "gx")
    return jax.shard_map(
        local,
        mesh=mesh,
        in_specs=(
            P("gy", ("gx", "gz")), P("gz"), P("gz"), P("gz", "gy", "gx"),
            P(), P(), P(), P(), P(), field, field, field,
        ),
        out_specs=(field, field, field),
        check_vma=False,
    )
```
